32 devices in a mesh: coil: 4 (over z), slab: 8 (over y, x, core).
Axes of the slice: x: 2, y: 2, z: 4, core: 2. Of those that a mesh axis runs over, the one named last changes fastest.
Arguments:
- image: float32 [2, 256, 256, 128], P(None, 'slab'), may hold values from -6 to 6
- sensitivity: bfloat16 [16, 2, 256, 256, 128], P('coil', None, 'slab'), may hold values from -5 to 5
- blocks: bfloat16 [8, 24, 128, 2048], P('slab'), may hold values from -0.125 to 0.125
- samples: bfloat16 [8, 24, 128, 16, 2, 128], P('slab', None, None, 'coil'), may hold values from -6 to 6
- offsets: int32 [8, 24], P('slab'), may hold values from 0 to 192
- counts: int32 [8], P('slab'), may hold values from 1 to 24, as said below
- auxiliary: float32 [2, 256, 256, 128], P(None, 'slab', 'coil'), may hold values from -4 to 4
- scaled_dual: float32 [2, 256, 256, 128], P(None, 'slab', 'coil'), may hold values from -3 to 3
Outputs:
- image_next: float32 [2, 256, 256, 128], P(None, 'slab', 'coil')
- auxiliary_next: float32 [2, 256, 256, 128], P(None, 'slab', 'coil')
- dual_next: float32 [2, 256, 256, 128], P(None, 'slab', 'coil')
The draws below stay inside these ranges and needn't reach their ends.
Inputs may be any that keep to these rules, and one draw needn't show every extreme that they name: Each tile's live groups are its first counts slots; some tile holds 24 live groups.
All inputs are finite; a program needn't handle non-finite values.
Results may differ from the reference program's by a relative error of at most 0.014.
Values may be sent and summed in bfloat16 or wider, within the bound.
A program may use at most 192 MiB of HBM per device.

```python
import math
import jax
import jax.numpy as jnp
from jax import lax

X = 256
Y = 256
Z = 128
C = 16
WIN = 64
P_SIZE = 128
CH = 24
TILES = 8
KYD = 32
CELLS = 2048


def draw_counts(key, part):
    tile = jnp.arange(TILES, dtype=jnp.int32)
    spread = jnp.abs(2 * tile + 1 - TILES)
    profile = jnp.maximum(1, CH * (TILES - spread) // TILES)
    factor = jax.random.randint(jax.random.fold_in(key, 11), (TILES,), 2, 5)
    loads = jnp.clip(profile * factor // 4, 1, CH)
    return jnp.where(tile == TILES // 2, CH, loads).astype(jnp.int32)


def touch_ends(values, rng, smallest, high):
    longest = values.shape.index(max(values.shape))
    spots = []
    for shift in (0, 1):
        where = [jax.random.randint(jax.random.fold_in(rng, axis), (), 0, length) for axis, length in enumerate(values.shape)]
        where[longest] = (where[longest] + shift) % values.shape[longest]
        spots.append(tuple(where))
    return values.at[spots[0]].set(smallest).at[spots[1]].set(high)


def steps_of(stream_key, shape, pieces, low, largest):
    def one(axis_at, blocks):
        steps = jax.random.uniform(jax.random.fold_in(jax.random.fold_in(stream_key, 6), axis_at), (blocks,), jnp.float32, low / len(pieces), largest / len(pieces))
        return jnp.repeat(jnp.exp(steps), shape[axis_at] // blocks).reshape((-1,) + (1,) * (len(shape) - axis_at - 1))

    level = one(*pieces[0])
    for cut in pieces[1:]:
        level = level * one(*cut)
    return level


def scatter_about(own_key, shape, width, most, shards=(), kind=jnp.bfloat16):
    entries = width * jax.random.normal(own_key, shape, jnp.float32)
    if shards:
        entries = entries * steps_of(own_key, shape, shards, -0.22, 0.18)
    return jnp.clip(entries, -most, most).astype(kind)


def setup_inputs(seed: int = 0) -> dict:
    arg_keys = jax.random.split(jax.random.key(seed), 9)
    return {
        "image": scatter_about(arg_keys[0], (2, X, Y, Z), 1.0, 6.0, ((1, 8),), jnp.float32),
        "sensitivity": scatter_about(arg_keys[1], (C, 2, X, Y, Z), 0.7, 5.0, ((0, 4), (2, 8))),
        "blocks": scatter_about(arg_keys[2], (TILES, CH, P_SIZE, CELLS), CELLS ** -0.5, 0.125, ((0, 8),)),
        "samples": scatter_about(arg_keys[3], (TILES, CH, P_SIZE, C, 2, Z), 1.0, 6.0, ((0, 8), (3, 4))),
        "offsets": touch_ends(jax.random.randint(arg_keys[4], (TILES, CH), 0, X - WIN + 1), jax.random.fold_in(arg_keys[4], 1), 0, X - WIN).astype(jnp.int32),
        "counts": draw_counts(jax.random.fold_in(arg_keys[8], 71), 0),
        "auxiliary": scatter_about(arg_keys[6], (2, X, Y, Z), 0.5, 4.0, ((1, 8), (2, 4)), jnp.float32),
        "scaled_dual": scatter_about(arg_keys[7], (2, X, Y, Z), 0.3, 3.0, ((1, 8), (2, 4)), jnp.float32),
    }


step_size = 0.5
penalty = 1.0
threshold = 0.3

def tables(length):
    index = jnp.arange(length, dtype=jnp.int32)
    product = index[:, None] * index[None, :] % length
    angle = product.astype(jnp.float32) * (2.0 * math.pi / length)
    factor = 1.0 / math.sqrt(length)
    return ((jnp.cos(angle) * factor).astype(jnp.bfloat16), (-jnp.sin(angle) * factor).astype(jnp.bfloat16))

def complex_apply(form, table_re, table_im, real, imag, inverse):

    def apply(table, values):
        return jnp.einsum(form, table.astype(jnp.float32), values.astype(jnp.float32), precision=lax.Precision.HIGHEST)
    if inverse:
        return (apply(table_re, real) + apply(table_im, imag), apply(table_re, imag) - apply(table_im, real))
    return (apply(table_re, real) - apply(table_im, imag), apply(table_im, real) + apply(table_re, imag))

def haar(values):
    parts, rows, cols, depth = values.shape
    blocked = values.reshape(parts, rows // 2, 2, cols // 2, 2, depth)
    first = blocked[:, :, 0, :, 0]
    second = blocked[:, :, 0, :, 1]
    third = blocked[:, :, 1, :, 0]
    fourth = blocked[:, :, 1, :, 1]
    upper = jnp.stack([(first + second + third + fourth) * 0.5, (first - second + third - fourth) * 0.5], axis=3)
    lower = jnp.stack([(first + second - third - fourth) * 0.5, (first - second - third + fourth) * 0.5], axis=3)
    return jnp.stack([upper, lower], axis=2).reshape(parts, rows, cols, depth)

def admm_update(current, gradient, auxiliary, scaled_dual):
    target = haar(auxiliary - scaled_dual)
    image_next = current - step_size * (gradient + penalty * (current - target))
    coeffs = haar(image_next) + scaled_dual
    magnitude = jnp.sqrt(coeffs[0] * coeffs[0] + coeffs[1] * coeffs[1])
    factor = jnp.maximum(1.0 - threshold / jnp.maximum(magnitude, threshold), 0.0)
    auxiliary_next = coeffs * factor
    return (image_next, auxiliary_next, coeffs - auxiliary_next)

def reference(image, sensitivity, blocks, samples, offsets, counts, auxiliary, scaled_dual):
    y_re, y_im = tables(Y)
    x_re, x_im = tables(X)

    def coil_kspace(coil_index):
        sens_re = sensitivity[coil_index, 0].astype(jnp.float32)
        sens_im = sensitivity[coil_index, 1].astype(jnp.float32)
        coil_re = (sens_re * image[0] - sens_im * image[1]).astype(jnp.bfloat16)
        coil_im = (sens_re * image[1] + sens_im * image[0]).astype(jnp.bfloat16)
        half_re, half_im = complex_apply('kn,xnz->xkz', y_re, y_im, coil_re, coil_im, False)
        half_re = half_re.astype(jnp.bfloat16)
        half_im = half_im.astype(jnp.bfloat16)
        out_re, out_im = complex_apply('kn,nyz->kyz', x_re, x_im, half_re, half_im, False)
        return jnp.stack([out_re, out_im]).astype(jnp.bfloat16)
    kspace = lax.map(coil_kspace, jnp.arange(C, dtype=jnp.int32))
    kspace = jnp.transpose(kspace, (2, 3, 0, 1, 4))
    columns = C * 2 * Z

    def grid_tile(tile):
        local = lax.dynamic_slice_in_dim(kspace, tile * KYD, KYD, 1)

        def grid_step(slot, total):
            start = offsets[tile, slot]
            window = lax.dynamic_slice_in_dim(local, start, WIN, 0).reshape(CELLS, columns)
            block = blocks[tile, slot]
            predicted = jnp.dot(block, window, preferred_element_type=jnp.float32)
            misfit = (predicted - samples[tile, slot].reshape(P_SIZE, columns).astype(jnp.float32)).astype(jnp.bfloat16)
            update = jnp.dot(block.T, misfit, preferred_element_type=jnp.float32).reshape(WIN, KYD, C, 2, Z)
            current = lax.dynamic_slice_in_dim(total, start, WIN, 0)
            return lax.dynamic_update_slice_in_dim(total, current + update, start, 0)
        total = lax.fori_loop(0, counts[tile], grid_step, jnp.zeros((X, KYD, C, 2, Z), jnp.float32))
        return total.astype(jnp.bfloat16)
    gridded = lax.map(grid_tile, jnp.arange(TILES, dtype=jnp.int32))
    gridded = jnp.transpose(gridded, (1, 0, 2, 3, 4, 5)).reshape(X, Y, C, 2, Z)

    def combine(total, coil_index):
        piece = lax.dynamic_index_in_dim(gridded, coil_index, 2, keepdims=False)
        back_re, back_im = complex_apply('kn,kyz->nyz', x_re, x_im, piece[:, :, 0], piece[:, :, 1], True)
        back_re = back_re.astype(jnp.bfloat16)
        back_im = back_im.astype(jnp.bfloat16)
        adj_re, adj_im = complex_apply('kn,xkz->xnz', y_re, y_im, back_re, back_im, True)
        adj_re = adj_re.astype(jnp.bfloat16).astype(jnp.float32)
        adj_im = adj_im.astype(jnp.bfloat16).astype(jnp.float32)
        sens_re = sensitivity[coil_index, 0].astype(jnp.float32)
        sens_im = sensitivity[coil_index, 1].astype(jnp.float32)
        term = jnp.stack([sens_re * adj_re + sens_im * adj_im, sens_re * adj_im - sens_im * adj_re])
        return (total + term, 0)
    gradient, unused = lax.scan(combine, jnp.zeros((2, X, Y, Z), jnp.float32), jnp.arange(C, dtype=jnp.int32))
    return admm_update(image, gradient, auxiliary, scaled_dual)
```

```python
import functools
import math

import jax
import jax.numpy as jnp
import numpy as np
from jax import lax
from jax.experimental import pallas as pl
from jax.experimental.pallas import tpu as pltpu
from jax.sharding import PartitionSpec as P

step_size = 0.5
penalty = 1.0
threshold = 0.3
VMEM_LIMIT = 62 * 1024 * 1024
F32 = jnp.float32
BF16 = jnp.bfloat16


def complex_table(length, inverse):
    index = np.arange(length, dtype=np.int64)
    angle = (index[:, None] * index[None, :] % length).astype(np.float64) * (2.0 * math.pi / length)
    factor = 1.0 / math.sqrt(length)
    re = np.cos(angle) * factor
    im = -np.sin(angle) * factor
    if inverse:
        whole = np.block([[re, im], [-im, re]])
    else:
        whole = np.block([[re, -im], [im, re]])
    return jnp.asarray(whole.astype(np.float32)).astype(BF16)


def params(**extra):
    return pltpu.CompilerParams(vmem_limit_bytes=VMEM_LIMIT, **extra)


def once(shape):
    return pl.BlockSpec(shape, lambda *i: (0,) * len(shape), pipeline_mode=pl.Buffered(1))


def cost(flops, nbytes):
    return pl.CostEstimate(flops=int(flops), bytes_accessed=int(nbytes), transcendentals=0)


def pitch(rows):
    tiles = -(-rows // 8)
    return 8 * (tiles + 1 - tiles % 2)


def gather_rows(ref, row, size, parts_n):
    pieces = []
    for p in range(2):
        for s in range(parts_n):
            pieces.append(ref[s, p, pl.ds(row, size), :])
    return jnp.concatenate(pieces, axis=0)


def forward_kernel(n, kl, xl, table, image, sens, *refs):
    outs, flat = refs[:n], refs[n]
    length = image.shape[2]
    me = lax.axis_index("slab")

    def pair(i, carry):
        columns = []
        for h in range(2):
            x = 2 * i + h
            sr = sens[0, 0, x].astype(F32)
            si = sens[0, 1, x].astype(F32)
            ir = image[0, x]
            ii = image[1, x]
            columns.append(
                jnp.concatenate(
                    [(sr * ir - si * ii).astype(BF16), (sr * ii + si * ir).astype(BF16)], axis=0
                )
            )
        both = jnp.concatenate(columns, axis=1)
        half = jnp.dot(table[...], both, preferred_element_type=F32)
        depth = half.shape[1] // 2
        for h in range(2):
            flat[pl.ds(2 * i + h, 2 * length, stride=pitch(xl)), :] = half[:, h * depth : (h + 1) * depth]
        return carry

    lax.fori_loop(0, xl // 2, pair, 0)
    for off in range(n):
        d = lax.rem(me + off, n)
        for p in range(2):

            def settle(k, carry):
                base = pl.multiple_of(((p * n + d) * kl + 2 * k) * pitch(xl), 8)
                rows = [flat[pl.ds(base + h * pitch(xl), xl), :] for h in range(2)]
                target = pl.ds(pl.multiple_of(2 * k * xl, 2 * xl), 2 * xl)
                outs[off][p, target, :] = jnp.concatenate(rows, axis=0).astype(BF16)
                return carry

            lax.fori_loop(0, kl // 2, settle, 0, unroll=4)


def forward_call(table, image, sensitivity, first, n, kl):
    _, _, xl, length, depth = sensitivity.shape
    return pl.pallas_call(
        functools.partial(forward_kernel, n, kl, xl),
        grid=(1,),
        in_specs=[
            once(table.shape),
            once(image.shape),
            pl.BlockSpec((1, 2, xl, length, depth), lambda i: (first, 0, 0, 0, 0)),
        ],
        out_specs=[pl.BlockSpec((2, kl * xl, depth), lambda i: (0, 0, 0))] * n,
        out_shape=[jax.ShapeDtypeStruct((2, kl * xl, depth), BF16)] * n,
        scratch_shapes=[pltpu.VMEM(((2 * length + 1) * pitch(xl), depth), F32)],
        compiler_params=params(),
        cost_estimate=cost(8 * length * length * xl * depth, 12 * xl * length * depth),
        name="forward",
    )(table, image, sensitivity)


def tile_kernel(n, kl, xl, win, offsets, counts, fwd, inv, blocks, samples, *refs):
    pieces, outs, refs = refs[:n], refs[n : 2 * n], refs[2 * n :]
    total, kspace, weights, piece, sem, piece_sem, *wide = refs
    me = lax.axis_index("slab")
    copies = []
    for off in range(n):
        origin = lax.rem(me + n - off, n)
        copies.append(pltpu.make_async_copy(pieces[off], piece.at[origin], piece_sem.at[off]))
    for copy in copies:
        copy.start()
    fetch = pltpu.make_async_copy(blocks.at[0], weights, sem)
    fetch.start()
    for copy in copies:
        copy.wait()
    length = n * xl
    depth = piece.shape[-1]
    if wide:
        source = wide[0]
        for p in range(2):
            for s in range(n):
                source[s, p] = piece[s, p].astype(F32)
    else:
        source = piece

    def to_kspace(i, carry):
        columns = []
        for h in range(2):
            row = pl.multiple_of((2 * i + h) * xl, xl)
            columns.append(gather_rows(source, row, xl, n).astype(BF16))
        spec = jnp.dot(fwd[...], jnp.concatenate(columns, axis=1), preferred_element_type=F32)
        for h in range(2):
            for p in range(2):
                total[p, pl.ds(2 * i + h, length, stride=pitch(kl)), :] = spec[
                    p * length : (p + 1) * length, h * depth : (h + 1) * depth
                ]
        return carry

    lax.fori_loop(0, kl // 2, to_kspace, 0)

    def settle(i, carry):
        rows = pl.ds(pl.multiple_of(i * pitch(kl), 8), kl)
        target = pl.ds(pl.multiple_of(i * kl, kl), kl)
        for p in range(2):
            kspace[target, p * depth : (p + 1) * depth] = total[p, rows, :].astype(kspace.dtype)
            total[p, rows, :] = jnp.zeros((kl, depth), F32)
        return carry

    lax.fori_loop(0, length, settle, 0, unroll=8)
    fetch.wait()
    cells = win * kl
    chunk = min(cells, 512)

    def group(slot, carry):
        first = offsets[0, slot]
        start = pl.multiple_of(first * kl, kl)
        window = kspace[pl.ds(start, cells), :].astype(BF16)
        predicted = jnp.dot(weights[slot], window, preferred_element_type=F32)
        misfit = (predicted - samples[slot].astype(F32)).astype(BF16)
        for c in range(0, cells, chunk):
            update = lax.dot_general(
                weights[slot, :, c : c + chunk],
                misfit,
                (((0,), (0,)), ((), ())),
                preferred_element_type=F32,
            )
            for k in range(chunk // kl):
                rows = pl.ds(pl.multiple_of((first + c // kl + k) * pitch(kl), 8), kl)
                for p in range(2):
                    total[p, rows, :] += update[k * kl : (k + 1) * kl, p * depth : (p + 1) * depth]
        return carry

    lax.fori_loop(0, counts[0], group, 0)

    def to_rows(i, carry):
        columns = []
        for h in range(2):
            columns.append(
                jnp.concatenate(
                    [total[p, pl.ds(2 * i + h, length, stride=pitch(kl)), :].astype(BF16) for p in range(2)], axis=0
                )
            )
        back = jnp.dot(inv[...], jnp.concatenate(columns, axis=1), preferred_element_type=F32)
        for h in range(2):
            for p in range(2):
                total[p, pl.ds(2 * i + h, length, stride=pitch(kl)), :] = back[
                    p * length : (p + 1) * length, h * depth : (h + 1) * depth
                ]
        return carry

    lax.fori_loop(0, kl // 2, to_rows, 0)
    for off in range(n):
        d = lax.rem(me + off, n)
        for p in range(2):

            def leave(k, carry):
                base = pl.multiple_of((d * xl + 2 * k) * pitch(kl), 8)
                rows = [total[p, pl.ds(base + h * pitch(kl), kl), :] for h in range(2)]
                target = pl.ds(pl.multiple_of(2 * k * kl, 2 * kl), 2 * kl)
                outs[off][p, target, :] = jnp.concatenate(rows, axis=0).astype(BF16)
                return carry

            lax.fori_loop(0, xl // 2, leave, 0, unroll=4)


def tile_call(fwd, inv, pieces, blocks, samples, offsets, counts, coil, n, kl, xl):
    shape = pieces[0].shape
    depth = shape[-1]
    _, slots, psize, cells = blocks.shape
    length = n * xl
    narrow = kl % 16 == 0 and xl % 16 == 0
    scratch = [
        pltpu.VMEM((2, (length + 1) * pitch(kl), depth), F32),
        pltpu.VMEM((length * kl, 2 * depth), BF16 if narrow else F32),
        pltpu.VMEM(blocks.shape[1:], BF16),
        pltpu.VMEM((n, *shape), BF16),
        pltpu.SemaphoreType.DMA,
        pltpu.SemaphoreType.DMA((n,)),
    ]
    if not narrow:
        scratch.append(pltpu.VMEM((n, *shape), F32))
    anywhere = pl.BlockSpec(memory_space=pl.ANY)
    smem = pl.BlockSpec(memory_space=pltpu.SMEM)
    return pl.pallas_call(
        functools.partial(tile_kernel, n, kl, xl, cells // kl),
        grid=(1,),
        in_specs=[
            smem,
            smem,
            once(fwd.shape),
            once(inv.shape),
            anywhere,
            pl.BlockSpec((slots, psize, 2 * depth), lambda i: (0, 0, coil), pipeline_mode=pl.Buffered(1)),
        ]
        + [anywhere] * n,
        out_specs=[pl.BlockSpec(shape, lambda i: (0, 0, 0))] * n,
        out_shape=[jax.ShapeDtypeStruct(shape, BF16)] * n,
        scratch_shapes=scratch,
        compiler_params=params(),
        cost_estimate=cost(
            16 * length * length * kl * depth + 8 * slots * psize * cells * depth,
            8 * length * kl * depth + 2 * blocks.size,
        ),
        name="tile",
    )(offsets, counts, fwd, inv, blocks, samples, *pieces)


def finish_kernel(n, shares, kl, xl, chunks, sent, table, sens, *refs):
    coils = sens.shape[0]
    backs, refs = [refs[k * n : (k + 1) * n] for k in range(coils)], refs[coils * n :]
    out, landing, sens_v, grad, got, recv, send, local, grad_recv, grad_send, *wide = refs
    ready = coils - sent
    length = n * kl
    depth = landing.shape[-1]
    share = length // shares
    rows = xl // chunks
    band = rows * kl
    me = lax.axis_index("slab")
    mine = lax.axis_index("coil")

    barrier = pltpu.get_barrier_semaphore()

    def greet(off, carry):
        pl.semaphore_signal(
            barrier, inc=1, device_id={"slab": lax.rem(me + off, n)}, device_id_type=pl.DeviceIdType.MESH
        )
        return carry

    lax.fori_loop(1, n, greet, 0)
    for off in range(1, shares):
        pl.semaphore_signal(
            barrier, inc=1, device_id={"coil": lax.rem(mine + off, shares)}, device_id_type=pl.DeviceIdType.MESH
        )
    pl.semaphore_wait(barrier, n - 1 + shares - 1)

    def send_band(j, carry):
        where = pl.ds(pl.multiple_of(j * band, band), band)
        for k in range(ready, coils):
            for off in range(1, n):
                pltpu.make_async_remote_copy(
                    src_ref=backs[k][off].at[:, where, :],
                    dst_ref=landing.at[k, me, :, where, :],
                    send_sem=send,
                    recv_sem=recv.at[j],
                    device_id={"slab": lax.rem(me + off, n)},
                    device_id_type=pl.DeviceIdType.MESH,
                ).start()
        return carry

    lax.fori_loop(0, chunks, send_band, 0)
    copies = []
    for k in range(coils):
        for off in range(n if k < ready else 1):
            origin = lax.rem(me + n - off, n)
            copies.append(pltpu.make_async_copy(backs[k][off], landing.at[k, origin], local.at[k * n + off]))
        copies.append(pltpu.make_async_copy(sens.at[k], sens_v.at[k], local.at[coils * n + k]))
    for copy in copies:
        copy.start()
    for copy in copies:
        copy.wait()

    def do_band(j, carry):
        where = pl.ds(pl.multiple_of(j * band, band), band)
        arrived = landing.at[ready:coils, 0 : n - 1, :, where, :]
        pltpu.make_async_copy(arrived, arrived, recv.at[j]).wait()
        if wide:
            for k in range(coils):
                for s in range(n):
                    for p in range(2):
                        wide[0][k, s, p] = landing[k, s, p, where, :].astype(F32)

        def columns_of(k, i):
            pieces = []
            for p in range(2):
                for s in range(n):
                    if wide:
                        pieces.append(wide[0][k, s, p, pl.ds(pl.multiple_of(i * kl, kl), kl), :])
                    else:
                        row = pl.multiple_of((j * rows + i) * kl, kl)
                        pieces.append(landing[k, s, p, pl.ds(row, kl), :])
            return jnp.concatenate(pieces, axis=0).astype(BF16)

        def pair(i, carry):
            total = [[None, None], [None, None]]
            for k in range(coils):
                both = jnp.concatenate([columns_of(k, 2 * i), columns_of(k, 2 * i + 1)], axis=1)
                adj = jnp.dot(table[...], both, preferred_element_type=F32)
                adj = adj.astype(BF16).astype(F32)
                for h in range(2):
                    x = j * rows + 2 * i + h
                    ar = adj[:length, h * depth : (h + 1) * depth]
                    ai = adj[length:, h * depth : (h + 1) * depth]
                    sr = sens_v[k, 0, x].astype(F32)
                    si = sens_v[k, 1, x].astype(F32)
                    re = sr * ar + si * ai
                    im = sr * ai - si * ar
                    total[h] = [re, im] if k == 0 else [total[h][0] + re, total[h][1] + im]
            for h in range(2):
                x = j * rows + 2 * i + h
                for p in range(2):
                    for q in range(shares):
                        grad[q, p, x] = total[h][p][q * share : (q + 1) * share].astype(BF16)
            return carry

        lax.fori_loop(0, rows // 2, pair, 0)
        lines = pl.ds(j * rows, rows)
        for off in range(1, shares):
            target = lax.rem(mine + off, shares)
            pltpu.make_async_remote_copy(
                src_ref=grad.at[target, :, lines],
                dst_ref=got.at[mine, :, lines],
                send_sem=grad_send,
                recv_sem=grad_recv.at[j],
                device_id={"coil": target},
                device_id_type=pl.DeviceIdType.MESH,
            ).start()
        return carry

    lax.fori_loop(0, chunks, do_band, 0)

    def add_band(j, carry):
        arrived = got.at[0 : shares - 1, :, pl.ds(j * rows, rows)]
        pltpu.make_async_copy(arrived, arrived, grad_recv.at[j]).wait()

        def line(i, carry):
            x = j * rows + i
            for p in range(2):
                value = grad[mine, p, x].astype(F32)
                for off in range(1, shares):
                    value += got[lax.rem(mine + off, shares), p, x].astype(F32)
                out[p, x] = value
            return carry

        lax.fori_loop(0, rows, line, 0)
        return carry

    lax.fori_loop(0, chunks, add_band, 0)
    gone = landing.at[ready:coils, 0 : n - 1]
    pltpu.make_async_copy(gone, gone, send).wait()
    gone = got.at[0 : shares - 1]
    pltpu.make_async_copy(gone, gone, grad_send).wait()


def finish_call(table, backs, sent, sensitivity, shares, n, kl):
    coils, _, xl, length, depth = sensitivity.shape
    chunks = xl // 4 if xl % 4 == 0 else 1
    rows = xl // chunks
    share = length // shares
    anywhere = pl.BlockSpec(memory_space=pl.ANY)
    vmem = pl.BlockSpec(memory_space=pltpu.VMEM)
    scratch = [
        pltpu.VMEM((coils, n, 2, xl * kl, depth), BF16),
        pltpu.VMEM(sensitivity.shape, BF16),
        pltpu.VMEM((shares, 2, xl, share, depth), BF16),
        pltpu.VMEM((shares, 2, xl, share, depth), BF16),
        pltpu.SemaphoreType.DMA((chunks,)),
        pltpu.SemaphoreType.DMA,
        pltpu.SemaphoreType.DMA((coils * n + coils,)),
        pltpu.SemaphoreType.DMA((chunks,)),
        pltpu.SemaphoreType.DMA,
    ]
    if kl % 16:
        scratch.append(pltpu.VMEM((coils, n, 2, rows * kl, depth), F32))
    return pl.pallas_call(
        functools.partial(finish_kernel, n, shares, kl, xl, chunks, sent),
        in_specs=[vmem, anywhere] + [anywhere] * (coils * n),
        out_specs=vmem,
        out_shape=jax.ShapeDtypeStruct((2, xl, share, depth), F32),
        scratch_shapes=scratch,
        compiler_params=params(collective_id=0, has_side_effects=True),
        name="finish",
    )(table, sensitivity, *[piece for back in backs for piece in back])


def haar_rows(first, second):
    even = lax.broadcasted_iota(jnp.int32, first.shape, 0) % 2 == 0
    rows = first.shape[0]

    def along(v):
        after = pltpu.roll(v, rows - 1, 0)
        ahead = pltpu.roll(v, 1, 0)
        return jnp.where(even, v + after, ahead - v) * 0.5

    return along(first + second), along(first - second)


def update_kernel(where, image, gradient, auxiliary, dual, image_out, aux_out, dual_out):
    del where
    rows = image.shape[1]
    for m in range(0, rows, 2):
        coeffs = []
        for p in range(2):
            target = haar_rows(
                auxiliary[p, m] - dual[p, m], auxiliary[p, m + 1] - dual[p, m + 1]
            )
            following = []
            for h in range(2):
                current = image[p, m + h]
                value = current - step_size * (
                    gradient[p, m + h].astype(F32) + penalty * (current - target[h])
                )
                image_out[p, m + h] = value
                following.append(value)
            spread = haar_rows(*following)
            coeffs.append([spread[h] + dual[p, m + h] for h in range(2)])
        for h in range(2):
            re, im = coeffs[0][h], coeffs[1][h]
            magnitude = jnp.sqrt(re * re + im * im)
            factor = jnp.maximum(1.0 - threshold / jnp.maximum(magnitude, threshold), 0.0)
            for p, value in enumerate((re, im)):
                kept = value * factor
                aux_out[p, m + h] = kept
                dual_out[p, m + h] = value - kept


def update_call(image, gradient, auxiliary, dual, position):
    _, xl, share, depth = auxiliary.shape
    rows = 8 if xl % 8 == 0 else 2
    block = (2, rows, share, depth)
    plain = pl.BlockSpec(block, lambda i, w: (0, i, 0, 0))
    shape = jax.ShapeDtypeStruct(auxiliary.shape, F32)
    return pl.pallas_call(
        update_kernel,
        grid_spec=pltpu.PrefetchScalarGridSpec(
            num_scalar_prefetch=1,
            grid=(xl // rows,),
            in_specs=[pl.BlockSpec(block, lambda i, w: (0, i, w[0], 0)), plain, plain, plain],
            out_specs=[plain, plain, plain],
        ),
        out_shape=[shape, shape, shape],
        compiler_params=params(),
        name="update",
    )(position, image, gradient, auxiliary, dual)


def body(image, sensitivity, blocks, samples, offsets, counts, auxiliary, scaled_dual):
    coils, _, xl, length_y, _ = sensitivity.shape
    n = lax.axis_size("slab")
    shares = lax.axis_size("coil")
    kl = length_y // n
    y_fwd = complex_table(length_y, False)
    y_inv = complex_table(length_y, True)
    x_fwd = complex_table(n * xl, False)
    x_inv = complex_table(n * xl, True)
    flat_samples = samples.reshape(samples.shape[1], samples.shape[2], -1)

    def swap(parts):
        moved = [parts[0]]
        for off in range(1, n):
            ring = [(i, (i + off) % n) for i in range(n)]
            moved.append(lax.ppermute(parts[off], "slab", ring))
        return moved

    def tile_of(pieces, c):
        return tile_call(x_fwd, x_inv, pieces, blocks, flat_samples, offsets, counts, c, n, kl, xl)

    pieces, tiles, table = [], [], y_fwd
    for c in range(coils):
        half = list(forward_call(table, image, sensitivity, c, n, kl))
        table, half[0] = lax.optimization_barrier((table, half[0]))
        pieces.append(swap(half))
    for c in range(coils):
        if c:
            pieces[c][0], tiles[-1][0] = lax.optimization_barrier((pieces[c][0], tiles[-1][0]))
        tiles.append(list(tile_of(pieces[c], c)))
    early = max(coils - 2, 0)
    backs = list(tiles)
    for c in range(early):
        backs[c] = swap(tiles[c])
    gradient = finish_call(y_inv, backs, coils - early, sensitivity, shares, n, kl)
    position = lax.axis_index("coil").astype(jnp.int32).reshape(1)
    return tuple(update_call(image, gradient, auxiliary, scaled_dual, position))


def solution(mesh):
    return jax.shard_map(
        body,
        mesh=mesh,
        in_specs=(
            P(None, "slab", None, None),
            P("coil", None, "slab", None, None),
            P("slab", None, None, None),
            P("slab", None, None, "coil", None, None),
            P("slab", None),
            P("slab"),
            P(None, "slab", "coil", None),
            P(None, "slab", "coil", None),
        ),
        out_specs=(
            P(None, "slab", "coil", None),
            P(None, "slab", "coil", None),
            P(None, "slab", "coil", None),
        ),
        check_vma=False,
    )
```

```python
import functools
import math

import jax
import jax.numpy as jnp
import numpy as np
from jax import lax
from jax.experimental import pallas as pl
from jax.experimental.pallas import tpu as pltpu
from jax.sharding import PartitionSpec as P

step_size = 0.5
penalty = 1.0
threshold = 0.3
VMEM_LIMIT = 67000000
F32 = jnp.float32
BF16 = jnp.bfloat16


def complex_table(length, inverse):
    index = np.arange(length, dtype=np.int64)
    angle = (index[:, None] * index[None, :] % length).astype(np.float64) * (2.0 * math.pi / length)
    factor = 1.0 / math.sqrt(length)
    re = np.cos(angle) * factor
    im = -np.sin(angle) * factor
    if inverse:
        whole = np.block([[re, im], [-im, re]])
    else:
        whole = np.block([[re, -im], [im, re]])
    return jnp.asarray(whole.astype(np.float32)).astype(BF16)


HBM = pl.BlockSpec(memory_space=pltpu.HBM)


def params(**extra):
    return pltpu.CompilerParams(vmem_limit_bytes=VMEM_LIMIT, **extra)


def once(shape):
    return pl.BlockSpec(shape, lambda *i: (0,) * len(shape), pipeline_mode=pl.Buffered(1))


def cost(flops, nbytes):
    return pl.CostEstimate(flops=int(flops), bytes_accessed=int(nbytes), transcendentals=0)


def pitch(rows):
    tiles = -(-rows // 8)
    return 8 * (tiles + 1 - tiles % 2)


def gather_rows(ref, row, parts_n):
    pieces = []
    for p in range(2):
        for s in range(parts_n):
            pieces.append(ref[s, p, row])
    return jnp.concatenate(pieces, axis=0)


def forward_kernel(n, kl, xp, table, image, sens, *refs):
    outs, flat = refs[:n], refs[n]
    rows, length = image.shape[1], image.shape[2]
    me = lax.axis_index("slab")
    step = pl.program_id(0)

    def pair(i, carry):
        columns = []
        for h in range(2):
            x = 2 * i + h
            sr = sens[0, 0, x].astype(F32)
            si = sens[0, 1, x].astype(F32)
            ir = image[0, x]
            ii = image[1, x]
            columns.append(
                jnp.concatenate(
                    [(sr * ir - si * ii).astype(BF16), (sr * ii + si * ir).astype(BF16)], axis=0
                )
            )
        both = jnp.concatenate(columns, axis=1)
        half = jnp.dot(table[...], both, preferred_element_type=F32)
        depth = half.shape[1] // 2
        for h in range(2):
            where = pl.ds(step * rows + 2 * i + h, 2 * length, stride=pitch(xp))
            flat[where, :] = half[:, h * depth : (h + 1) * depth]
        return carry

    lax.fori_loop(0, rows // 2, pair, 0)

    @pl.when(step == pl.num_programs(0) - 1)
    def last():
        for off in range(n):
            d = lax.rem(me + off, n)
            for p in range(2):

                def settle(k, carry):
                    base = pl.multiple_of(((p * n + d) * kl + 2 * k) * pitch(xp), 8)
                    for h in range(2):
                        outs[off][p, 2 * k + h] = flat[pl.ds(base + h * pitch(xp), xp), :].astype(BF16)
                    return carry

                lax.fori_loop(0, kl // 2, settle, 0, unroll=4)


def forward_call(table, image, sensitivity, coil, part, parts, n, kl):
    _, _, xl, length, depth = sensitivity.shape
    xp = xl // parts
    rows = 8 if xp % 8 == 0 else xp
    steps = xp // rows
    return pl.pallas_call(
        functools.partial(forward_kernel, n, kl, xp),
        grid=(steps,),
        in_specs=[
            once(table.shape),
            pl.BlockSpec((2, rows, length, depth), lambda i: (0, part * steps + i, 0, 0)),
            pl.BlockSpec((1, 2, rows, length, depth), lambda i: (coil, 0, part * steps + i, 0, 0)),
        ],
        out_specs=[once((2, kl, xp, depth))] * n,
        out_shape=[jax.ShapeDtypeStruct((2, kl, xp, depth), BF16)] * n,
        scratch_shapes=[pltpu.VMEM(((2 * length + 1) * pitch(xp), depth), F32)],
        compiler_params=params(),
        cost_estimate=cost(8 * length * length * xp * depth, 12 * xp * length * depth),
        name="forward",
    )(table, image, sensitivity)


def sort_kernel(samples, out, flat):
    parts = out.shape[0]
    psize = out.shape[2]
    depth = samples.shape[2]
    for g in range(samples.shape[0]):
        flat[...] = samples[g].astype(F32)
        for c in range(parts):
            for p in range(2):
                rows = flat[pl.ds(2 * c + p, psize, stride=2 * parts), :]
                out[c, g, :, p * depth : (p + 1) * depth] = rows.astype(BF16)


def sort_call(samples):
    _, slots, psize, coils, parts, depth = samples.shape
    group = 4 if slots % 4 == 0 else 1
    lines = psize * coils * parts
    return pl.pallas_call(
        sort_kernel,
        grid=(slots // group,),
        in_specs=[pl.BlockSpec((group, lines, depth), lambda i: (i, 0, 0))],
        out_specs=pl.BlockSpec((coils, group, psize, parts * depth), lambda i: (0, i, 0, 0)),
        out_shape=jax.ShapeDtypeStruct((coils, slots, psize, parts * depth), BF16),
        scratch_shapes=[pltpu.VMEM((lines, depth), F32)],
        compiler_params=params(),
        cost_estimate=cost(samples.size, 4 * samples.size),
        name="sort",
    )(samples.reshape(slots, lines, depth))


def tile_kernel(n, kl, xl, win, parts, coil, offsets, counts, fwd, inv, blocks, sorted_samples, *refs):
    pieces, outs, refs = refs[: n * parts], refs[n * parts : n * parts + n], refs[n * parts + n :]
    total, kspace, weights, piece, samples, leaving, sem, piece_sem, *wide = refs
    me = lax.axis_index("slab")
    copies = []
    xp = xl // parts
    for off in range(n):
        origin = lax.rem(me + n - off, n)
        for h in range(parts):
            target = piece.at[origin, :, :, pl.ds(h * xp, xp)]
            copies.append(pltpu.make_async_copy(pieces[h * n + off], target, piece_sem.at[h * n + off]))
    for copy in copies:
        copy.start()
    for copy in copies:
        copy.wait()
    fetches = [
        pltpu.make_async_copy(blocks.at[0], weights, sem.at[0]),
        pltpu.make_async_copy(sorted_samples.at[coil], samples, sem.at[1]),
    ]
    for fetch in fetches:
        fetch.start()
    length = n * xl
    depth = piece.shape[-1]
    if wide:
        source = wide[0]
        for p in range(2):
            for s in range(n):
                source[s, p] = piece[s, p].astype(F32)
    else:
        source = piece

    def to_kspace(i, carry):
        columns = []
        for h in range(2):
            columns.append(gather_rows(source, 2 * i + h, n).astype(BF16))
        spec = jnp.dot(fwd[...], jnp.concatenate(columns, axis=1), preferred_element_type=F32)
        for h in range(2):
            for p in range(2):
                total[p, pl.ds(2 * i + h, length, stride=pitch(kl)), :] = spec[
                    p * length : (p + 1) * length, h * depth : (h + 1) * depth
                ]
        return carry

    lax.fori_loop(0, kl // 2, to_kspace, 0)

    def settle(i, carry):
        rows = pl.ds(pl.multiple_of(i * pitch(kl), 8), kl)
        target = pl.ds(pl.multiple_of(i * kl, kl), kl)
        for p in range(2):
            kspace[target, p * depth : (p + 1) * depth] = total[p, rows, :].astype(kspace.dtype)
            total[p, rows, :] = jnp.zeros((kl, depth), F32)
        return carry

    lax.fori_loop(0, length, settle, 0, unroll=8)
    for fetch in fetches:
        fetch.wait()
    cells = win * kl
    chunk = min(cells, 512)

    def group(slot, carry):
        first = offsets[0, slot]
        start = pl.multiple_of(first * kl, kl)
        window = kspace[pl.ds(start, cells), :].astype(BF16)
        predicted = jnp.dot(weights[slot], window, preferred_element_type=F32)
        misfit = (predicted - samples[slot].astype(F32)).astype(BF16)
        for c in range(0, cells, chunk):
            update = lax.dot_general(
                weights[slot, :, c : c + chunk],
                misfit,
                (((0,), (0,)), ((), ())),
                preferred_element_type=F32,
            )
            for k in range(chunk // kl):
                rows = pl.ds(pl.multiple_of((first + c // kl + k) * pitch(kl), 8), kl)
                for p in range(2):
                    total[p, rows, :] += update[k * kl : (k + 1) * kl, p * depth : (p + 1) * depth]
        return carry

    lax.fori_loop(0, counts[0], group, 0)

    def to_rows(i, carry):
        columns = []
        for h in range(2):
            columns.append(
                jnp.concatenate(
                    [total[p, pl.ds(2 * i + h, length, stride=pitch(kl)), :].astype(BF16) for p in range(2)], axis=0
                )
            )
        back = jnp.dot(inv[...], jnp.concatenate(columns, axis=1), preferred_element_type=F32)
        for h in range(2):
            for p in range(2):
                total[p, pl.ds(2 * i + h, length, stride=pitch(kl)), :] = back[
                    p * length : (p + 1) * length, h * depth : (h + 1) * depth
                ]
        return carry

    lax.fori_loop(0, kl // 2, to_rows, 0)
    for off in range(n):
        d = lax.rem(me + off, n)
        for p in range(2):

            def leave(k, carry):
                base = pl.multiple_of((d * xl + 2 * k) * pitch(kl), 8)
                rows = [total[p, pl.ds(base + h * pitch(kl), kl), :] for h in range(2)]
                target = pl.ds(pl.multiple_of(2 * k * kl, 2 * kl), 2 * kl)
                leaving[off, p, target, :] = jnp.concatenate(rows, axis=0).astype(BF16)
                return carry

            lax.fori_loop(0, xl // 2, leave, 0, unroll=4)
        pltpu.make_async_copy(leaving.at[off], outs[off], piece_sem.at[off]).start()
    for off in range(n):
        pltpu.make_async_copy(leaving.at[off], outs[off], piece_sem.at[off]).wait()


def tile_call(fwd, inv, pieces, blocks, samples, offsets, counts, coil, n, kl, xl):
    depth = pieces[0].shape[-1]
    parts = len(pieces) // n
    _, slots, psize, cells = blocks.shape
    length = n * xl
    narrow = kl % 16 == 0 and xl % 16 == 0
    scratch = [
        pltpu.VMEM((2, (length + 1) * pitch(kl), depth), F32),
        pltpu.VMEM((length * kl, 2 * depth), BF16 if narrow else F32),
        pltpu.VMEM(blocks.shape[1:], BF16),
        pltpu.VMEM((n, 2, kl, xl, depth), BF16),
        pltpu.VMEM((slots, psize, 2 * depth), BF16),
        pltpu.VMEM((n, 2, xl * kl, depth), BF16),
        pltpu.SemaphoreType.DMA((2,)),
        pltpu.SemaphoreType.DMA((n * parts,)),
    ]
    if not narrow:
        scratch.append(pltpu.VMEM((n, 2, kl, xl, depth), F32))
    smem = pl.BlockSpec(memory_space=pltpu.SMEM)
    return pl.pallas_call(
        functools.partial(tile_kernel, n, kl, xl, cells // kl, parts, coil),
        grid=(1,),
        in_specs=[smem, smem, once(fwd.shape), once(inv.shape), HBM, HBM] + [HBM] * (n * parts),
        out_specs=[HBM] * n,
        out_shape=[jax.ShapeDtypeStruct((2, xl * kl, depth), BF16)] * n,
        scratch_shapes=scratch,
        compiler_params=params(),
        cost_estimate=cost(
            16 * length * length * kl * depth + 8 * slots * psize * cells * depth,
            8 * length * kl * depth + 2 * blocks.size,
        ),
        name="tile",
    )(offsets, counts, fwd, inv, blocks, samples, *pieces)


def finish_kernel(n, shares, kl, xl, chunks, sent, table, sens, *refs):
    coils = sens.shape[0]
    backs, refs = [refs[k * n : (k + 1) * n] for k in range(coils)], refs[coils * n :]
    out, landing, sens_v, grad, got, recv, send, local, grad_recv, grad_send, *wide = refs
    ready = coils - sent
    length = n * kl
    depth = landing.shape[-1]
    share = length // shares
    rows = xl // chunks
    band = rows * kl
    me = lax.axis_index("slab")
    mine = lax.axis_index("coil")

    barrier = pltpu.get_barrier_semaphore()

    def greet(off, carry):
        pl.semaphore_signal(
            barrier, inc=1, device_id={"slab": lax.rem(me + off, n)}, device_id_type=pl.DeviceIdType.MESH
        )
        return carry

    lax.fori_loop(1, n, greet, 0)
    for off in range(1, shares):
        pl.semaphore_signal(
            barrier, inc=1, device_id={"coil": lax.rem(mine + off, shares)}, device_id_type=pl.DeviceIdType.MESH
        )
    pl.semaphore_wait(barrier, n - 1 + shares - 1)

    def send_band(j, carry):
        where = pl.ds(pl.multiple_of(j * band, band), band)
        for k in range(ready, coils):
            for off in range(1, n):
                pltpu.make_async_remote_copy(
                    src_ref=backs[k][off].at[:, where, :],
                    dst_ref=landing.at[k, me, :, where, :],
                    send_sem=send,
                    recv_sem=recv.at[j],
                    device_id={"slab": lax.rem(me + off, n)},
                    device_id_type=pl.DeviceIdType.MESH,
                ).start()
        return carry

    lax.fori_loop(0, chunks, send_band, 0)
    copies = []
    for k in range(coils):
        for off in range(n if k < ready else 1):
            origin = lax.rem(me + n - off, n)
            copies.append(pltpu.make_async_copy(backs[k][off], landing.at[k, origin], local.at[k * n + off]))
        copies.append(pltpu.make_async_copy(sens.at[k], sens_v.at[k], local.at[coils * n + k]))
    for copy in copies:
        copy.start()
    for copy in copies:
        copy.wait()

    def do_band(j, carry):
        where = pl.ds(pl.multiple_of(j * band, band), band)
        arrived = landing.at[ready:coils, 0 : n - 1, :, where, :]
        pltpu.make_async_copy(arrived, arrived, recv.at[j]).wait()
        if wide:
            for k in range(coils):
                for s in range(n):
                    for p in range(2):
                        wide[0][k, s, p] = landing[k, s, p, where, :].astype(F32)

        def columns_of(k, i):
            pieces = []
            for p in range(2):
                for s in range(n):
                    if wide:
                        pieces.append(wide[0][k, s, p, pl.ds(pl.multiple_of(i * kl, kl), kl), :])
                    else:
                        row = pl.multiple_of((j * rows + i) * kl, kl)
                        pieces.append(landing[k, s, p, pl.ds(row, kl), :])
            return jnp.concatenate(pieces, axis=0).astype(BF16)

        def pair(i, carry):
            total = [[None, None], [None, None]]
            for k in range(coils):
                both = jnp.concatenate([columns_of(k, 2 * i), columns_of(k, 2 * i + 1)], axis=1)
                adj = jnp.dot(table[...], both, preferred_element_type=F32)
                adj = adj.astype(BF16).astype(F32)
                for h in range(2):
                    x = j * rows + 2 * i + h
                    ar = adj[:length, h * depth : (h + 1) * depth]
                    ai = adj[length:, h * depth : (h + 1) * depth]
                    sr = sens_v[k, 0, x].astype(F32)
                    si = sens_v[k, 1, x].astype(F32)
                    re = sr * ar + si * ai
                    im = sr * ai - si * ar
                    total[h] = [re, im] if k == 0 else [total[h][0] + re, total[h][1] + im]
            for h in range(2):
                x = j * rows + 2 * i + h
                for p in range(2):
                    for q in range(shares):
                        grad[q, p, x] = total[h][p][q * share : (q + 1) * share].astype(BF16)
            return carry

        lax.fori_loop(0, rows // 2, pair, 0)
        lines = pl.ds(j * rows, rows)
        for off in range(1, shares):
            target = lax.rem(mine + off, shares)
            pltpu.make_async_remote_copy(
                src_ref=grad.at[target, :, lines],
                dst_ref=got.at[mine, :, lines],
                send_sem=grad_send,
                recv_sem=grad_recv.at[j],
                device_id={"coil": target},
                device_id_type=pl.DeviceIdType.MESH,
            ).start()
        return carry

    lax.fori_loop(0, chunks, do_band, 0)

    def add_band(j, carry):
        arrived = got.at[0 : shares - 1, :, pl.ds(j * rows, rows)]
        pltpu.make_async_copy(arrived, arrived, grad_recv.at[j]).wait()

        def line(i, carry):
            x = j * rows + i
            for p in range(2):
                value = grad[mine, p, x].astype(F32)
                for off in range(1, shares):
                    value += got[lax.rem(mine + off, shares), p, x].astype(F32)
                out[p, x] = value
            return carry

        lax.fori_loop(0, rows, line, 0)
        return carry

    lax.fori_loop(0, chunks, add_band, 0)
    gone = landing.at[ready:coils, 0 : n - 1]
    pltpu.make_async_copy(gone, gone, send).wait()
    gone = got.at[0 : shares - 1]
    pltpu.make_async_copy(gone, gone, grad_send).wait()


def finish_call(table, backs, sent, sensitivity, shares, n, kl):
    coils, _, xl, length, depth = sensitivity.shape
    chunks = xl // 2 if xl % 2 == 0 else 1
    rows = xl // chunks
    share = length // shares
    vmem = pl.BlockSpec(memory_space=pltpu.VMEM)
    scratch = [
        pltpu.VMEM((coils, n, 2, xl * kl, depth), BF16),
        pltpu.VMEM(sensitivity.shape, BF16),
        pltpu.VMEM((shares, 2, xl, share, depth), BF16),
        pltpu.VMEM((shares, 2, xl, share, depth), BF16),
        pltpu.SemaphoreType.DMA((chunks,)),
        pltpu.SemaphoreType.DMA,
        pltpu.SemaphoreType.DMA((coils * n + coils,)),
        pltpu.SemaphoreType.DMA((chunks,)),
        pltpu.SemaphoreType.DMA,
    ]
    if kl % 16:
        scratch.append(pltpu.VMEM((coils, n, 2, rows * kl, depth), F32))
    return pl.pallas_call(
        functools.partial(finish_kernel, n, shares, kl, xl, chunks, sent),
        in_specs=[vmem, HBM] + [HBM] * (coils * n),
        out_specs=vmem,
        out_shape=jax.ShapeDtypeStruct((2, xl, share, depth), F32),
        scratch_shapes=scratch,
        compiler_params=params(collective_id=0, has_side_effects=True),
        name="finish",
    )(table, sensitivity, *[piece for back in backs for piece in back])


def haar_rows(first, second):
    even = lax.broadcasted_iota(jnp.int32, first.shape, 0) % 2 == 0
    rows = first.shape[0]

    def along(v):
        after = pltpu.roll(v, rows - 1, 0)
        ahead = pltpu.roll(v, 1, 0)
        return jnp.where(even, v + after, ahead - v) * 0.5

    return along(first + second), along(first - second)


def update_kernel(where, image, gradient, auxiliary, dual, image_out, aux_out, dual_out):
    del where
    rows = image.shape[1]
    for m in range(0, rows, 2):
        coeffs = []
        for p in range(2):
            target = haar_rows(
                auxiliary[p, m] - dual[p, m], auxiliary[p, m + 1] - dual[p, m + 1]
            )
            following = []
            for h in range(2):
                current = image[p, m + h]
                value = current - step_size * (
                    gradient[p, m + h].astype(F32) + penalty * (current - target[h])
                )
                image_out[p, m + h] = value
                following.append(value)
            spread = haar_rows(*following)
            coeffs.append([spread[h] + dual[p, m + h] for h in range(2)])
        for h in range(2):
            re, im = coeffs[0][h], coeffs[1][h]
            magnitude = jnp.sqrt(re * re + im * im)
            factor = jnp.maximum(1.0 - threshold / jnp.maximum(magnitude, threshold), 0.0)
            for p, value in enumerate((re, im)):
                kept = value * factor
                aux_out[p, m + h] = kept
                dual_out[p, m + h] = value - kept


def update_call(image, gradient, auxiliary, dual, position):
    _, xl, share, depth = auxiliary.shape
    rows = 4 if xl % 4 == 0 else 2
    block = (2, rows, share, depth)
    plain = pl.BlockSpec(block, lambda i, w: (0, i, 0, 0))
    shape = jax.ShapeDtypeStruct(auxiliary.shape, F32)
    return pl.pallas_call(
        update_kernel,
        grid_spec=pltpu.PrefetchScalarGridSpec(
            num_scalar_prefetch=1,
            grid=(xl // rows,),
            in_specs=[pl.BlockSpec(block, lambda i, w: (0, i, w[0], 0)), plain, plain, plain],
            out_specs=[plain, plain, plain],
        ),
        out_shape=[shape, shape, shape],
        compiler_params=params(),
        name="update",
    )(position, image, gradient, auxiliary, dual)


def body(image, sensitivity, blocks, samples, offsets, counts, auxiliary, scaled_dual):
    coils, _, xl, length_y, _ = sensitivity.shape
    n = lax.axis_size("slab")
    shares = lax.axis_size("coil")
    kl = length_y // n
    y_fwd = complex_table(length_y, False)
    y_inv = complex_table(length_y, True)
    x_fwd = complex_table(n * xl, False)
    x_inv = complex_table(n * xl, True)

    def swap(parts):
        moved = [parts[0]]
        for off in range(1, n):
            ring = [(i, (i + off) % n) for i in range(n)]
            moved.append(lax.ppermute(parts[off], "slab", ring))
        return moved

    def tile_of(pieces, c):
        return tile_call(x_fwd, x_inv, pieces, blocks, sorted_samples, offsets, counts, c, n, kl, xl)

    pieces, tiles, table = [], [], y_fwd
    for c in range(coils):
        parts = 2 if c == 0 and xl % 32 == 0 else 1
        moved = []
        for part in range(parts):
            half = list(forward_call(table, image, sensitivity, c, part, parts, n, kl))
            table, half[0] = lax.optimization_barrier((table, half[0]))
            moved += swap(half)
        pieces.append(moved)
    table, samples = lax.optimization_barrier((table, samples))
    sorted_samples = sort_call(samples)
    for c in range(coils):
        if c:
            pieces[c][0], tiles[-1][0] = lax.optimization_barrier((pieces[c][0], tiles[-1][0]))
        tiles.append(list(tile_of(pieces[c], c)))
    early = max(coils - 2, 0)
    backs = list(tiles)
    for c in range(early):
        backs[c] = swap(tiles[c])
    gradient = finish_call(y_inv, backs, coils - early, sensitivity, shares, n, kl)
    position = lax.axis_index("coil").astype(jnp.int32).reshape(1)
    return tuple(update_call(image, gradient, auxiliary, scaled_dual, position))


def solution(mesh):
    return jax.shard_map(
        body,
        mesh=mesh,
        in_specs=(
            P(None, "slab", None, None),
            P("coil", None, "slab", None, None),
            P("slab", None, None, None),
            P("slab", None, None, "coil", None, None),
            P("slab", None),
            P("slab"),
            P(None, "slab", "coil", None),
            P(None, "slab", "coil", None),
        ),
        out_specs=(
            P(None, "slab", "coil", None),
            P(None, "slab", "coil", None),
            P(None, "slab", "coil", None),
        ),
        check_vma=False,
    )
```

```python
import functools
import math

import jax
import jax.numpy as jnp
import numpy as np
from jax import lax
from jax.experimental import pallas as pl
from jax.experimental.pallas import tpu as pltpu
from jax.sharding import PartitionSpec as P

step_size = 0.5
penalty = 1.0
threshold = 0.3
VMEM_LIMIT = 67000000
LAG = 3
F32 = jnp.float32
BF16 = jnp.bfloat16


def complex_table(length, inverse):
    index = np.arange(length, dtype=np.int64)
    angle = (index[:, None] * index[None, :] % length).astype(np.float64) * (2.0 * math.pi / length)
    factor = 1.0 / math.sqrt(length)
    re = np.cos(angle) * factor
    im = -np.sin(angle) * factor
    if inverse:
        whole = np.block([[re, im], [-im, re]])
    else:
        whole = np.block([[re, -im], [im, re]])
    return jnp.asarray(whole.astype(np.float32)).astype(BF16)


HBM = pl.BlockSpec(memory_space=pltpu.HBM)


def params(limit=VMEM_LIMIT, **extra):
    return pltpu.CompilerParams(vmem_limit_bytes=limit, **extra)


def once(shape):
    return pl.BlockSpec(shape, lambda *i: (0,) * len(shape), pipeline_mode=pl.Buffered(1))


def cost(flops, nbytes):
    return pl.CostEstimate(flops=int(flops), bytes_accessed=int(nbytes), transcendentals=0)


def pitch(rows):
    tiles = -(-rows // 8)
    return 8 * (tiles + 1 - tiles % 2)


def gather_rows(ref, row, parts_n):
    pieces = []
    for p in range(2):
        for s in range(parts_n):
            pieces.append(ref[s, p, row])
    return jnp.concatenate(pieces, axis=0)


def forward_kernel(n, kl, xp, table, image, sens, *refs):
    outs, flat = refs[:n], refs[n]
    rows, length = image.shape[1], image.shape[2]
    me = lax.axis_index("slab")
    step = pl.program_id(0)

    def pair(i, carry):
        columns = []
        for h in range(2):
            x = 2 * i + h
            sr = sens[0, 0, x].astype(F32)
            si = sens[0, 1, x].astype(F32)
            ir = image[0, x]
            ii = image[1, x]
            columns.append(
                jnp.concatenate(
                    [(sr * ir - si * ii).astype(BF16), (sr * ii + si * ir).astype(BF16)], axis=0
                )
            )
        both = jnp.concatenate(columns, axis=1)
        half = jnp.dot(table[...], both, preferred_element_type=F32)
        depth = half.shape[1] // 2
        for h in range(2):
            where = pl.ds(step * rows + 2 * i + h, 2 * length, stride=pitch(xp))
            flat[where, :] = half[:, h * depth : (h + 1) * depth]
        return carry

    lax.fori_loop(0, rows // 2, pair, 0, unroll=2)

    @pl.when(step == pl.num_programs(0) - 1)
    def last():
        for off in range(n):
            d = lax.rem(me + off, n)
            for p in range(2):

                def settle(k, carry):
                    base = pl.multiple_of(((p * n + d) * kl + 2 * k) * pitch(xp), 8)
                    for h in range(2):
                        outs[off][p, 2 * k + h] = flat[pl.ds(base + h * pitch(xp), xp), :].astype(BF16)
                    return carry

                lax.fori_loop(0, kl // 2, settle, 0, unroll=4)


def forward_call(table, image, sensitivity, coil, part, parts, n, kl):
    _, _, xl, length, depth = sensitivity.shape
    xp = xl // parts
    rows = 8 if xp % 8 == 0 else xp
    steps = xp // rows
    return pl.pallas_call(
        functools.partial(forward_kernel, n, kl, xp),
        grid=(steps,),
        in_specs=[
            once(table.shape),
            pl.BlockSpec((2, rows, length, depth), lambda i: (0, part * steps + i, 0, 0)),
            pl.BlockSpec((1, 2, rows, length, depth), lambda i: (coil, 0, part * steps + i, 0, 0)),
        ],
        out_specs=[once((2, kl, xp, depth))] * n,
        out_shape=[jax.ShapeDtypeStruct((2, kl, xp, depth), BF16)] * n,
        scratch_shapes=[pltpu.VMEM(((2 * length + 1) * pitch(xp), depth), F32)],
        compiler_params=params(),
        cost_estimate=cost(8 * length * length * xp * depth, 12 * xp * length * depth),
        name="forward",
    )(table, image, sensitivity)


def sort_kernel(samples, out, flat):
    parts = out.shape[0]
    psize = out.shape[2]
    depth = samples.shape[2]
    for g in range(samples.shape[0]):
        flat[...] = samples[g].astype(F32)
        for c in range(parts):
            for p in range(2):
                rows = flat[pl.ds(2 * c + p, psize, stride=2 * parts), :]
                out[c, g, :, p * depth : (p + 1) * depth] = rows.astype(BF16)


def sort_call(samples):
    _, slots, psize, coils, parts, depth = samples.shape
    group = 4 if slots % 4 == 0 else 1
    lines = psize * coils * parts
    return pl.pallas_call(
        sort_kernel,
        grid=(slots // group,),
        in_specs=[pl.BlockSpec((group, lines, depth), lambda i: (i, 0, 0))],
        out_specs=pl.BlockSpec((coils, group, psize, parts * depth), lambda i: (0, i, 0, 0)),
        out_shape=jax.ShapeDtypeStruct((coils, slots, psize, parts * depth), BF16),
        scratch_shapes=[pltpu.VMEM((lines, depth), F32)],
        compiler_params=params(),
        cost_estimate=cost(samples.size, 4 * samples.size),
        name="sort",
    )(samples.reshape(slots, lines, depth))


def tile_kernel(n, kl, xl, win, parts, coil, offsets, counts, fwd, inv, blocks, sorted_samples, *refs):
    pieces, outs, refs = refs[: n * parts], refs[n * parts : n * parts + n], refs[n * parts + n :]
    total, kspace, weights, piece, samples, leaving, sem, piece_sem, *wide = refs
    me = lax.axis_index("slab")
    copies = []
    xp = xl // parts
    for off in range(n):
        origin = lax.rem(me + n - off, n)
        for h in range(parts):
            target = piece.at[origin, :, :, pl.ds(h * xp, xp)]
            copies.append(pltpu.make_async_copy(pieces[h * n + off], target, piece_sem.at[h * n + off]))
    for copy in copies:
        copy.start()
    for copy in copies:
        copy.wait()
    fetches = [
        pltpu.make_async_copy(blocks.at[0], weights, sem.at[0]),
        pltpu.make_async_copy(sorted_samples.at[coil], samples, sem.at[1]),
    ]
    for fetch in fetches:
        fetch.start()
    length = n * xl
    depth = piece.shape[-1]
    if wide:
        source = wide[0]
        for p in range(2):
            for s in range(n):
                source[s, p] = piece[s, p].astype(F32)
    else:
        source = piece

    def to_kspace(i, carry):
        columns = []
        for h in range(2):
            columns.append(gather_rows(source, 2 * i + h, n).astype(BF16))
        spec = jnp.dot(fwd[...], jnp.concatenate(columns, axis=1), preferred_element_type=F32)
        for h in range(2):
            for p in range(2):
                total[p, pl.ds(2 * i + h, length, stride=pitch(kl)), :] = spec[
                    p * length : (p + 1) * length, h * depth : (h + 1) * depth
                ]
        return carry

    lax.fori_loop(0, kl // 2, to_kspace, 0, unroll=2)

    def settle(i, carry):
        rows = pl.ds(pl.multiple_of(i * pitch(kl), 8), kl)
        target = pl.ds(pl.multiple_of(i * kl, kl), kl)
        for p in range(2):
            kspace[target, p * depth : (p + 1) * depth] = total[p, rows, :].astype(kspace.dtype)
            total[p, rows, :] = jnp.zeros((kl, depth), F32)
        return carry

    lax.fori_loop(0, length, settle, 0, unroll=8)
    for fetch in fetches:
        fetch.wait()
    cells = win * kl
    chunk = min(cells, 512)

    def misfit_of(slot):
        start = pl.multiple_of(offsets[0, slot] * kl, kl)
        window = kspace[pl.ds(start, cells), :].astype(BF16)
        predicted = jnp.dot(weights[slot], window, preferred_element_type=F32)
        return (predicted - samples[slot].astype(F32)).astype(BF16)

    def group(slot, misfit):
        following = misfit_of(jnp.minimum(slot + 1, weights.shape[0] - 1))
        first = offsets[0, slot]
        for c in range(0, cells, chunk):
            update = lax.dot_general(
                weights[slot, :, c : c + chunk],
                misfit,
                (((0,), (0,)), ((), ())),
                preferred_element_type=F32,
            )
            for k in range(chunk // kl):
                rows = pl.ds(pl.multiple_of((first + c // kl + k) * pitch(kl), 8), kl)
                for p in range(2):
                    total[p, rows, :] += update[k * kl : (k + 1) * kl, p * depth : (p + 1) * depth]
        return following

    lax.fori_loop(0, counts[0], group, misfit_of(0))

    def to_rows(i, carry):
        columns = []
        for h in range(2):
            columns.append(
                jnp.concatenate(
                    [total[p, pl.ds(2 * i + h, length, stride=pitch(kl)), :].astype(BF16) for p in range(2)], axis=0
                )
            )
        back = jnp.dot(inv[...], jnp.concatenate(columns, axis=1), preferred_element_type=F32)
        for h in range(2):
            for p in range(2):
                total[p, pl.ds(2 * i + h, length, stride=pitch(kl)), :] = back[
                    p * length : (p + 1) * length, h * depth : (h + 1) * depth
                ]
        return carry

    lax.fori_loop(0, kl // 2, to_rows, 0, unroll=2)
    for off in range(n):
        d = lax.rem(me + off, n)
        for p in range(2):

            def leave(k, carry):
                base = pl.multiple_of((d * xl + 2 * k) * pitch(kl), 8)
                rows = [total[p, pl.ds(base + h * pitch(kl), kl), :] for h in range(2)]
                target = pl.ds(pl.multiple_of(2 * k * kl, 2 * kl), 2 * kl)
                leaving[off, p, target, :] = jnp.concatenate(rows, axis=0).astype(BF16)
                return carry

            lax.fori_loop(0, xl // 2, leave, 0, unroll=4)
        pltpu.make_async_copy(leaving.at[off], outs[off], piece_sem.at[off]).start()
    for off in range(n):
        pltpu.make_async_copy(leaving.at[off], outs[off], piece_sem.at[off]).wait()


def tile_call(fwd, inv, pieces, blocks, samples, offsets, counts, coil, n, kl, xl):
    depth = pieces[0].shape[-1]
    parts = len(pieces) // n
    _, slots, psize, cells = blocks.shape
    length = n * xl
    narrow = kl % 16 == 0 and xl % 16 == 0
    scratch = [
        pltpu.VMEM((2, (length + 1) * pitch(kl), depth), F32),
        pltpu.VMEM((length * kl, 2 * depth), BF16 if narrow else F32),
        pltpu.VMEM(blocks.shape[1:], BF16),
        pltpu.VMEM((n, 2, kl, xl, depth), BF16),
        pltpu.VMEM((slots, psize, 2 * depth), BF16),
        pltpu.VMEM((n, 2, xl * kl, depth), BF16),
        pltpu.SemaphoreType.DMA((2,)),
        pltpu.SemaphoreType.DMA((n * parts,)),
    ]
    if not narrow:
        scratch.append(pltpu.VMEM((n, 2, kl, xl, depth), F32))
    smem = pl.BlockSpec(memory_space=pltpu.SMEM)
    return pl.pallas_call(
        functools.partial(tile_kernel, n, kl, xl, cells // kl, parts, coil),
        grid=(1,),
        in_specs=[smem, smem, once(fwd.shape), once(inv.shape), HBM, HBM] + [HBM] * (n * parts),
        out_specs=[HBM] * n,
        out_shape=[jax.ShapeDtypeStruct((2, xl * kl, depth), BF16)] * n,
        scratch_shapes=scratch,
        compiler_params=params(),
        cost_estimate=cost(
            16 * length * length * kl * depth + 8 * slots * psize * cells * depth,
            8 * length * kl * depth + 2 * blocks.size,
        ),
        name="tile",
    )(offsets, counts, fwd, inv, blocks, samples, *pieces)


def finish_kernel(n, shares, kl, xl, chunks, sent, table, sens, *refs):
    coils = sens.shape[0]
    backs, refs = [refs[k * n : (k + 1) * n] for k in range(coils)], refs[coils * n :]
    out, landing, sens_v, grad, got, recv, send, local, grad_recv, grad_send, *wide = refs
    ready = coils - sent
    length = n * kl
    depth = landing.shape[-1]
    share = length // shares
    rows = xl // chunks
    band = rows * kl
    me = lax.axis_index("slab")
    mine = lax.axis_index("coil")

    barrier = pltpu.get_barrier_semaphore()

    def greet(off, carry):
        pl.semaphore_signal(
            barrier, inc=1, device_id={"slab": lax.rem(me + off, n)}, device_id_type=pl.DeviceIdType.MESH
        )
        return carry

    lax.fori_loop(1, n, greet, 0)
    for off in range(1, shares):
        pl.semaphore_signal(
            barrier, inc=1, device_id={"coil": lax.rem(mine + off, shares)}, device_id_type=pl.DeviceIdType.MESH
        )
    pl.semaphore_wait(barrier, n - 1 + shares - 1)

    def send_band(j, carry):
        where = pl.ds(pl.multiple_of(j * band, band), band)
        for k in range(ready, coils):
            for off in range(1, n):
                pltpu.make_async_remote_copy(
                    src_ref=backs[k][off].at[:, where, :],
                    dst_ref=landing.at[k, me, :, where, :],
                    send_sem=send,
                    recv_sem=recv.at[j],
                    device_id={"slab": lax.rem(me + off, n)},
                    device_id_type=pl.DeviceIdType.MESH,
                ).start()
        return carry

    lax.fori_loop(0, chunks, send_band, 0)
    copies = []
    for k in range(coils):
        for off in range(n if k < ready else 1):
            origin = lax.rem(me + n - off, n)
            copies.append(pltpu.make_async_copy(backs[k][off], landing.at[k, origin], local.at[k * n + off]))
        copies.append(pltpu.make_async_copy(sens.at[k], sens_v.at[k], local.at[coils * n + k]))
    for copy in copies:
        copy.start()
    for copy in copies:
        copy.wait()

    def add_band(j, carry):
        arrived = got.at[0 : shares - 1, :, pl.ds(j * rows, rows)]
        pltpu.make_async_copy(arrived, arrived, grad_recv.at[j]).wait()

        def line(i, carry):
            x = j * rows + i
            for p in range(2):
                value = grad[mine, p, x].astype(F32)
                for off in range(1, shares):
                    value += got[lax.rem(mine + off, shares), p, x].astype(F32)
                out[p, x] = value
            return carry

        lax.fori_loop(0, rows, line, 0)
        return carry

    def do_band(j, carry):
        where = pl.ds(pl.multiple_of(j * band, band), band)
        arrived = landing.at[ready:coils, 0 : n - 1, :, where, :]
        pltpu.make_async_copy(arrived, arrived, recv.at[j]).wait()
        if wide:
            for k in range(coils):
                for s in range(n):
                    for p in range(2):
                        wide[0][k, s, p] = landing[k, s, p, where, :].astype(F32)

        def columns_of(k, i):
            pieces = []
            for p in range(2):
                for s in range(n):
                    if wide:
                        pieces.append(wide[0][k, s, p, pl.ds(pl.multiple_of(i * kl, kl), kl), :])
                    else:
                        row = pl.multiple_of((j * rows + i) * kl, kl)
                        pieces.append(landing[k, s, p, pl.ds(row, kl), :])
            return jnp.concatenate(pieces, axis=0).astype(BF16)

        def pair(i, carry):
            total = [[None, None], [None, None]]
            for k in range(coils):
                both = jnp.concatenate([columns_of(k, 2 * i), columns_of(k, 2 * i + 1)], axis=1)
                adj = jnp.dot(table[...], both, preferred_element_type=F32)
                adj = adj.astype(BF16).astype(F32)
                for h in range(2):
                    x = j * rows + 2 * i + h
                    ar = adj[:length, h * depth : (h + 1) * depth]
                    ai = adj[length:, h * depth : (h + 1) * depth]
                    sr = sens_v[k, 0, x].astype(F32)
                    si = sens_v[k, 1, x].astype(F32)
                    re = sr * ar + si * ai
                    im = sr * ai - si * ar
                    total[h] = [re, im] if k == 0 else [total[h][0] + re, total[h][1] + im]
            for h in range(2):
                x = j * rows + 2 * i + h
                for p in range(2):
                    for q in range(shares):
                        grad[q, p, x] = total[h][p][q * share : (q + 1) * share].astype(BF16)
            return carry

        lax.fori_loop(0, rows // 2, pair, 0)
        lines = pl.ds(j * rows, rows)
        for off in range(1, shares):
            target = lax.rem(mine + off, shares)
            pltpu.make_async_remote_copy(
                src_ref=grad.at[target, :, lines],
                dst_ref=got.at[mine, :, lines],
                send_sem=grad_send,
                recv_sem=grad_recv.at[j],
                device_id={"coil": target},
                device_id_type=pl.DeviceIdType.MESH,
            ).start()

        @pl.when(j >= LAG)
        def settled():
            add_band(j - LAG, 0)

        return carry

    lax.fori_loop(0, chunks, do_band, 0)
    lax.fori_loop(max(chunks - LAG, 0), chunks, add_band, 0)
    gone = landing.at[ready:coils, 0 : n - 1]
    pltpu.make_async_copy(gone, gone, send).wait()
    gone = got.at[0 : shares - 1]
    pltpu.make_async_copy(gone, gone, grad_send).wait()


def finish_call(table, backs, sent, sensitivity, shares, n, kl):
    coils, _, xl, length, depth = sensitivity.shape
    chunks = xl // 2 if xl % 2 == 0 else 1
    rows = xl // chunks
    share = length // shares
    vmem = pl.BlockSpec(memory_space=pltpu.VMEM)
    scratch = [
        pltpu.VMEM((coils, n, 2, xl * kl, depth), BF16),
        pltpu.VMEM(sensitivity.shape, BF16),
        pltpu.VMEM((shares, 2, xl, share, depth), BF16),
        pltpu.VMEM((shares, 2, xl, share, depth), BF16),
        pltpu.SemaphoreType.DMA((chunks,)),
        pltpu.SemaphoreType.DMA,
        pltpu.SemaphoreType.DMA((coils * n + coils,)),
        pltpu.SemaphoreType.DMA((chunks,)),
        pltpu.SemaphoreType.DMA,
    ]
    if kl % 16:
        scratch.append(pltpu.VMEM((coils, n, 2, rows * kl, depth), F32))
    limit = VMEM_LIMIT - 24 * xl * share * depth
    return pl.pallas_call(
        functools.partial(finish_kernel, n, shares, kl, xl, chunks, sent),
        in_specs=[vmem, HBM] + [HBM] * (coils * n),
        out_specs=vmem,
        out_shape=jax.ShapeDtypeStruct((2, xl, share, depth), F32),
        scratch_shapes=scratch,
        compiler_params=params(limit, collective_id=0, has_side_effects=True),
        name="finish",
    )(table, sensitivity, *[piece for back in backs for piece in back])


def haar_rows(first, second):
    even = lax.broadcasted_iota(jnp.int32, first.shape, 0) % 2 == 0
    rows = first.shape[0]

    def along(v):
        after = pltpu.roll(v, rows - 1, 0)
        ahead = pltpu.roll(v, 1, 0)
        return jnp.where(even, v + after, ahead - v) * 0.5

    return along(first + second), along(first - second)


def update_kernel(image, gradient, auxiliary, dual, image_out, aux_out, dual_out):
    rows = image.shape[1]
    for m in range(0, rows, 2):
        coeffs = []
        for p in range(2):
            target = haar_rows(
                auxiliary[p, m] - dual[p, m], auxiliary[p, m + 1] - dual[p, m + 1]
            )
            following = []
            for h in range(2):
                current = image[p, m + h]
                value = current - step_size * (
                    gradient[p, m + h].astype(F32) + penalty * (current - target[h])
                )
                image_out[p, m + h] = value
                following.append(value)
            spread = haar_rows(*following)
            coeffs.append([spread[h] + dual[p, m + h] for h in range(2)])
        for h in range(2):
            re, im = coeffs[0][h], coeffs[1][h]
            magnitude = jnp.sqrt(re * re + im * im)
            factor = jnp.maximum(1.0 - threshold / jnp.maximum(magnitude, threshold), 0.0)
            for p, value in enumerate((re, im)):
                kept = value * factor
                aux_out[p, m + h] = kept
                dual_out[p, m + h] = value - kept


def update_call(image, gradient, auxiliary, dual):
    _, xl, share, depth = auxiliary.shape
    rows = 8 if xl % 8 == 0 else 2
    plain = pl.BlockSpec((2, rows, share, depth), lambda i: (0, i, 0, 0))
    shape = jax.ShapeDtypeStruct(auxiliary.shape, F32)
    return pl.pallas_call(
        update_kernel,
        grid=(xl // rows,),
        in_specs=[plain, plain, plain, plain],
        out_specs=[plain, plain, plain],
        out_shape=[shape, shape, shape],
        compiler_params=params(VMEM_LIMIT - 24 * xl * share * depth),
        name="update",
    )(image, gradient, auxiliary, dual)


def body(image, sensitivity, blocks, samples, offsets, counts, auxiliary, scaled_dual):
    coils, _, xl, length_y, _ = sensitivity.shape
    n = lax.axis_size("slab")
    shares = lax.axis_size("coil")
    kl = length_y // n
    y_fwd = complex_table(length_y, False)
    y_inv = complex_table(length_y, True)
    x_fwd = complex_table(n * xl, False)
    x_inv = complex_table(n * xl, True)

    def swap(parts):
        moved = [parts[0]]
        for off in range(1, n):
            ring = [(i, (i + off) % n) for i in range(n)]
            moved.append(lax.ppermute(parts[off], "slab", ring))
        return moved

    def tile_of(pieces, c):
        return tile_call(x_fwd, x_inv, pieces, blocks, sorted_samples, offsets, counts, c, n, kl, xl)

    share = length_y // shares
    pieces, tiles, table = [], [], y_fwd
    for c in range(coils):
        parts = 2 if c == 0 and xl % 32 == 0 else 1
        moved = []
        for part in range(parts):
            half = list(forward_call(table, image, sensitivity, c, part, parts, n, kl))
            table, half[0] = lax.optimization_barrier((table, half[0]))
            moved += swap(half)
        pieces.append(moved)
    table, samples, source = lax.optimization_barrier((table, samples, image))
    sorted_samples = sort_call(samples)
    current = lax.dynamic_slice_in_dim(source, lax.axis_index("coil") * share, share, 2)
    for c in range(coils):
        if c:
            pieces[c][0], tiles[-1][0] = lax.optimization_barrier((pieces[c][0], tiles[-1][0]))
        tiles.append(list(tile_of(pieces[c], c)))
    early = max(coils - 3, 0)
    backs = list(tiles)
    for c in range(early):
        backs[c] = swap(tiles[c])
    gradient = finish_call(y_inv, backs, coils - early, sensitivity, shares, n, kl)
    return tuple(update_call(current, gradient, auxiliary, scaled_dual))


def solution(mesh):
    return jax.shard_map(
        body,
        mesh=mesh,
        in_specs=(
            P(None, "slab", None, None),
            P("coil", None, "slab", None, None),
            P("slab", None, None, None),
            P("slab", None, None, "coil", None, None),
            P("slab", None),
            P("slab"),
            P(None, "slab", "coil", None),
            P(None, "slab", "coil", None),
        ),
        out_specs=(
            P(None, "slab", "coil", None),
            P(None, "slab", "coil", None),
            P(None, "slab", "coil", None),
        ),
        check_vma=False,
    )
```

```python
import functools
import math

import jax
import jax.numpy as jnp
import numpy as np
from jax import lax
from jax.experimental import pallas as pl
from jax.experimental.pallas import tpu as pltpu
from jax.sharding import PartitionSpec as P

step_size = 0.5
penalty = 1.0
threshold = 0.3
VMEM_LIMIT = 67000000
LAG = 3
F32 = jnp.float32
BF16 = jnp.bfloat16


def complex_table(length, inverse):
    index = np.arange(length, dtype=np.int64)
    angle = (index[:, None] * index[None, :] % length).astype(np.float64) * (2.0 * math.pi / length)
    factor = 1.0 / math.sqrt(length)
    re = np.cos(angle) * factor
    im = -np.sin(angle) * factor
    if inverse:
        whole = np.block([[re, im], [-im, re]])
    else:
        whole = np.block([[re, -im], [im, re]])
    return jnp.asarray(whole.astype(np.float32)).astype(BF16)


HBM = pl.BlockSpec(memory_space=pltpu.HBM)


def params(limit=VMEM_LIMIT, **extra):
    return pltpu.CompilerParams(vmem_limit_bytes=limit, **extra)


def partner(me, off, n):
    other, bit = me, 1
    while bit < n:
        if off & bit:
            other = other + bit * (1 - 2 * (me // bit % 2))
        bit *= 2
    return other


def turns(n):
    return [*range(2, n, 2), *range(3, n, 2), 1]


def once(shape):
    return pl.BlockSpec(shape, lambda *i: (0,) * len(shape), pipeline_mode=pl.Buffered(1))


def cost(flops, nbytes):
    return pl.CostEstimate(flops=int(flops), bytes_accessed=int(nbytes), transcendentals=0)


def pitch(rows):
    tiles = -(-rows // 8)
    return 8 * (tiles + 1 - tiles % 2)


def gather_rows(ref, row, parts_n):
    pieces = []
    for p in range(2):
        for s in range(parts_n):
            pieces.append(ref[s, p, row])
    return jnp.concatenate(pieces, axis=0)


def forward_kernel(n, kl, xp, table, image, sens, *refs):
    outs, flat = refs[:n], refs[n]
    rows, length = image.shape[1], image.shape[2]
    me = lax.axis_index("slab")
    step = pl.program_id(0)

    def pair(i, carry):
        columns = []
        for h in range(2):
            x = 2 * i + h
            sr = sens[0, 0, x].astype(F32)
            si = sens[0, 1, x].astype(F32)
            ir = image[0, x]
            ii = image[1, x]
            columns.append(
                jnp.concatenate(
                    [(sr * ir - si * ii).astype(BF16), (sr * ii + si * ir).astype(BF16)], axis=0
                )
            )
        both = jnp.concatenate(columns, axis=1)
        half = jnp.dot(table[...], both, preferred_element_type=F32)
        depth = half.shape[1] // 2
        for h in range(2):
            where = pl.ds(step * rows + 2 * i + h, 2 * length, stride=pitch(xp))
            flat[where, :] = half[:, h * depth : (h + 1) * depth]
        return carry

    lax.fori_loop(0, rows // 2, pair, 0, unroll=2)

    @pl.when(step == pl.num_programs(0) - 1)
    def last():
        for off in range(n):
            d = partner(me, off, n)
            for p in range(2):

                def settle(k, carry):
                    base = pl.multiple_of(((p * n + d) * kl + 2 * k) * pitch(xp), 8)
                    for h in range(2):
                        outs[off][p, 2 * k + h] = flat[pl.ds(base + h * pitch(xp), xp), :].astype(BF16)
                    return carry

                lax.fori_loop(0, kl // 2, settle, 0, unroll=4)


def forward_call(table, image, sensitivity, coil, first, xp, n, kl):
    _, _, _, length, depth = sensitivity.shape
    rows = 8 if xp % 8 == 0 else xp
    steps, skip = xp // rows, first // rows
    return pl.pallas_call(
        functools.partial(forward_kernel, n, kl, xp),
        grid=(steps,),
        in_specs=[
            once(table.shape),
            pl.BlockSpec((2, rows, length, depth), lambda i: (0, skip + i, 0, 0)),
            pl.BlockSpec((1, 2, rows, length, depth), lambda i: (coil, 0, skip + i, 0, 0)),
        ],
        out_specs=[once((2, kl, xp, depth))] * n,
        out_shape=[jax.ShapeDtypeStruct((2, kl, xp, depth), BF16)] * n,
        scratch_shapes=[pltpu.VMEM(((2 * length + 1) * pitch(xp), depth), F32)],
        compiler_params=params(),
        cost_estimate=cost(8 * length * length * xp * depth, 12 * xp * length * depth),
        name="forward",
    )(table, image, sensitivity)


def sort_kernel(samples, out, flat):
    parts = out.shape[0]
    psize = out.shape[2]
    depth = samples.shape[2]
    for g in range(samples.shape[0]):
        flat[...] = samples[g].astype(F32)
        for c in range(parts):
            for p in range(2):
                rows = flat[pl.ds(2 * c + p, psize, stride=2 * parts), :]
                out[c, g, :, p * depth : (p + 1) * depth] = rows.astype(BF16)


def sort_call(samples):
    _, slots, psize, coils, parts, depth = samples.shape
    group = 4 if slots % 4 == 0 else 1
    lines = psize * coils * parts
    return pl.pallas_call(
        sort_kernel,
        grid=(slots // group,),
        in_specs=[pl.BlockSpec((group, lines, depth), lambda i: (i, 0, 0))],
        out_specs=pl.BlockSpec((coils, group, psize, parts * depth), lambda i: (0, i, 0, 0)),
        out_shape=jax.ShapeDtypeStruct((coils, slots, psize, parts * depth), BF16),
        scratch_shapes=[pltpu.VMEM((lines, depth), F32)],
        compiler_params=params(),
        cost_estimate=cost(samples.size, 4 * samples.size),
        name="sort",
    )(samples.reshape(slots, lines, depth))


def tile_kernel(n, kl, xl, win, parts, coil, offsets, counts, fwd, inv, blocks, sorted_samples, *refs):
    count = n * len(parts)
    pieces, outs, refs = refs[:count], refs[count : count + n], refs[count + n :]
    total, kspace, weights, piece, samples, leaving, sem, piece_sem, *wide = refs
    me = lax.axis_index("slab")
    copies = []
    for off in range(n):
        for h, (start, size) in enumerate(parts):
            target = piece.at[partner(me, off, n), :, :, pl.ds(start, size)]
            copies.append(pltpu.make_async_copy(pieces[h * n + off], target, piece_sem.at[h * n + off]))
    for copy in copies:
        copy.start()
    for copy in copies:
        copy.wait()
    fetches = [
        pltpu.make_async_copy(blocks.at[0], weights, sem.at[0]),
        pltpu.make_async_copy(sorted_samples.at[coil], samples, sem.at[1]),
    ]
    for fetch in fetches:
        fetch.start()
    length = n * xl
    depth = piece.shape[-1]
    if wide:
        source = wide[0]
        for p in range(2):
            for s in range(n):
                source[s, p] = piece[s, p].astype(F32)
    else:
        source = piece

    def to_kspace(i, carry):
        columns = []
        for h in range(2):
            columns.append(gather_rows(source, 2 * i + h, n).astype(BF16))
        spec = jnp.dot(fwd[...], jnp.concatenate(columns, axis=1), preferred_element_type=F32)
        for h in range(2):
            for p in range(2):
                total[p, pl.ds(2 * i + h, length, stride=pitch(kl)), :] = spec[
                    p * length : (p + 1) * length, h * depth : (h + 1) * depth
                ]
        return carry

    lax.fori_loop(0, kl // 2, to_kspace, 0, unroll=2)

    def settle(i, carry):
        rows = pl.ds(pl.multiple_of(i * pitch(kl), 8), kl)
        target = pl.ds(pl.multiple_of(i * kl, kl), kl)
        for p in range(2):
            kspace[target, p * depth : (p + 1) * depth] = total[p, rows, :].astype(kspace.dtype)
            total[p, rows, :] = jnp.zeros((kl, depth), F32)
        return carry

    lax.fori_loop(0, length, settle, 0, unroll=8)
    for fetch in fetches:
        fetch.wait()
    cells = win * kl
    chunk = min(cells, 512)

    def misfit_of(slot):
        start = pl.multiple_of(offsets[0, slot] * kl, kl)
        window = kspace[pl.ds(start, cells), :].astype(BF16)
        predicted = jnp.dot(weights[slot], window, preferred_element_type=F32)
        return (predicted - samples[slot].astype(F32)).astype(BF16)

    def group(slot, misfit):
        following = misfit_of(jnp.minimum(slot + 1, weights.shape[0] - 1))
        first = offsets[0, slot]
        for c in range(0, cells, chunk):
            update = lax.dot_general(
                weights[slot, :, c : c + chunk],
                misfit,
                (((0,), (0,)), ((), ())),
                preferred_element_type=F32,
            )
            for k in range(chunk // kl):
                rows = pl.ds(pl.multiple_of((first + c // kl + k) * pitch(kl), 8), kl)
                for p in range(2):
                    total[p, rows, :] += update[k * kl : (k + 1) * kl, p * depth : (p + 1) * depth]
        return following

    lax.fori_loop(0, counts[0], group, misfit_of(0))

    def to_rows(i, carry):
        columns = []
        for h in range(2):
            columns.append(
                jnp.concatenate(
                    [total[p, pl.ds(2 * i + h, length, stride=pitch(kl)), :].astype(BF16) for p in range(2)], axis=0
                )
            )
        back = jnp.dot(inv[...], jnp.concatenate(columns, axis=1), preferred_element_type=F32)
        for h in range(2):
            for p in range(2):
                total[p, pl.ds(2 * i + h, length, stride=pitch(kl)), :] = back[
                    p * length : (p + 1) * length, h * depth : (h + 1) * depth
                ]
        return carry

    lax.fori_loop(0, kl // 2, to_rows, 0, unroll=2)
    for off in range(n):
        d = partner(me, off, n)
        for p in range(2):

            def leave(k, carry):
                base = pl.multiple_of((d * xl + 2 * k) * pitch(kl), 8)
                rows = [total[p, pl.ds(base + h * pitch(kl), kl), :] for h in range(2)]
                target = pl.ds(pl.multiple_of(2 * k * kl, 2 * kl), 2 * kl)
                leaving[off, p, target, :] = jnp.concatenate(rows, axis=0).astype(BF16)
                return carry

            lax.fori_loop(0, xl // 2, leave, 0, unroll=4)
        pltpu.make_async_copy(leaving.at[off], outs[off], piece_sem.at[off]).start()
    for off in range(n):
        pltpu.make_async_copy(leaving.at[off], outs[off], piece_sem.at[off]).wait()


def tile_call(fwd, inv, pieces, parts, blocks, samples, offsets, counts, coil, n, kl, xl):
    depth = pieces[0].shape[-1]
    _, slots, psize, cells = blocks.shape
    length = n * xl
    narrow = kl % 16 == 0 and xl % 16 == 0
    scratch = [
        pltpu.VMEM((2, (length + 1) * pitch(kl), depth), F32),
        pltpu.VMEM((length * kl, 2 * depth), BF16 if narrow else F32),
        pltpu.VMEM(blocks.shape[1:], BF16),
        pltpu.VMEM((n, 2, kl, xl, depth), BF16),
        pltpu.VMEM((slots, psize, 2 * depth), BF16),
        pltpu.VMEM((n, 2, xl * kl, depth), BF16),
        pltpu.SemaphoreType.DMA((2,)),
        pltpu.SemaphoreType.DMA((len(pieces),)),
    ]
    if not narrow:
        scratch.append(pltpu.VMEM((n, 2, kl, xl, depth), F32))
    smem = pl.BlockSpec(memory_space=pltpu.SMEM)
    return pl.pallas_call(
        functools.partial(tile_kernel, n, kl, xl, cells // kl, parts, coil),
        grid=(1,),
        in_specs=[smem, smem, once(fwd.shape), once(inv.shape), HBM, HBM] + [HBM] * len(pieces),
        out_specs=[HBM] * n,
        out_shape=[jax.ShapeDtypeStruct((2, xl * kl, depth), BF16)] * n,
        scratch_shapes=scratch,
        compiler_params=params(),
        cost_estimate=cost(
            16 * length * length * kl * depth + 8 * slots * psize * cells * depth,
            8 * length * kl * depth + 2 * blocks.size,
        ),
        name="tile",
    )(offsets, counts, fwd, inv, blocks, samples, *pieces)


def finish_kernel(n, shares, kl, xl, chunks, sent, table, sens, *refs):
    coils = sens.shape[0]
    backs, refs = [refs[k * n : (k + 1) * n] for k in range(coils)], refs[coils * n :]
    out, landing, sens_v, grad, got, recv, send, local, grad_recv, grad_send, *wide = refs
    ready = coils - sent
    length = n * kl
    depth = landing.shape[-1]
    share = length // shares
    rows = xl // chunks
    band = rows * kl
    group = min(rows, 2)
    me = lax.axis_index("slab")
    mine = lax.axis_index("coil")

    barrier = pltpu.get_barrier_semaphore()

    def greet(off, carry):
        pl.semaphore_signal(
            barrier, inc=1, device_id={"slab": lax.rem(me + off, n)}, device_id_type=pl.DeviceIdType.MESH
        )
        return carry

    lax.fori_loop(1, n, greet, 0)
    for off in range(1, shares):
        pl.semaphore_signal(
            barrier, inc=1, device_id={"coil": lax.rem(mine + off, shares)}, device_id_type=pl.DeviceIdType.MESH
        )
    pl.semaphore_wait(barrier, n - 1 + shares - 1)

    def send_band(j, carry):
        where = pl.ds(pl.multiple_of(j * band, band), band)
        for k in range(ready, coils):
            for off in turns(n):
                pltpu.make_async_remote_copy(
                    src_ref=backs[k][off].at[:, where, :],
                    dst_ref=landing.at[k, me, :, where, :],
                    send_sem=send,
                    recv_sem=recv.at[j],
                    device_id={"slab": partner(me, off, n)},
                    device_id_type=pl.DeviceIdType.MESH,
                ).start()
        return carry

    lax.fori_loop(0, chunks, send_band, 0)
    copies = []
    for k in range(coils):
        for off in range(n if k < ready else 1):
            origin = landing.at[k, partner(me, off, n)]
            copies.append(pltpu.make_async_copy(backs[k][off], origin, local.at[k * n + off]))
        copies.append(pltpu.make_async_copy(sens.at[k], sens_v.at[k], local.at[coils * n + k]))
    for copy in copies:
        copy.start()
    for copy in copies:
        copy.wait()

    def add_band(j, carry):
        arrived = got.at[0 : shares - 1, :, pl.ds(j * rows, rows)]
        pltpu.make_async_copy(arrived, arrived, grad_recv.at[j]).wait()

        def line(i, carry):
            x = j * rows + i
            for p in range(2):
                value = grad[mine, p, x].astype(F32)
                for off in range(1, shares):
                    value += got[lax.rem(mine + off, shares), p, x].astype(F32)
                out[p, x] = value
            return carry

        lax.fori_loop(0, rows, line, 0)
        return carry

    def do_band(j, carry):
        where = pl.ds(pl.multiple_of(j * band, band), band)
        arrived = landing.at[ready:coils, 0 : n - 1, :, where, :]
        pltpu.make_async_copy(arrived, arrived, recv.at[j]).wait()
        if wide:
            for k in range(coils):
                for s in range(n):
                    for p in range(2):
                        wide[0][k, s, p] = landing[k, s, p, where, :].astype(F32)

        def columns_of(k, i):
            pieces = []
            for p in range(2):
                for s in range(n):
                    if wide:
                        pieces.append(wide[0][k, s, p, pl.ds(pl.multiple_of(i * kl, kl), kl), :])
                    else:
                        row = pl.multiple_of((j * rows + i) * kl, kl)
                        pieces.append(landing[k, s, p, pl.ds(row, kl), :])
            return jnp.concatenate(pieces, axis=0).astype(BF16)

        def pair(i, carry):
            total = [[None, None]] * group
            for k in range(coils):
                both = jnp.concatenate([columns_of(k, group * i + h) for h in range(group)], axis=1)
                adj = jnp.dot(table[...], both, preferred_element_type=F32)
                adj = adj.astype(BF16).astype(F32)
                for h in range(group):
                    x = j * rows + group * i + h
                    ar = adj[:length, h * depth : (h + 1) * depth]
                    ai = adj[length:, h * depth : (h + 1) * depth]
                    sr = sens_v[k, 0, x].astype(F32)
                    si = sens_v[k, 1, x].astype(F32)
                    re = sr * ar + si * ai
                    im = sr * ai - si * ar
                    total[h] = [re, im] if k == 0 else [total[h][0] + re, total[h][1] + im]
            for h in range(group):
                x = j * rows + group * i + h
                for p in range(2):
                    for q in range(shares):
                        grad[q, p, x] = total[h][p][q * share : (q + 1) * share].astype(BF16)
            return carry

        lax.fori_loop(0, rows // group, pair, 0)
        lines = pl.ds(j * rows, rows)
        for off in range(1, shares):
            target = lax.rem(mine + off, shares)
            pltpu.make_async_remote_copy(
                src_ref=grad.at[target, :, lines],
                dst_ref=got.at[mine, :, lines],
                send_sem=grad_send,
                recv_sem=grad_recv.at[j],
                device_id={"coil": target},
                device_id_type=pl.DeviceIdType.MESH,
            ).start()

        @pl.when(j >= LAG)
        def settled():
            add_band(j - LAG, 0)

        return carry

    lax.fori_loop(0, chunks, do_band, 0)
    lax.fori_loop(max(chunks - LAG, 0), chunks, add_band, 0)
    gone = landing.at[ready:coils, 0 : n - 1]
    pltpu.make_async_copy(gone, gone, send).wait()
    gone = got.at[0 : shares - 1]
    pltpu.make_async_copy(gone, gone, grad_send).wait()


def finish_call(table, backs, sent, sensitivity, shares, n, kl):
    coils, _, xl, length, depth = sensitivity.shape
    chunks = xl
    rows = xl // chunks
    share = length // shares
    vmem = pl.BlockSpec(memory_space=pltpu.VMEM)
    scratch = [
        pltpu.VMEM((coils, n, 2, xl * kl, depth), BF16),
        pltpu.VMEM(sensitivity.shape, BF16),
        pltpu.VMEM((shares, 2, xl, share, depth), BF16),
        pltpu.VMEM((shares, 2, xl, share, depth), BF16),
        pltpu.SemaphoreType.DMA((chunks,)),
        pltpu.SemaphoreType.DMA,
        pltpu.SemaphoreType.DMA((coils * n + coils,)),
        pltpu.SemaphoreType.DMA((chunks,)),
        pltpu.SemaphoreType.DMA,
    ]
    if kl % 16:
        scratch.append(pltpu.VMEM((coils, n, 2, rows * kl, depth), F32))
    limit = VMEM_LIMIT - 32 * xl * share * depth
    return pl.pallas_call(
        functools.partial(finish_kernel, n, shares, kl, xl, chunks, sent),
        in_specs=[vmem, HBM] + [HBM] * (coils * n),
        out_specs=vmem,
        out_shape=jax.ShapeDtypeStruct((2, xl, share, depth), F32),
        scratch_shapes=scratch,
        compiler_params=params(limit, collective_id=0, has_side_effects=True),
        name="finish",
    )(table, sensitivity, *[piece for back in backs for piece in back])


def haar_rows(first, second):
    even = lax.broadcasted_iota(jnp.int32, first.shape, 0) % 2 == 0
    rows = first.shape[0]

    def along(v):
        after = pltpu.roll(v, rows - 1, 0)
        ahead = pltpu.roll(v, 1, 0)
        return jnp.where(even, v + after, ahead - v) * 0.5

    return along(first + second), along(first - second)


def update_kernel(image, gradient, auxiliary, dual, image_out, aux_out, dual_out):
    rows = image.shape[1]
    for m in range(0, rows, 2):
        coeffs = []
        for p in range(2):
            target = haar_rows(
                auxiliary[p, m] - dual[p, m], auxiliary[p, m + 1] - dual[p, m + 1]
            )
            following = []
            for h in range(2):
                current = image[p, m + h]
                value = current - step_size * (
                    gradient[p, m + h].astype(F32) + penalty * (current - target[h])
                )
                image_out[p, m + h] = value
                following.append(value)
            spread = haar_rows(*following)
            coeffs.append([spread[h] + dual[p, m + h] for h in range(2)])
        for h in range(2):
            re, im = coeffs[0][h], coeffs[1][h]
            magnitude = jnp.sqrt(re * re + im * im)
            factor = jnp.maximum(1.0 - threshold / jnp.maximum(magnitude, threshold), 0.0)
            for p, value in enumerate((re, im)):
                kept = value * factor
                aux_out[p, m + h] = kept
                dual_out[p, m + h] = value - kept


def update_call(image, gradient, auxiliary, dual):
    _, xl, share, depth = auxiliary.shape
    rows = 8 if xl % 8 == 0 else 2
    plain = pl.BlockSpec((2, rows, share, depth), lambda i: (0, i, 0, 0))
    shape = jax.ShapeDtypeStruct(auxiliary.shape, F32)
    return pl.pallas_call(
        update_kernel,
        grid=(xl // rows,),
        in_specs=[plain, plain, plain, plain],
        out_specs=[plain, plain, plain],
        out_shape=[shape, shape, shape],
        compiler_params=params(VMEM_LIMIT - 128 * xl * share * depth),
        name="update",
    )(image, gradient, auxiliary, dual)


def body(image, sensitivity, blocks, samples, offsets, counts, auxiliary, scaled_dual):
    coils, _, xl, length_y, _ = sensitivity.shape
    n = lax.axis_size("slab")
    shares = lax.axis_size("coil")
    kl = length_y // n
    y_fwd = complex_table(length_y, False)
    y_inv = complex_table(length_y, True)
    x_fwd = complex_table(n * xl, False)
    x_inv = complex_table(n * xl, True)

    def swap(parts):
        moved = list(parts)
        for off in turns(n):
            moved[off] = lax.ppermute(parts[off], "slab", [(i, partner(i, off, n)) for i in range(n)])
        return moved

    def parts_of(c):
        if c == 0 and xl % 32 == 0:
            return [(0, xl // 4), (xl // 4, xl // 4), (xl // 2, xl // 2)]
        return [(0, xl)]

    def tile_of(pieces, c):
        return tile_call(x_fwd, x_inv, pieces, parts_of(c), blocks, sorted_samples, offsets, counts, c, n, kl, xl)

    share = length_y // shares
    pieces, tiles, table = [], [], y_fwd
    for c in range(coils):
        moved = []
        for first, size in parts_of(c):
            half = list(forward_call(table, image, sensitivity, c, first, size, n, kl))
            table, half[0] = lax.optimization_barrier((table, half[0]))
            moved += swap(half)
        pieces.append(moved)
    table, samples, source = lax.optimization_barrier((table, samples, image))
    sorted_samples = sort_call(samples)
    current = lax.dynamic_slice_in_dim(source, lax.axis_index("coil") * share, share, 2)
    for c in range(coils):
        if c:
            pieces[c][0], tiles[-1][0] = lax.optimization_barrier((pieces[c][0], tiles[-1][0]))
        tiles.append(list(tile_of(pieces[c], c)))
    early = max(coils - 3, 0)
    backs = list(tiles)
    for c in range(early):
        backs[c] = swap(tiles[c])
    gradient = finish_call(y_inv, backs, coils - early, sensitivity, shares, n, kl)
    return tuple(update_call(current, gradient, auxiliary, scaled_dual))


def solution(mesh):
    return jax.shard_map(
        body,
        mesh=mesh,
        in_specs=(
            P(None, "slab", None, None),
            P("coil", None, "slab", None, None),
            P("slab", None, None, None),
            P("slab", None, None, "coil", None, None),
            P("slab", None),
            P("slab"),
            P(None, "slab", "coil", None),
            P(None, "slab", "coil", None),
        ),
        out_specs=(
            P(None, "slab", "coil", None),
            P(None, "slab", "coil", None),
            P(None, "slab", "coil", None),
        ),
        check_vma=False,
    )
```

```python
import functools
import math

import jax
import jax.numpy as jnp
import numpy as np
from jax import lax
from jax.experimental import pallas as pl
from jax.experimental.pallas import tpu as pltpu
from jax.sharding import PartitionSpec as P

step_size = 0.5
penalty = 1.0
threshold = 0.3
VMEM_LIMIT = 67000000
LAG = 3
F32 = jnp.float32
BF16 = jnp.bfloat16


def complex_table(length, inverse):
    index = np.arange(length, dtype=np.int64)
    angle = (index[:, None] * index[None, :] % length).astype(np.float64) * (2.0 * math.pi / length)
    factor = 1.0 / math.sqrt(length)
    re = np.cos(angle) * factor
    im = -np.sin(angle) * factor
    if inverse:
        whole = np.block([[re, im], [-im, re]])
    else:
        whole = np.block([[re, -im], [im, re]])
    return jnp.asarray(whole.astype(np.float32)).astype(BF16)


HBM = pl.BlockSpec(memory_space=pltpu.HBM)


def params(limit=VMEM_LIMIT, **extra):
    return pltpu.CompilerParams(vmem_limit_bytes=limit, **extra)


def ahead(me, off, n):
    return (me + off) % n


def behind(me, off, n):
    return (me + n - off) % n


def turns(n):
    return [*range(2, n, 2), *range(3, n, 2), 1]


def once(shape):
    return pl.BlockSpec(shape, lambda *i: (0,) * len(shape), pipeline_mode=pl.Buffered(1))


def cost(flops, nbytes):
    return pl.CostEstimate(flops=int(flops), bytes_accessed=int(nbytes), transcendentals=0)


def pitch(rows):
    tiles = -(-rows // 8)
    return 8 * (tiles + 1 - tiles % 2)


def gather_rows(ref, row, parts_n):
    pieces = []
    for p in range(2):
        for s in range(parts_n):
            pieces.append(ref[s, p, row])
    return jnp.concatenate(pieces, axis=0)


def forward_kernel(n, kl, xp, table, image, sens, *refs):
    outs, flat = refs[:n], refs[n]
    rows, length = image.shape[1], image.shape[2]
    me = lax.axis_index("slab")
    coil, step = pl.program_id(0), pl.program_id(1)

    def pair(i, carry):
        columns = []
        for h in range(2):
            x = 2 * i + h
            sr = sens[0, 0, x].astype(F32)
            si = sens[0, 1, x].astype(F32)
            ir = image[0, x]
            ii = image[1, x]
            columns.append(
                jnp.concatenate(
                    [(sr * ir - si * ii).astype(BF16), (sr * ii + si * ir).astype(BF16)], axis=0
                )
            )
        both = jnp.concatenate(columns, axis=1)
        half = jnp.dot(table[...], both, preferred_element_type=F32)
        depth = half.shape[1] // 2
        for h in range(2):
            where = pl.ds(step * rows + 2 * i + h, 2 * length, stride=pitch(xp))
            flat[where, :] = half[:, h * depth : (h + 1) * depth]
        return carry

    lax.fori_loop(0, rows // 2, pair, 0, unroll=2)

    @pl.when(step == pl.num_programs(1) - 1)
    def last():
        for off in range(n):
            d = ahead(me, off, n)
            for p in range(2):

                def settle(k, carry):
                    base = pl.multiple_of(((p * n + d) * kl + 2 * k) * pitch(xp), 8)
                    for h in range(2):
                        outs[off][coil, p, 2 * k + h] = flat[pl.ds(base + h * pitch(xp), xp), :].astype(BF16)
                    return carry

                lax.fori_loop(0, kl // 2, settle, 0, unroll=4)


def forward_call(table, image, sensitivity, batch, first, xp, n, kl):
    _, _, _, length, depth = sensitivity.shape
    rows = 8 if xp % 8 == 0 else xp
    steps, skip = xp // rows, first // rows
    shape = (len(batch), 2, kl, xp, depth)
    return pl.pallas_call(
        functools.partial(forward_kernel, n, kl, xp),
        grid=(len(batch), steps),
        in_specs=[
            once(table.shape),
            pl.BlockSpec((2, rows, length, depth), lambda c, i: (0, skip + i, 0, 0)),
            pl.BlockSpec((1, 2, rows, length, depth), lambda c, i: (batch[0] + c, 0, skip + i, 0, 0)),
        ],
        out_specs=[once(shape)] * n,
        out_shape=[jax.ShapeDtypeStruct(shape, BF16)] * n,
        scratch_shapes=[pltpu.VMEM(((2 * length + 1) * pitch(xp), depth), F32)],
        compiler_params=params(),
        cost_estimate=cost(8 * len(batch) * length * length * xp * depth, 12 * len(batch) * xp * length * depth),
        name="forward",
    )(table, image, sensitivity)


def sort_kernel(samples, out, flat):
    parts = out.shape[0]
    psize = out.shape[2]
    depth = samples.shape[2]
    for g in range(samples.shape[0]):
        flat[...] = samples[g].astype(F32)
        for c in range(parts):
            for p in range(2):
                rows = flat[pl.ds(2 * c + p, psize, stride=2 * parts), :]
                out[c, g, :, p * depth : (p + 1) * depth] = rows.astype(BF16)


def sort_call(samples):
    _, slots, psize, coils, parts, depth = samples.shape
    group = 4 if slots % 4 == 0 else 1
    lines = psize * coils * parts
    return pl.pallas_call(
        sort_kernel,
        grid=(slots // group,),
        in_specs=[pl.BlockSpec((group, lines, depth), lambda i: (i, 0, 0))],
        out_specs=pl.BlockSpec((coils, group, psize, parts * depth), lambda i: (0, i, 0, 0)),
        out_shape=jax.ShapeDtypeStruct((coils, slots, psize, parts * depth), BF16),
        scratch_shapes=[pltpu.VMEM((lines, depth), F32)],
        compiler_params=params(),
        cost_estimate=cost(samples.size, 4 * samples.size),
        name="sort",
    )(samples.reshape(slots, lines, depth))


def tile_kernel(n, kl, xl, win, parts, coil, place, offsets, counts, fwd, inv, blocks, sorted_samples, *refs):
    count = n * len(parts)
    pieces, outs, refs = refs[:count], refs[count : count + n], refs[count + n :]
    total, kspace, weights, piece, samples, leaving, sem, piece_sem, *wide = refs
    me = lax.axis_index("slab")
    copies = []
    for off in range(n):
        for h, (start, size) in enumerate(parts):
            target = piece.at[behind(me, off, n), :, :, pl.ds(start, size)]
            copies.append(pltpu.make_async_copy(pieces[h * n + off].at[place], target, piece_sem.at[h * n + off]))
    for copy in copies:
        copy.start()
    for copy in copies:
        copy.wait()
    fetches = [
        pltpu.make_async_copy(blocks.at[0], weights, sem.at[0]),
        pltpu.make_async_copy(sorted_samples.at[coil], samples, sem.at[1]),
    ]
    for fetch in fetches:
        fetch.start()
    length = n * xl
    depth = piece.shape[-1]
    if wide:
        source = wide[0]
        for p in range(2):
            for s in range(n):
                source[s, p] = piece[s, p].astype(F32)
    else:
        source = piece

    def to_kspace(i, carry):
        columns = []
        for h in range(2):
            columns.append(gather_rows(source, 2 * i + h, n).astype(BF16))
        spec = jnp.dot(fwd[...], jnp.concatenate(columns, axis=1), preferred_element_type=F32)
        for h in range(2):
            for p in range(2):
                total[p, pl.ds(2 * i + h, length, stride=pitch(kl)), :] = spec[
                    p * length : (p + 1) * length, h * depth : (h + 1) * depth
                ]
        return carry

    lax.fori_loop(0, kl // 2, to_kspace, 0, unroll=2)

    def settle(i, carry):
        rows = pl.ds(pl.multiple_of(i * pitch(kl), 8), kl)
        target = pl.ds(pl.multiple_of(i * kl, kl), kl)
        for p in range(2):
            kspace[target, p * depth : (p + 1) * depth] = total[p, rows, :].astype(kspace.dtype)
            total[p, rows, :] = jnp.zeros((kl, depth), F32)
        return carry

    lax.fori_loop(0, length, settle, 0, unroll=8)
    for fetch in fetches:
        fetch.wait()
    cells = win * kl
    chunk = min(cells, 512)

    def misfit_of(slot):
        start = pl.multiple_of(offsets[0, slot] * kl, kl)
        window = kspace[pl.ds(start, cells), :].astype(BF16)
        predicted = jnp.dot(weights[slot], window, preferred_element_type=F32)
        return (predicted - samples[slot].astype(F32)).astype(BF16)

    def group(slot, misfit):
        following = misfit_of(jnp.minimum(slot + 1, weights.shape[0] - 1))
        first = offsets[0, slot]
        for c in range(0, cells, chunk):
            update = lax.dot_general(
                weights[slot, :, c : c + chunk],
                misfit,
                (((0,), (0,)), ((), ())),
                preferred_element_type=F32,
            )
            for k in range(chunk // kl):
                rows = pl.ds(pl.multiple_of((first + c // kl + k) * pitch(kl), 8), kl)
                for p in range(2):
                    total[p, rows, :] += update[k * kl : (k + 1) * kl, p * depth : (p + 1) * depth]
        return following

    lax.fori_loop(0, counts[0], group, misfit_of(0))

    def to_rows(i, carry):
        columns = []
        for h in range(2):
            columns.append(
                jnp.concatenate(
                    [total[p, pl.ds(2 * i + h, length, stride=pitch(kl)), :].astype(BF16) for p in range(2)], axis=0
                )
            )
        back = jnp.dot(inv[...], jnp.concatenate(columns, axis=1), preferred_element_type=F32)
        for h in range(2):
            for p in range(2):
                total[p, pl.ds(2 * i + h, length, stride=pitch(kl)), :] = back[
                    p * length : (p + 1) * length, h * depth : (h + 1) * depth
                ]
        return carry

    lax.fori_loop(0, kl // 2, to_rows, 0, unroll=2)
    for off in range(n):
        d = ahead(me, off, n)
        for p in range(2):

            def leave(k, carry):
                base = pl.multiple_of((d * xl + 2 * k) * pitch(kl), 8)
                rows = [total[p, pl.ds(base + h * pitch(kl), kl), :] for h in range(2)]
                target = pl.ds(pl.multiple_of(2 * k * kl, 2 * kl), 2 * kl)
                leaving[off, p, target, :] = jnp.concatenate(rows, axis=0).astype(BF16)
                return carry

            lax.fori_loop(0, xl // 2, leave, 0, unroll=4)
        pltpu.make_async_copy(leaving.at[off], outs[off], piece_sem.at[off]).start()
    for off in range(n):
        pltpu.make_async_copy(leaving.at[off], outs[off], piece_sem.at[off]).wait()


def tile_call(fwd, inv, pieces, parts, place, blocks, samples, offsets, counts, coil, n, kl, xl):
    depth = pieces[0].shape[-1]
    _, slots, psize, cells = blocks.shape
    length = n * xl
    narrow = kl % 16 == 0 and xl % 16 == 0
    scratch = [
        pltpu.VMEM((2, (length + 1) * pitch(kl), depth), F32),
        pltpu.VMEM((length * kl, 2 * depth), BF16 if narrow else F32),
        pltpu.VMEM(blocks.shape[1:], BF16),
        pltpu.VMEM((n, 2, kl, xl, depth), BF16),
        pltpu.VMEM((slots, psize, 2 * depth), BF16),
        pltpu.VMEM((n, 2, xl * kl, depth), BF16),
        pltpu.SemaphoreType.DMA((2,)),
        pltpu.SemaphoreType.DMA((len(pieces),)),
    ]
    if not narrow:
        scratch.append(pltpu.VMEM((n, 2, kl, xl, depth), F32))
    smem = pl.BlockSpec(memory_space=pltpu.SMEM)
    return pl.pallas_call(
        functools.partial(tile_kernel, n, kl, xl, cells // kl, parts, coil, place),
        grid=(1,),
        in_specs=[smem, smem, once(fwd.shape), once(inv.shape), HBM, HBM] + [HBM] * len(pieces),
        out_specs=[HBM] * n,
        out_shape=[jax.ShapeDtypeStruct((2, xl * kl, depth), BF16)] * n,
        scratch_shapes=scratch,
        compiler_params=params(),
        cost_estimate=cost(
            16 * length * length * kl * depth + 8 * slots * psize * cells * depth,
            8 * length * kl * depth + 2 * blocks.size,
        ),
        name="tile",
    )(offsets, counts, fwd, inv, blocks, samples, *pieces)


def finish_kernel(n, shares, kl, xl, chunks, sent, table_ref, sens, *refs):
    coils = sens.shape[0]
    backs, refs = [refs[k * n : (k + 1) * n] for k in range(coils)], refs[coils * n :]
    out, table, landing, sens_v, grad, got, recv, send, local, grad_recv, grad_send, *wide = refs
    ready = coils - sent
    length = n * kl
    depth = landing.shape[-1]
    share = length // shares
    rows = xl // chunks
    band = rows * kl
    group = min(rows, 2)
    me = lax.axis_index("slab")
    mine = lax.axis_index("coil")

    barrier = pltpu.get_barrier_semaphore()

    def greet(off, carry):
        pl.semaphore_signal(
            barrier, inc=1, device_id={"slab": lax.rem(me + off, n)}, device_id_type=pl.DeviceIdType.MESH
        )
        return carry

    lax.fori_loop(1, n, greet, 0)
    for off in range(1, shares):
        pl.semaphore_signal(
            barrier, inc=1, device_id={"coil": lax.rem(mine + off, shares)}, device_id_type=pl.DeviceIdType.MESH
        )
    pl.semaphore_wait(barrier, n - 1 + shares - 1)

    def send_band(j, carry):
        where = pl.ds(pl.multiple_of(j * band, band), band)
        for k in range(ready, coils):
            for off in turns(n):
                pltpu.make_async_remote_copy(
                    src_ref=backs[k][off].at[:, where, :],
                    dst_ref=landing.at[k, me, :, where, :],
                    send_sem=send,
                    recv_sem=recv.at[j],
                    device_id={"slab": ahead(me, off, n)},
                    device_id_type=pl.DeviceIdType.MESH,
                ).start()
        return carry

    lax.fori_loop(0, chunks, send_band, 0)
    copies = [pltpu.make_async_copy(table_ref, table, local.at[coils * n + coils])]
    for k in range(coils):
        for off in range(n if k < ready else 1):
            origin = landing.at[k, behind(me, off, n)]
            copies.append(pltpu.make_async_copy(backs[k][off], origin, local.at[k * n + off]))
        copies.append(pltpu.make_async_copy(sens.at[k], sens_v.at[k], local.at[coils * n + k]))
    for copy in copies:
        copy.start()
    for copy in copies:
        copy.wait()

    def add_band(j, carry):
        arrived = got.at[0 : shares - 1, :, pl.ds(j * rows, rows)]
        pltpu.make_async_copy(arrived, arrived, grad_recv.at[j]).wait()

        def line(i, carry):
            x = j * rows + i
            for p in range(2):
                value = grad[mine, p, x].astype(F32)
                for off in range(1, shares):
                    value += got[lax.rem(mine + off, shares), p, x].astype(F32)
                out[p, x] = value
            return carry

        lax.fori_loop(0, rows, line, 0)
        return carry

    def do_band(j, carry):
        where = pl.ds(pl.multiple_of(j * band, band), band)
        arrived = landing.at[ready:coils, 0 : n - 1, :, where, :]
        pltpu.make_async_copy(arrived, arrived, recv.at[j]).wait()
        if wide:
            for k in range(coils):
                for s in range(n):
                    for p in range(2):
                        wide[0][k, s, p] = landing[k, s, p, where, :].astype(F32)

        def columns_of(k, i):
            pieces = []
            for p in range(2):
                for s in range(n):
                    if wide:
                        pieces.append(wide[0][k, s, p, pl.ds(pl.multiple_of(i * kl, kl), kl), :])
                    else:
                        row = pl.multiple_of((j * rows + i) * kl, kl)
                        pieces.append(landing[k, s, p, pl.ds(row, kl), :])
            return jnp.concatenate(pieces, axis=0).astype(BF16)

        def pair(i, carry):
            total = [[None, None]] * group
            for k in range(coils):
                both = jnp.concatenate([columns_of(k, group * i + h) for h in range(group)], axis=1)
                adj = jnp.dot(table[...], both, preferred_element_type=F32)
                adj = adj.astype(BF16).astype(F32)
                for h in range(group):
                    x = j * rows + group * i + h
                    ar = adj[:length, h * depth : (h + 1) * depth]
                    ai = adj[length:, h * depth : (h + 1) * depth]
                    sr = sens_v[k, 0, x].astype(F32)
                    si = sens_v[k, 1, x].astype(F32)
                    re = sr * ar + si * ai
                    im = sr * ai - si * ar
                    total[h] = [re, im] if k == 0 else [total[h][0] + re, total[h][1] + im]
            for h in range(group):
                x = j * rows + group * i + h
                for p in range(2):
                    for q in range(shares):
                        grad[q, p, x] = total[h][p][q * share : (q + 1) * share].astype(BF16)
            return carry

        lax.fori_loop(0, rows // group, pair, 0)
        lines = pl.ds(j * rows, rows)
        for off in range(1, shares):
            target = lax.rem(mine + off, shares)
            pltpu.make_async_remote_copy(
                src_ref=grad.at[target, :, lines],
                dst_ref=got.at[mine, :, lines],
                send_sem=grad_send,
                recv_sem=grad_recv.at[j],
                device_id={"coil": target},
                device_id_type=pl.DeviceIdType.MESH,
            ).start()

        @pl.when(j >= LAG)
        def settled():
            add_band(j - LAG, 0)

        return carry

    lax.fori_loop(0, chunks, do_band, 0)
    lax.fori_loop(max(chunks - LAG, 0), chunks, add_band, 0)
    gone = landing.at[ready:coils, 0 : n - 1]
    pltpu.make_async_copy(gone, gone, send).wait()
    gone = got.at[0 : shares - 1]
    pltpu.make_async_copy(gone, gone, grad_send).wait()


def finish_call(table, backs, sent, sensitivity, shares, n, kl):
    coils, _, xl, length, depth = sensitivity.shape
    chunks = xl
    rows = xl // chunks
    share = length // shares
    vmem = pl.BlockSpec(memory_space=pltpu.VMEM)
    scratch = [
        pltpu.VMEM(table.shape, BF16),
        pltpu.VMEM((coils, n, 2, xl * kl, depth), BF16),
        pltpu.VMEM(sensitivity.shape, BF16),
        pltpu.VMEM((shares, 2, xl, share, depth), BF16),
        pltpu.VMEM((shares, 2, xl, share, depth), BF16),
        pltpu.SemaphoreType.DMA((chunks,)),
        pltpu.SemaphoreType.DMA,
        pltpu.SemaphoreType.DMA((coils * n + coils + 1,)),
        pltpu.SemaphoreType.DMA((chunks,)),
        pltpu.SemaphoreType.DMA,
    ]
    if kl % 16:
        scratch.append(pltpu.VMEM((coils, n, 2, rows * kl, depth), F32))
    limit = VMEM_LIMIT - 32 * xl * share * depth
    return pl.pallas_call(
        functools.partial(finish_kernel, n, shares, kl, xl, chunks, sent),
        in_specs=[HBM] * (2 + coils * n),
        out_specs=vmem,
        out_shape=pltpu.VMEM((2, xl, share, depth), F32),
        scratch_shapes=scratch,
        compiler_params=params(limit, collective_id=0, has_side_effects=True),
        name="finish",
    )(table, sensitivity, *[piece for back in backs for piece in back])


def haar_rows(first, second):
    even = lax.broadcasted_iota(jnp.int32, first.shape, 0) % 2 == 0
    rows = first.shape[0]

    def along(v):
        after = pltpu.roll(v, rows - 1, 0)
        ahead = pltpu.roll(v, 1, 0)
        return jnp.where(even, v + after, ahead - v) * 0.5

    return along(first + second), along(first - second)


def update_kernel(image, gradient, auxiliary, dual, image_out, aux_out, dual_out):
    rows = image.shape[1]
    for m in range(0, rows, 2):
        coeffs = []
        for p in range(2):
            target = haar_rows(
                auxiliary[p, m] - dual[p, m], auxiliary[p, m + 1] - dual[p, m + 1]
            )
            following = []
            for h in range(2):
                current = image[p, m + h]
                value = current - step_size * (
                    gradient[p, m + h].astype(F32) + penalty * (current - target[h])
                )
                image_out[p, m + h] = value
                following.append(value)
            spread = haar_rows(*following)
            coeffs.append([spread[h] + dual[p, m + h] for h in range(2)])
        for h in range(2):
            re, im = coeffs[0][h], coeffs[1][h]
            magnitude = jnp.sqrt(re * re + im * im)
            factor = jnp.maximum(1.0 - threshold / jnp.maximum(magnitude, threshold), 0.0)
            for p, value in enumerate((re, im)):
                kept = value * factor
                aux_out[p, m + h] = kept
                dual_out[p, m + h] = value - kept


def update_call(image, gradient, auxiliary, dual):
    _, xl, share, depth = auxiliary.shape
    rows = 8 if xl % 8 == 0 else 2
    plain = pl.BlockSpec((2, rows, share, depth), lambda i: (0, i, 0, 0))
    shape = jax.ShapeDtypeStruct(auxiliary.shape, F32)
    return pl.pallas_call(
        update_kernel,
        grid=(xl // rows,),
        in_specs=[plain, plain, plain, plain],
        out_specs=[plain, plain, plain],
        out_shape=[shape, shape, shape],
        compiler_params=params(VMEM_LIMIT - 128 * xl * share * depth),
        name="update",
    )(image, gradient, auxiliary, dual)


def body(image, sensitivity, blocks, samples, offsets, counts, auxiliary, scaled_dual):
    coils, _, xl, length_y, _ = sensitivity.shape
    n = lax.axis_size("slab")
    shares = lax.axis_size("coil")
    kl = length_y // n
    y_fwd = complex_table(length_y, False)
    y_inv = complex_table(length_y, True)
    x_fwd = complex_table(n * xl, False)
    x_inv = complex_table(n * xl, True)

    def swap(parts):
        moved = list(parts)
        for off in turns(n):
            moved[off] = lax.ppermute(parts[off], "slab", [(i, ahead(i, off, n)) for i in range(n)])
        return moved

    batches = [[c] for c in range(min(coils, 2))] + [
        list(range(c, min(c + 2, coils))) for c in range(2, coils, 2)
    ]

    def parts_of(c):
        if c == 0 and xl % 32 == 0:
            return [(0, xl // 4), (xl // 4, xl // 4), (xl // 2, xl // 2)]
        return [(0, xl)]

    def tile_of(pieces, place, c):
        return tile_call(
            x_fwd, x_inv, pieces, parts_of(c), place, blocks, sorted_samples, offsets, counts, c, n, kl, xl
        )

    share = length_y // shares
    pieces, tiles, table = [], [], y_fwd
    for batch in batches:
        c = batch[0]
        moved = []
        for first, size in parts_of(c):
            half = list(forward_call(table, image, sensitivity, batch, first, size, n, kl))
            table, half[0] = lax.optimization_barrier((table, half[0]))
            moved += swap(half)
        pieces += [(moved, place) for place in range(len(batch))]
    table, samples, source = lax.optimization_barrier((table, samples, image))
    sorted_samples = sort_call(samples)
    current = lax.dynamic_slice_in_dim(source, lax.axis_index("coil") * share, share, 2)
    for c in range(coils):
        arrived, place = pieces[c]
        if c:
            arrived = list(arrived)
            arrived[0], tiles[-1][0] = lax.optimization_barrier((arrived[0], tiles[-1][0]))
        tiles.append(list(tile_of(arrived, place, c)))
    early = max(coils - 3, 0)
    backs = list(tiles)
    for c in range(early):
        backs[c] = swap(tiles[c])
    gradient = finish_call(y_inv, backs, coils - early, sensitivity, shares, n, kl)
    return tuple(update_call(current, gradient, auxiliary, scaled_dual))


def solution(mesh):
    return jax.shard_map(
        body,
        mesh=mesh,
        in_specs=(
            P(None, "slab", None, None),
            P("coil", None, "slab", None, None),
            P("slab", None, None, None),
            P("slab", None, None, "coil", None, None),
            P("slab", None),
            P("slab"),
            P(None, "slab", "coil", None),
            P(None, "slab", "coil", None),
        ),
        out_specs=(
            P(None, "slab", "coil", None),
            P(None, "slab", "coil", None),
            P(None, "slab", "coil", None),
        ),
        check_vma=False,
    )
```

```python
import functools
import math

import jax
import jax.numpy as jnp
import numpy as np
from jax import lax
from jax.experimental import pallas as pl
from jax.experimental.pallas import tpu as pltpu
from jax.sharding import PartitionSpec as P

step_size = 0.5
penalty = 1.0
threshold = 0.3
VMEM_LIMIT = 67000000
LAG = 3
F32 = jnp.float32
BF16 = jnp.bfloat16


def complex_table(length, inverse):
    index = np.arange(length, dtype=np.int64)
    angle = (index[:, None] * index[None, :] % length).astype(np.float64) * (2.0 * math.pi / length)
    factor = 1.0 / math.sqrt(length)
    re = np.cos(angle) * factor
    im = -np.sin(angle) * factor
    if inverse:
        whole = np.block([[re, im], [-im, re]])
    else:
        whole = np.block([[re, -im], [im, re]])
    return jnp.asarray(whole.astype(np.float32)).astype(BF16)


HBM = pl.BlockSpec(memory_space=pltpu.HBM)


def params(limit=VMEM_LIMIT, **extra):
    return pltpu.CompilerParams(vmem_limit_bytes=limit, **extra)


def ahead(me, off, n):
    return (me + off) % n


def behind(me, off, n):
    return (me + n - off) % n


def turns(n):
    return [*range(2, n, 2), *range(3, n, 2), 1]


def once(shape):
    return pl.BlockSpec(shape, lambda *i: (0,) * len(shape), pipeline_mode=pl.Buffered(1))


def cost(flops, nbytes):
    return pl.CostEstimate(flops=int(flops), bytes_accessed=int(nbytes), transcendentals=0)


def pitch(rows):
    tiles = -(-rows // 8)
    return 8 * (tiles + 1 - tiles % 2)


def gather_rows(ref, row, parts_n):
    pieces = []
    for p in range(2):
        for s in range(parts_n):
            pieces.append(ref[s, p, row])
    return jnp.concatenate(pieces, axis=0)


def forward_kernel(n, kl, xp, table, image, sens, *refs):
    outs, flat = refs[:n], refs[n]
    rows, length = image.shape[1], image.shape[2]
    me = lax.axis_index("slab")
    coil, step = pl.program_id(0), pl.program_id(1)

    def pair(i, carry):
        columns = []
        for h in range(2):
            x = 2 * i + h
            sr = sens[0, 0, x].astype(F32)
            si = sens[0, 1, x].astype(F32)
            ir = image[0, x]
            ii = image[1, x]
            columns.append(
                jnp.concatenate(
                    [(sr * ir - si * ii).astype(BF16), (sr * ii + si * ir).astype(BF16)], axis=0
                )
            )
        both = jnp.concatenate(columns, axis=1)
        half = jnp.dot(table[...], both, preferred_element_type=F32)
        depth = half.shape[1] // 2
        for h in range(2):
            where = pl.ds(step * rows + 2 * i + h, 2 * length, stride=pitch(xp))
            flat[where, :] = half[:, h * depth : (h + 1) * depth]
        return carry

    lax.fori_loop(0, rows // 2, pair, 0, unroll=2)

    @pl.when(step == pl.num_programs(1) - 1)
    def last():
        for off in range(n):
            d = ahead(me, off, n)
            for p in range(2):

                def settle(k, carry):
                    base = pl.multiple_of(((p * n + d) * kl + 2 * k) * pitch(xp), 8)
                    for h in range(2):
                        outs[off][coil, p, 2 * k + h] = flat[pl.ds(base + h * pitch(xp), xp), :].astype(BF16)
                    return carry

                lax.fori_loop(0, kl // 2, settle, 0, unroll=4)


def forward_call(table, image, sensitivity, batch, first, xp, n, kl):
    _, _, _, length, depth = sensitivity.shape
    rows = 8 if xp % 8 == 0 else xp
    steps, skip = xp // rows, first // rows
    shape = (len(batch), 2, kl, xp, depth)
    return pl.pallas_call(
        functools.partial(forward_kernel, n, kl, xp),
        grid=(len(batch), steps),
        in_specs=[
            once(table.shape),
            pl.BlockSpec((2, rows, length, depth), lambda c, i: (0, skip + i, 0, 0)),
            pl.BlockSpec((1, 2, rows, length, depth), lambda c, i: (batch[0] + c, 0, skip + i, 0, 0)),
        ],
        out_specs=[once(shape)] * n,
        out_shape=[jax.ShapeDtypeStruct(shape, BF16)] * n,
        scratch_shapes=[pltpu.VMEM(((2 * length + 1) * pitch(xp), depth), F32)],
        compiler_params=params(),
        cost_estimate=cost(8 * len(batch) * length * length * xp * depth, 12 * len(batch) * xp * length * depth),
        name="forward",
    )(table, image, sensitivity)


def sort_kernel(samples, out, flat):
    parts = out.shape[0]
    psize = out.shape[2]
    depth = samples.shape[2]
    for g in range(samples.shape[0]):
        flat[...] = samples[g].astype(F32)
        for c in range(parts):
            for p in range(2):
                rows = flat[pl.ds(2 * c + p, psize, stride=2 * parts), :]
                out[c, g, :, p * depth : (p + 1) * depth] = rows.astype(BF16)


def sort_call(samples):
    _, slots, psize, coils, parts, depth = samples.shape
    group = 4 if slots % 4 == 0 else 1
    lines = psize * coils * parts
    return pl.pallas_call(
        sort_kernel,
        grid=(slots // group,),
        in_specs=[pl.BlockSpec((group, lines, depth), lambda i: (i, 0, 0))],
        out_specs=pl.BlockSpec((coils, group, psize, parts * depth), lambda i: (0, i, 0, 0)),
        out_shape=jax.ShapeDtypeStruct((coils, slots, psize, parts * depth), BF16),
        scratch_shapes=[pltpu.VMEM((lines, depth), F32)],
        compiler_params=params(),
        cost_estimate=cost(samples.size, 4 * samples.size),
        name="sort",
    )(samples.reshape(slots, lines, depth))


def tile_kernel(n, kl, xl, win, parts, coil, place, offsets, counts, fwd, inv, blocks, sorted_samples, *refs):
    count = n * len(parts)
    pieces, outs, refs = refs[:count], refs[count : count + n], refs[count + n :]
    total, kspace, weights, piece, samples, leaving, sem, piece_sem, *wide = refs
    me = lax.axis_index("slab")
    copies = []
    for off in range(n):
        for h, (start, size) in enumerate(parts):
            target = piece.at[behind(me, off, n), :, :, pl.ds(start, size)]
            copies.append(pltpu.make_async_copy(pieces[h * n + off].at[place], target, piece_sem.at[h * n + off]))
    for copy in copies:
        copy.start()
    for copy in copies:
        copy.wait()
    fetches = [
        pltpu.make_async_copy(blocks.at[0], weights, sem.at[0]),
        pltpu.make_async_copy(sorted_samples.at[coil], samples, sem.at[1]),
    ]
    for fetch in fetches:
        fetch.start()
    length = n * xl
    depth = piece.shape[-1]
    if wide:
        source = wide[0]
        for p in range(2):
            for s in range(n):
                source[s, p] = piece[s, p].astype(F32)
    else:
        source = piece

    def to_kspace(i, carry):
        columns = []
        for h in range(2):
            columns.append(gather_rows(source, 2 * i + h, n).astype(BF16))
        spec = jnp.dot(fwd[...], jnp.concatenate(columns, axis=1), preferred_element_type=F32)
        for h in range(2):
            for p in range(2):
                total[p, pl.ds(2 * i + h, length, stride=pitch(kl)), :] = spec[
                    p * length : (p + 1) * length, h * depth : (h + 1) * depth
                ]
        return carry

    lax.fori_loop(0, kl // 2, to_kspace, 0, unroll=2)

    def settle(i, carry):
        rows = pl.ds(pl.multiple_of(i * pitch(kl), 8), kl)
        target = pl.ds(pl.multiple_of(i * kl, kl), kl)
        for p in range(2):
            kspace[target, p * depth : (p + 1) * depth] = total[p, rows, :].astype(kspace.dtype)
            total[p, rows, :] = jnp.zeros((kl, depth), F32)
        return carry

    lax.fori_loop(0, length, settle, 0, unroll=8)
    for fetch in fetches:
        fetch.wait()
    cells = win * kl
    chunk = min(cells, 512)

    def misfit_of(slot):
        start = pl.multiple_of(offsets[0, slot] * kl, kl)
        window = kspace[pl.ds(start, cells), :].astype(BF16)
        predicted = jnp.dot(weights[slot], window, preferred_element_type=F32)
        return (predicted - samples[slot].astype(F32)).astype(BF16)

    def group(slot, misfit):
        following = misfit_of(jnp.minimum(slot + 1, weights.shape[0] - 1))
        first = offsets[0, slot]
        for c in range(0, cells, chunk):
            update = lax.dot_general(
                weights[slot, :, c : c + chunk],
                misfit,
                (((0,), (0,)), ((), ())),
                preferred_element_type=F32,
            )
            for k in range(chunk // kl):
                rows = pl.ds(pl.multiple_of((first + c // kl + k) * pitch(kl), 8), kl)
                for p in range(2):
                    total[p, rows, :] += update[k * kl : (k + 1) * kl, p * depth : (p + 1) * depth]
        return following

    lax.fori_loop(0, counts[0], group, misfit_of(0))

    def to_rows(i, carry):
        columns = []
        for h in range(2):
            columns.append(
                jnp.concatenate(
                    [total[p, pl.ds(2 * i + h, length, stride=pitch(kl)), :].astype(BF16) for p in range(2)], axis=0
                )
            )
        back = jnp.dot(inv[...], jnp.concatenate(columns, axis=1), preferred_element_type=F32)
        for h in range(2):
            for p in range(2):
                total[p, pl.ds(2 * i + h, length, stride=pitch(kl)), :] = back[
                    p * length : (p + 1) * length, h * depth : (h + 1) * depth
                ]
        return carry

    lax.fori_loop(0, kl // 2, to_rows, 0, unroll=2)
    for off in range(n):
        d = ahead(me, off, n)
        for p in range(2):

            def leave(k, carry):
                base = pl.multiple_of((d * xl + 2 * k) * pitch(kl), 8)
                rows = [total[p, pl.ds(base + h * pitch(kl), kl), :] for h in range(2)]
                target = pl.ds(pl.multiple_of(2 * k * kl, 2 * kl), 2 * kl)
                leaving[off, p, target, :] = jnp.concatenate(rows, axis=0).astype(BF16)
                return carry

            lax.fori_loop(0, xl // 2, leave, 0, unroll=4)
        pltpu.make_async_copy(leaving.at[off], outs[off], piece_sem.at[off]).start()
    for off in range(n):
        pltpu.make_async_copy(leaving.at[off], outs[off], piece_sem.at[off]).wait()


def tile_call(fwd, inv, pieces, parts, place, blocks, samples, offsets, counts, coil, n, kl, xl):
    depth = pieces[0].shape[-1]
    _, slots, psize, cells = blocks.shape
    length = n * xl
    narrow = kl % 16 == 0 and xl % 16 == 0
    scratch = [
        pltpu.VMEM((2, (length + 1) * pitch(kl), depth), F32),
        pltpu.VMEM((length * kl, 2 * depth), BF16 if narrow else F32),
        pltpu.VMEM(blocks.shape[1:], BF16),
        pltpu.VMEM((n, 2, kl, xl, depth), BF16),
        pltpu.VMEM((slots, psize, 2 * depth), BF16),
        pltpu.VMEM((n, 2, xl * kl, depth), BF16),
        pltpu.SemaphoreType.DMA((2,)),
        pltpu.SemaphoreType.DMA((len(pieces),)),
    ]
    if not narrow:
        scratch.append(pltpu.VMEM((n, 2, kl, xl, depth), F32))
    smem = pl.BlockSpec(memory_space=pltpu.SMEM)
    return pl.pallas_call(
        functools.partial(tile_kernel, n, kl, xl, cells // kl, parts, coil, place),
        grid=(1,),
        in_specs=[smem, smem, once(fwd.shape), once(inv.shape), HBM, HBM] + [HBM] * len(pieces),
        out_specs=[HBM] * n,
        out_shape=[jax.ShapeDtypeStruct((2, xl * kl, depth), BF16)] * n,
        scratch_shapes=scratch,
        compiler_params=params(),
        cost_estimate=cost(
            16 * length * length * kl * depth + 8 * slots * psize * cells * depth,
            8 * length * kl * depth + 2 * blocks.size,
        ),
        name="tile",
    )(offsets, counts, fwd, inv, blocks, samples, *pieces)


def finish_kernel(n, shares, kl, xl, chunks, sent, table_ref, sens, *refs):
    coils = sens.shape[0]
    backs, refs = [refs[k * n : (k + 1) * n] for k in range(coils)], refs[coils * n :]
    out, table, landing, sens_v, grad, got, recv, send, local, grad_recv, grad_send, *wide = refs
    ready = coils - sent
    length = n * kl
    depth = landing.shape[-1]
    share = length // shares
    rows = xl // chunks
    band = rows * kl
    group = min(rows, 2)
    me = lax.axis_index("slab")
    mine = lax.axis_index("coil")

    barrier = pltpu.get_barrier_semaphore()

    def greet(off, carry):
        pl.semaphore_signal(
            barrier, inc=1, device_id={"slab": lax.rem(me + off, n)}, device_id_type=pl.DeviceIdType.MESH
        )
        return carry

    lax.fori_loop(1, n, greet, 0)
    for off in range(1, shares):
        pl.semaphore_signal(
            barrier, inc=1, device_id={"coil": lax.rem(mine + off, shares)}, device_id_type=pl.DeviceIdType.MESH
        )
    pl.semaphore_wait(barrier, n - 1 + shares - 1)

    def send_band(j, carry):
        where = pl.ds(pl.multiple_of(j * band, band), band)
        for k in range(ready, coils):
            for off in turns(n):
                pltpu.make_async_remote_copy(
                    src_ref=backs[k][off].at[:, where, :],
                    dst_ref=landing.at[k, me, :, where, :],
                    send_sem=send,
                    recv_sem=recv.at[j],
                    device_id={"slab": ahead(me, off, n)},
                    device_id_type=pl.DeviceIdType.MESH,
                ).start()
        return carry

    lax.fori_loop(0, chunks, send_band, 0)
    copies = [pltpu.make_async_copy(table_ref, table, local.at[coils * n + coils])]
    for k in range(coils):
        for off in range(n if k < ready else 1):
            origin = landing.at[k, behind(me, off, n)]
            copies.append(pltpu.make_async_copy(backs[k][off], origin, local.at[k * n + off]))
        copies.append(pltpu.make_async_copy(sens.at[k], sens_v.at[k], local.at[coils * n + k]))
    for copy in copies:
        copy.start()
    for copy in copies:
        copy.wait()

    def add_band(j, carry):
        arrived = got.at[0 : shares - 1, :, pl.ds(j * rows, rows)]
        pltpu.make_async_copy(arrived, arrived, grad_recv.at[j]).wait()

        def line(i, carry):
            x = j * rows + i
            for p in range(2):
                value = grad[mine, p, x].astype(F32)
                for off in range(1, shares):
                    value += got[lax.rem(mine + off, shares), p, x].astype(F32)
                out[p, x] = value
            return carry

        lax.fori_loop(0, rows, line, 0)
        return carry

    def do_band(j, carry):
        where = pl.ds(pl.multiple_of(j * band, band), band)
        arrived = landing.at[ready:coils, 0 : n - 1, :, where, :]
        pltpu.make_async_copy(arrived, arrived, recv.at[j]).wait()
        if wide:
            for k in range(coils):
                for s in range(n):
                    for p in range(2):
                        wide[0][k, s, p] = landing[k, s, p, where, :].astype(F32)

        def columns_of(k, i):
            pieces = []
            for p in range(2):
                for s in range(n):
                    if wide:
                        pieces.append(wide[0][k, s, p, pl.ds(pl.multiple_of(i * kl, kl), kl), :])
                    else:
                        row = pl.multiple_of((j * rows + i) * kl, kl)
                        pieces.append(landing[k, s, p, pl.ds(row, kl), :])
            return jnp.concatenate(pieces, axis=0).astype(BF16)

        def pair(i, carry):
            total = [[None, None]] * group
            for k in range(coils):
                both = jnp.concatenate([columns_of(k, group * i + h) for h in range(group)], axis=1)
                adj = jnp.dot(table[...], both, preferred_element_type=F32)
                adj = adj.astype(BF16).astype(F32)
                for h in range(group):
                    x = j * rows + group * i + h
                    ar = adj[:length, h * depth : (h + 1) * depth]
                    ai = adj[length:, h * depth : (h + 1) * depth]
                    sr = sens_v[k, 0, x].astype(F32)
                    si = sens_v[k, 1, x].astype(F32)
                    re = sr * ar + si * ai
                    im = sr * ai - si * ar
                    total[h] = [re, im] if k == 0 else [total[h][0] + re, total[h][1] + im]
            for h in range(group):
                x = j * rows + group * i + h
                for p in range(2):
                    for q in range(shares):
                        grad[q, p, x] = total[h][p][q * share : (q + 1) * share].astype(BF16)
            return carry

        lax.fori_loop(0, rows // group, pair, 0)
        lines = pl.ds(j * rows, rows)
        for off in range(1, shares):
            target = lax.rem(mine + off, shares)
            pltpu.make_async_remote_copy(
                src_ref=grad.at[target, :, lines],
                dst_ref=got.at[mine, :, lines],
                send_sem=grad_send,
                recv_sem=grad_recv.at[j],
                device_id={"coil": target},
                device_id_type=pl.DeviceIdType.MESH,
            ).start()

        @pl.when(j >= LAG)
        def settled():
            add_band(j - LAG, 0)

        return carry

    lax.fori_loop(0, chunks, do_band, 0)
    lax.fori_loop(max(chunks - LAG, 0), chunks, add_band, 0)
    gone = landing.at[ready:coils, 0 : n - 1]
    pltpu.make_async_copy(gone, gone, send).wait()
    gone = got.at[0 : shares - 1]
    pltpu.make_async_copy(gone, gone, grad_send).wait()


def finish_call(table, backs, sent, sensitivity, shares, n, kl):
    coils, _, xl, length, depth = sensitivity.shape
    chunks = xl
    rows = xl // chunks
    share = length // shares
    vmem = pl.BlockSpec(memory_space=pltpu.VMEM)
    scratch = [
        pltpu.VMEM(table.shape, BF16),
        pltpu.VMEM((coils, n, 2, xl * kl, depth), BF16),
        pltpu.VMEM(sensitivity.shape, BF16),
        pltpu.VMEM((shares, 2, xl, share, depth), BF16),
        pltpu.VMEM((shares, 2, xl, share, depth), BF16),
        pltpu.SemaphoreType.DMA((chunks,)),
        pltpu.SemaphoreType.DMA,
        pltpu.SemaphoreType.DMA((coils * n + coils + 1,)),
        pltpu.SemaphoreType.DMA((chunks,)),
        pltpu.SemaphoreType.DMA,
    ]
    if kl % 16:
        scratch.append(pltpu.VMEM((coils, n, 2, rows * kl, depth), F32))
    limit = VMEM_LIMIT - 32 * xl * share * depth
    return pl.pallas_call(
        functools.partial(finish_kernel, n, shares, kl, xl, chunks, sent),
        in_specs=[HBM] * (2 + coils * n),
        out_specs=vmem,
        out_shape=pltpu.VMEM((2, xl, share, depth), F32),
        scratch_shapes=scratch,
        compiler_params=params(limit, collective_id=0, has_side_effects=True),
        name="finish",
    )(table, sensitivity, *[piece for back in backs for piece in back])


def haar_rows(first, second):
    even = lax.broadcasted_iota(jnp.int32, first.shape, 0) % 2 == 0
    rows = first.shape[0]

    def along(v):
        after = pltpu.roll(v, rows - 1, 0)
        ahead = pltpu.roll(v, 1, 0)
        return jnp.where(even, v + after, ahead - v) * 0.5

    return along(first + second), along(first - second)


def update_kernel(image, gradient, auxiliary, dual, image_out, aux_out, dual_out):
    rows = image.shape[1]
    for m in range(0, rows, 2):
        coeffs = []
        for p in range(2):
            target = haar_rows(
                auxiliary[p, m] - dual[p, m], auxiliary[p, m + 1] - dual[p, m + 1]
            )
            following = []
            for h in range(2):
                current = image[p, m + h]
                value = current - step_size * (
                    gradient[p, m + h].astype(F32) + penalty * (current - target[h])
                )
                image_out[p, m + h] = value
                following.append(value)
            spread = haar_rows(*following)
            coeffs.append([spread[h] + dual[p, m + h] for h in range(2)])
        for h in range(2):
            re, im = coeffs[0][h], coeffs[1][h]
            magnitude = jnp.sqrt(re * re + im * im)
            factor = jnp.maximum(1.0 - threshold / jnp.maximum(magnitude, threshold), 0.0)
            for p, value in enumerate((re, im)):
                kept = value * factor
                aux_out[p, m + h] = kept
                dual_out[p, m + h] = value - kept


def update_call(image, gradient, auxiliary, dual):
    _, xl, share, depth = auxiliary.shape
    rows = 8 if xl % 8 == 0 else 2
    plain = pl.BlockSpec((2, rows, share, depth), lambda i: (0, i, 0, 0))
    shape = jax.ShapeDtypeStruct(auxiliary.shape, F32)
    return pl.pallas_call(
        update_kernel,
        grid=(xl // rows,),
        in_specs=[plain, plain, plain, plain],
        out_specs=[plain, plain, plain],
        out_shape=[shape, shape, shape],
        compiler_params=params(VMEM_LIMIT - 128 * xl * share * depth),
        name="update",
    )(image, gradient, auxiliary, dual)


def body(image, sensitivity, blocks, samples, offsets, counts, auxiliary, scaled_dual):
    coils, _, xl, length_y, _ = sensitivity.shape
    n = lax.axis_size("slab")
    shares = lax.axis_size("coil")
    kl = length_y // n
    y_fwd = complex_table(length_y, False)
    y_inv = complex_table(length_y, True)
    x_fwd = complex_table(n * xl, False)
    x_inv = complex_table(n * xl, True)

    def swap(parts):
        moved = list(parts)
        for off in turns(n):
            moved[off] = lax.ppermute(parts[off], "slab", [(i, ahead(i, off, n)) for i in range(n)])
        return moved

    batches = [[c] for c in range(coils)]

    def parts_of(c):
        if c == 0 and xl % 32 == 0:
            return [(0, xl // 2), (xl // 2, xl // 2)]
        return [(0, xl)]

    def tile_of(pieces, place, c):
        return tile_call(
            x_fwd, x_inv, pieces, parts_of(c), place, blocks, sorted_samples, offsets, counts, c, n, kl, xl
        )

    share = length_y // shares
    pieces, tiles, table = [], [], y_fwd
    for batch in batches:
        c = batch[0]
        moved = []
        for first, size in parts_of(c):
            half = list(forward_call(table, image, sensitivity, batch, first, size, n, kl))
            table, half[0] = lax.optimization_barrier((table, half[0]))
            moved += swap(half)
        pieces += [(moved, place) for place in range(len(batch))]
    table, samples, source = lax.optimization_barrier((table, samples, image))
    sorted_samples = sort_call(samples)
    current = lax.dynamic_slice_in_dim(source, lax.axis_index("coil") * share, share, 2)
    for c in range(coils):
        arrived, place = pieces[c]
        if c:
            arrived = list(arrived)
            arrived[0], tiles[-1][0] = lax.optimization_barrier((arrived[0], tiles[-1][0]))
        tiles.append(list(tile_of(arrived, place, c)))
    early = max(coils - 3, 0)
    backs = list(tiles)
    for c in range(early):
        backs[c] = swap(tiles[c])
    gradient = finish_call(y_inv, backs, coils - early, sensitivity, shares, n, kl)
    return tuple(update_call(current, gradient, auxiliary, scaled_dual))


def solution(mesh):
    return jax.shard_map(
        body,
        mesh=mesh,
        in_specs=(
            P(None, "slab", None, None),
            P("coil", None, "slab", None, None),
            P("slab", None, None, None),
            P("slab", None, None, "coil", None, None),
            P("slab", None),
            P("slab"),
            P(None, "slab", "coil", None),
            P(None, "slab", "coil", None),
        ),
        out_specs=(
            P(None, "slab", "coil", None),
            P(None, "slab", "coil", None),
            P(None, "slab", "coil", None),
        ),
        check_vma=False,
    )
```

```python
import functools
import math

import jax
import jax.numpy as jnp
import numpy as np
from jax import lax
from jax.experimental import pallas as pl
from jax.experimental.pallas import tpu as pltpu
from jax.sharding import PartitionSpec as P

step_size = 0.5
penalty = 1.0
threshold = 0.3
VMEM_LIMIT = 67000000
F32 = jnp.float32
BF16 = jnp.bfloat16


def complex_table(length, inverse):
    index = np.arange(length, dtype=np.int64)
    angle = (index[:, None] * index[None, :] % length).astype(np.float64) * (2.0 * math.pi / length)
    factor = 1.0 / math.sqrt(length)
    re = np.cos(angle) * factor
    im = -np.sin(angle) * factor
    if inverse:
        whole = np.block([[re, im], [-im, re]])
    else:
        whole = np.block([[re, -im], [im, re]])
    return jnp.asarray(whole.astype(np.float32)).astype(BF16)


HBM = pl.BlockSpec(memory_space=pltpu.HBM)


def params(limit=VMEM_LIMIT, **extra):
    return pltpu.CompilerParams(vmem_limit_bytes=limit, **extra)


def ahead(me, off, n):
    return (me + off) % n


def behind(me, off, n):
    return (me + n - off) % n


def turns(n):
    return [*range(2, n, 2), *range(3, n, 2), 1]


def once(shape):
    return pl.BlockSpec(shape, lambda *i: (0,) * len(shape), pipeline_mode=pl.Buffered(1))


def cost(flops, nbytes):
    return pl.CostEstimate(flops=int(flops), bytes_accessed=int(nbytes), transcendentals=0)


def pitch(rows):
    tiles = -(-rows // 8)
    return 8 * (tiles + 1 - tiles % 2)


def gather_rows(ref, row, parts_n):
    pieces = []
    for p in range(2):
        for s in range(parts_n):
            pieces.append(ref[s, p, row])
    return jnp.concatenate(pieces, axis=0)


def forward_kernel(n, kl, xp, table, image, sens, *refs):
    outs, flat = refs[:n], refs[n]
    rows, length = image.shape[1], image.shape[2]
    me = lax.axis_index("slab")
    coil, step = pl.program_id(0), pl.program_id(1)

    def pair(i, carry):
        columns = []
        for h in range(2):
            x = 2 * i + h
            sr = sens[0, 0, x].astype(F32)
            si = sens[0, 1, x].astype(F32)
            ir = image[0, x]
            ii = image[1, x]
            columns.append(
                jnp.concatenate(
                    [(sr * ir - si * ii).astype(BF16), (sr * ii + si * ir).astype(BF16)], axis=0
                )
            )
        both = jnp.concatenate(columns, axis=1)
        half = jnp.dot(table[...], both, preferred_element_type=F32)
        depth = half.shape[1] // 2
        for h in range(2):
            where = pl.ds(step * rows + 2 * i + h, 2 * length, stride=pitch(xp))
            flat[where, :] = half[:, h * depth : (h + 1) * depth]
        return carry

    lax.fori_loop(0, rows // 2, pair, 0, unroll=2)

    @pl.when(step == pl.num_programs(1) - 1)
    def last():
        for off in range(n):
            d = ahead(me, off, n)
            for p in range(2):

                def settle(k, carry):
                    base = pl.multiple_of(((p * n + d) * kl + 2 * k) * pitch(xp), 8)
                    for h in range(2):
                        outs[off][coil, p, 2 * k + h] = flat[pl.ds(base + h * pitch(xp), xp), :].astype(BF16)
                    return carry

                lax.fori_loop(0, kl // 2, settle, 0, unroll=8)


def forward_call(table, image, sensitivity, batch, first, xp, n, kl):
    _, _, _, length, depth = sensitivity.shape
    rows = 4 if xp % 4 == 0 else xp
    steps, skip = xp // rows, first // rows
    shape = (len(batch), 2, kl, xp, depth)
    return pl.pallas_call(
        functools.partial(forward_kernel, n, kl, xp),
        grid=(len(batch), steps),
        in_specs=[
            once(table.shape),
            pl.BlockSpec((2, rows, length, depth), lambda c, i: (0, skip + i, 0, 0)),
            pl.BlockSpec((1, 2, rows, length, depth), lambda c, i: (batch[0] + c, 0, skip + i, 0, 0)),
        ],
        out_specs=[once(shape)] * n,
        out_shape=[jax.ShapeDtypeStruct(shape, BF16)] * n,
        scratch_shapes=[pltpu.VMEM(((2 * length + 1) * pitch(xp), depth), F32)],
        compiler_params=params(),
        cost_estimate=cost(8 * len(batch) * length * length * xp * depth, 12 * len(batch) * xp * length * depth),
        name="forward",
    )(table, image, sensitivity)


def sort_kernel(samples, out, flat):
    parts = out.shape[0]
    psize = out.shape[2]
    depth = samples.shape[2]
    for g in range(samples.shape[0]):
        flat[...] = samples[g].astype(F32)
        for c in range(parts):
            for p in range(2):
                rows = flat[pl.ds(2 * c + p, psize, stride=2 * parts), :]
                out[c, g, :, p * depth : (p + 1) * depth] = rows.astype(BF16)


def sort_call(samples):
    _, slots, psize, coils, parts, depth = samples.shape
    group = 4 if slots % 4 == 0 else 1
    lines = psize * coils * parts
    return pl.pallas_call(
        sort_kernel,
        grid=(slots // group,),
        in_specs=[pl.BlockSpec((group, lines, depth), lambda i: (i, 0, 0))],
        out_specs=pl.BlockSpec((coils, group, psize, parts * depth), lambda i: (0, i, 0, 0)),
        out_shape=jax.ShapeDtypeStruct((coils, slots, psize, parts * depth), BF16),
        scratch_shapes=[pltpu.VMEM((lines, depth), F32)],
        compiler_params=params(),
        cost_estimate=cost(samples.size, 4 * samples.size),
        name="sort",
    )(samples.reshape(slots, lines, depth))


def tile_kernel(n, kl, xl, win, parts, coil, place, offsets, counts, fwd, inv, blocks, sorted_samples, *refs):
    count = n * len(parts)
    pieces, outs, refs = refs[:count], refs[count : count + n], refs[count + n :]
    total, kspace, weights, piece, samples, leaving, sem, piece_sem, *wide = refs
    me = lax.axis_index("slab")
    copies = []
    for off in range(n):
        for h, (start, size) in enumerate(parts):
            target = piece.at[behind(me, off, n), :, :, pl.ds(start, size)]
            copies.append(pltpu.make_async_copy(pieces[h * n + off].at[place], target, piece_sem.at[h * n + off]))
    for copy in copies:
        copy.start()
    for copy in copies:
        copy.wait()
    fetches = [
        pltpu.make_async_copy(blocks.at[0], weights, sem.at[0]),
        pltpu.make_async_copy(sorted_samples.at[coil], samples, sem.at[1]),
    ]
    for fetch in fetches:
        fetch.start()
    length = n * xl
    depth = piece.shape[-1]
    if wide:
        source = wide[0]
        for p in range(2):
            for s in range(n):
                source[s, p] = piece[s, p].astype(F32)
    else:
        source = piece

    def to_kspace(i, carry):
        columns = []
        for h in range(2):
            columns.append(gather_rows(source, 2 * i + h, n).astype(BF16))
        spec = jnp.dot(fwd[...], jnp.concatenate(columns, axis=1), preferred_element_type=F32)
        for h in range(2):
            for p in range(2):
                total[p, pl.ds(2 * i + h, length, stride=pitch(kl)), :] = spec[
                    p * length : (p + 1) * length, h * depth : (h + 1) * depth
                ]
        return carry

    lax.fori_loop(0, kl // 2, to_kspace, 0, unroll=2)

    def settle(i, carry):
        rows = pl.ds(pl.multiple_of(i * pitch(kl), 8), kl)
        target = pl.ds(pl.multiple_of(i * kl, kl), kl)
        for p in range(2):
            kspace[target, p * depth : (p + 1) * depth] = total[p, rows, :].astype(kspace.dtype)
            total[p, rows, :] = jnp.zeros((kl, depth), F32)
        return carry

    lax.fori_loop(0, length, settle, 0, unroll=8)
    for fetch in fetches:
        fetch.wait()
    cells = win * kl
    chunk = min(cells, 512)

    def misfit_of(slot):
        start = pl.multiple_of(offsets[0, slot] * kl, kl)
        window = kspace[pl.ds(start, cells), :].astype(BF16)
        predicted = jnp.dot(weights[slot], window, preferred_element_type=F32)
        return (predicted - samples[slot].astype(F32)).astype(BF16)

    def group(slot, misfit):
        following = misfit_of(jnp.minimum(slot + 1, weights.shape[0] - 1))
        first = offsets[0, slot]
        for c in range(0, cells, chunk):
            update = lax.dot_general(
                weights[slot, :, c : c + chunk],
                misfit,
                (((0,), (0,)), ((), ())),
                preferred_element_type=F32,
            )
            for k in range(chunk // kl):
                rows = pl.ds(pl.multiple_of((first + c // kl + k) * pitch(kl), 8), kl)
                for p in range(2):
                    total[p, rows, :] += update[k * kl : (k + 1) * kl, p * depth : (p + 1) * depth]
        return following

    lax.fori_loop(0, counts[0], group, misfit_of(0))

    def to_rows(i, carry):
        columns = []
        for h in range(2):
            columns.append(
                jnp.concatenate(
                    [total[p, pl.ds(2 * i + h, length, stride=pitch(kl)), :].astype(BF16) for p in range(2)], axis=0
                )
            )
        back = jnp.dot(inv[...], jnp.concatenate(columns, axis=1), preferred_element_type=F32)
        for h in range(2):
            for p in range(2):
                total[p, pl.ds(2 * i + h, length, stride=pitch(kl)), :] = back[
                    p * length : (p + 1) * length, h * depth : (h + 1) * depth
                ]
        return carry

    lax.fori_loop(0, kl // 2, to_rows, 0, unroll=2)
    for off in range(n):
        d = ahead(me, off, n)
        for p in range(2):

            def leave(k, carry):
                base = pl.multiple_of((d * xl + 2 * k) * pitch(kl), 8)
                rows = [total[p, pl.ds(base + h * pitch(kl), kl), :] for h in range(2)]
                target = pl.ds(pl.multiple_of(2 * k * kl, 2 * kl), 2 * kl)
                leaving[off, p, target, :] = jnp.concatenate(rows, axis=0).astype(BF16)
                return carry

            lax.fori_loop(0, xl // 2, leave, 0, unroll=4)
        pltpu.make_async_copy(leaving.at[off], outs[off], piece_sem.at[off]).start()
    for off in range(n):
        pltpu.make_async_copy(leaving.at[off], outs[off], piece_sem.at[off]).wait()


def tile_call(fwd, inv, pieces, parts, place, blocks, samples, offsets, counts, coil, n, kl, xl):
    depth = pieces[0].shape[-1]
    _, slots, psize, cells = blocks.shape
    length = n * xl
    narrow = kl % 16 == 0 and xl % 16 == 0
    scratch = [
        pltpu.VMEM((2, (length + 1) * pitch(kl), depth), F32),
        pltpu.VMEM((length * kl, 2 * depth), BF16 if narrow else F32),
        pltpu.VMEM(blocks.shape[1:], BF16),
        pltpu.VMEM((n, 2, kl, xl, depth), BF16),
        pltpu.VMEM((slots, psize, 2 * depth), BF16),
        pltpu.VMEM((n, 2, xl * kl, depth), BF16),
        pltpu.SemaphoreType.DMA((2,)),
        pltpu.SemaphoreType.DMA((len(pieces),)),
    ]
    if not narrow:
        scratch.append(pltpu.VMEM((n, 2, kl, xl, depth), F32))
    smem = pl.BlockSpec(memory_space=pltpu.SMEM)
    return pl.pallas_call(
        functools.partial(tile_kernel, n, kl, xl, cells // kl, parts, coil, place),
        grid=(1,),
        in_specs=[smem, smem, once(fwd.shape), once(inv.shape), HBM, HBM] + [HBM] * len(pieces),
        out_specs=[HBM] * n,
        out_shape=[jax.ShapeDtypeStruct((2, xl * kl, depth), BF16)] * n,
        scratch_shapes=scratch,
        compiler_params=params(),
        cost_estimate=cost(
            16 * length * length * kl * depth + 8 * slots * psize * cells * depth,
            8 * length * kl * depth + 2 * blocks.size,
        ),
        name="tile",
    )(offsets, counts, fwd, inv, blocks, samples, *pieces)


def haar_rows(first, second):
    even = lax.broadcasted_iota(jnp.int32, first.shape, 0) % 2 == 0
    rows = first.shape[0]

    def along(v):
        after = pltpu.roll(v, rows - 1, 0)
        ahead = pltpu.roll(v, 1, 0)
        return jnp.where(even, v + after, ahead - v) * 0.5

    return along(first + second), along(first - second)


def update_pair(m, image, gradient, auxiliary, dual, image_out, aux_out, dual_out):
    coeffs = []
    for p in range(2):
        target = haar_rows(auxiliary[p, m] - dual[p, m], auxiliary[p, m + 1] - dual[p, m + 1])
        following = []
        for h in range(2):
            current = image[p, m + h]
            value = current - step_size * (gradient[p, m + h] + penalty * (current - target[h]))
            following.append(value)
        for h in range(2):
            image_out[p, m + h] = following[h]
        spread = haar_rows(*following)
        coeffs.append([spread[h] + dual[p, m + h] for h in range(2)])
    for h in range(2):
        re, im = coeffs[0][h], coeffs[1][h]
        magnitude = jnp.sqrt(re * re + im * im)
        factor = jnp.maximum(1.0 - threshold / jnp.maximum(magnitude, threshold), 0.0)
        for p, value in enumerate((re, im)):
            kept = value * factor
            aux_out[p, m + h] = kept
            dual_out[p, m + h] = value - kept


def store_kernel(*refs):
    count = len(refs) // 2
    copies = [
        pltpu.make_async_copy(refs[k].at[p], refs[count + k].at[p], refs[-1].at[k, p])
        for k in range(count)
        for p in range(2)
    ]
    for copy in copies:
        copy.start()
    for copy in copies:
        copy.wait()


def store_call(*values):
    return pl.pallas_call(
        store_kernel,
        in_specs=[pl.BlockSpec(memory_space=pltpu.VMEM)] * len(values),
        out_specs=[HBM] * len(values),
        out_shape=[jax.ShapeDtypeStruct(value.shape, value.dtype) for value in values],
        scratch_shapes=[pltpu.SemaphoreType.DMA((len(values), 2))],
        compiler_params=params(2**24),
        name="store",
    )(*values)


def finish_kernel(n, shares, kl, xl, chunks, sent, table_ref, sens, image, auxiliary, dual, *refs):
    coils = sens.shape[0]
    backs, refs = [refs[k * n : (k + 1) * n] for k in range(coils)], refs[coils * n :]
    image_out, aux_out, dual_out, table, held, landing, sens_v, grad, got, recv, send, local, grad_recv, grad_send, *wide = refs
    ready = coils - sent
    length = n * kl
    depth = landing.shape[-1]
    share = length // shares
    rows = xl // chunks
    band = rows * kl
    group = min(rows, 2)
    me = lax.axis_index("slab")
    mine = lax.axis_index("coil")

    barrier = pltpu.get_barrier_semaphore()

    def greet(off, carry):
        pl.semaphore_signal(
            barrier, inc=1, device_id={"slab": lax.rem(me + off, n)}, device_id_type=pl.DeviceIdType.MESH
        )
        return carry

    lax.fori_loop(1, n, greet, 0)
    for off in range(1, shares):
        pl.semaphore_signal(
            barrier, inc=1, device_id={"coil": lax.rem(mine + off, shares)}, device_id_type=pl.DeviceIdType.MESH
        )
    pl.semaphore_wait(barrier, n - 1 + shares - 1)

    def send_band(j, carry):
        where = pl.ds(pl.multiple_of(j * band, band), band)
        for k in range(ready, coils):
            for off in turns(n):
                pltpu.make_async_remote_copy(
                    src_ref=backs[k][off].at[:, where, :],
                    dst_ref=landing.at[k, me, :, where, :],
                    send_sem=send,
                    recv_sem=recv.at[j],
                    device_id={"slab": ahead(me, off, n)},
                    device_id_type=pl.DeviceIdType.MESH,
                ).start()
        return carry

    lax.fori_loop(0, chunks, send_band, 0)
    columns = pl.ds(pl.multiple_of(mine * share, share), share)
    copies = [pltpu.make_async_copy(table_ref, table, local.at[coils * n + coils])]
    for k, source in enumerate((image.at[:, :, columns], auxiliary, dual)):
        copies.append(pltpu.make_async_copy(source, held.at[k], local.at[coils * n + coils + 1 + k]))
    for k in range(coils):
        for off in range(n if k < ready else 1):
            origin = landing.at[k, behind(me, off, n)]
            copies.append(pltpu.make_async_copy(backs[k][off], origin, local.at[k * n + off]))
        copies.append(pltpu.make_async_copy(sens.at[k], sens_v.at[k], local.at[coils * n + k]))
    for copy in copies:
        copy.start()
    for copy in copies:
        copy.wait()

    def add_band(j):
        arrived = got.at[0 : shares - 1, :, pl.ds(j * rows, rows)]
        pltpu.make_async_copy(arrived, arrived, grad_recv.at[j]).wait()
        for i in range(rows):
            x = j * rows + i
            for p in range(2):
                value = grad[mine, p, x].astype(F32)
                for off in range(1, shares):
                    value += got[lax.rem(mine + off, shares), p, x].astype(F32)
                image_out[p, x] = value

    def settle(m):
        for k in range(2 // rows):
            add_band(2 // rows * m + k)
        update_pair(2 * m, held.at[0], image_out, held.at[1], held.at[2], image_out, aux_out, dual_out)

    def do_band(j, carry):
        where = pl.ds(pl.multiple_of(j * band, band), band)
        arrived = landing.at[ready:coils, 0 : n - 1, :, where, :]
        pltpu.make_async_copy(arrived, arrived, recv.at[j]).wait()
        if wide:
            for k in range(coils):
                for s in range(n):
                    for p in range(2):
                        wide[0][k, s, p] = landing[k, s, p, where, :].astype(F32)

        def columns_of(k, i):
            pieces = []
            for p in range(2):
                for s in range(n):
                    if wide:
                        pieces.append(wide[0][k, s, p, pl.ds(pl.multiple_of(i * kl, kl), kl), :])
                    else:
                        row = pl.multiple_of((j * rows + i) * kl, kl)
                        pieces.append(landing[k, s, p, pl.ds(row, kl), :])
            return jnp.concatenate(pieces, axis=0).astype(BF16)

        def pair(i, carry):
            total = [[None, None]] * group
            for k in range(coils):
                both = jnp.concatenate([columns_of(k, group * i + h) for h in range(group)], axis=1)
                adj = jnp.dot(table[...], both, preferred_element_type=F32)
                adj = adj.astype(BF16).astype(F32)
                for h in range(group):
                    x = j * rows + group * i + h
                    ar = adj[:length, h * depth : (h + 1) * depth]
                    ai = adj[length:, h * depth : (h + 1) * depth]
                    sr = sens_v[k, 0, x].astype(F32)
                    si = sens_v[k, 1, x].astype(F32)
                    re = sr * ar + si * ai
                    im = sr * ai - si * ar
                    total[h] = [re, im] if k == 0 else [total[h][0] + re, total[h][1] + im]
            for h in range(group):
                x = j * rows + group * i + h
                for p in range(2):
                    for q in range(shares):
                        grad[q, p, x] = total[h][p][q * share : (q + 1) * share].astype(BF16)
            return carry

        lax.fori_loop(0, rows // group, pair, 0)
        lines = pl.ds(j * rows, rows)
        for off in range(1, shares):
            target = lax.rem(mine + off, shares)
            pltpu.make_async_remote_copy(
                src_ref=grad.at[target, :, lines],
                dst_ref=got.at[mine, :, lines],
                send_sem=grad_send,
                recv_sem=grad_recv.at[j],
                device_id={"coil": target},
                device_id_type=pl.DeviceIdType.MESH,
            ).start()

        @pl.when((j % 2 == 1) & (j >= 3))
        def settled():
            settle((j - 3) // 2)

        return carry

    lax.fori_loop(0, chunks, do_band, 0)
    settle(chunks // 2 - 1)
    gone = landing.at[ready:coils, 0 : n - 1]
    pltpu.make_async_copy(gone, gone, send).wait()
    gone = got.at[0 : shares - 1]
    pltpu.make_async_copy(gone, gone, grad_send).wait()


def finish_call(table, backs, sent, sensitivity, image, auxiliary, dual, shares, n, kl):
    coils, _, xl, length, depth = sensitivity.shape
    chunks = xl
    rows = xl // chunks
    share = length // shares
    vmem = pl.BlockSpec(memory_space=pltpu.VMEM)
    scratch = [
        pltpu.VMEM(table.shape, BF16),
        pltpu.VMEM((3, 2, xl, share, depth), F32),
        pltpu.VMEM((coils, n, 2, xl * kl, depth), BF16),
        pltpu.VMEM(sensitivity.shape, BF16),
        pltpu.VMEM((shares, 2, xl, share, depth), BF16),
        pltpu.VMEM((shares, 2, xl, share, depth), BF16),
        pltpu.SemaphoreType.DMA((chunks,)),
        pltpu.SemaphoreType.DMA,
        pltpu.SemaphoreType.DMA((coils * n + coils + 4,)),
        pltpu.SemaphoreType.DMA((chunks,)),
        pltpu.SemaphoreType.DMA,
    ]
    if kl % 16:
        scratch.append(pltpu.VMEM((coils, n, 2, rows * kl, depth), F32))
    limit = VMEM_LIMIT - 26 * xl * share * depth
    return pl.pallas_call(
        functools.partial(finish_kernel, n, shares, kl, xl, chunks, sent),
        in_specs=[HBM] * (5 + coils * n),
        out_specs=[vmem] * 3,
        out_shape=[pltpu.VMEM((2, xl, share, depth), F32)] * 3,
        scratch_shapes=scratch,
        compiler_params=params(limit, collective_id=0, has_side_effects=True),
        name="finish",
    )(table, sensitivity, image, auxiliary, dual, *[piece for back in backs for piece in back])


def body(image, sensitivity, blocks, samples, offsets, counts, auxiliary, scaled_dual):
    coils, _, xl, length_y, _ = sensitivity.shape
    n = lax.axis_size("slab")
    shares = lax.axis_size("coil")
    kl = length_y // n
    y_fwd = complex_table(length_y, False)
    y_inv = complex_table(length_y, True)
    x_fwd = complex_table(n * xl, False)
    x_inv = complex_table(n * xl, True)

    def swap(parts):
        moved = list(parts)
        for off in turns(n):
            moved[off] = lax.ppermute(parts[off], "slab", [(i, ahead(i, off, n)) for i in range(n)])
        return moved

    batches = [[c] for c in range(coils)]

    def parts_of(c):
        if c == 0 and xl % 32 == 0:
            return [(0, xl // 2), (xl // 2, xl // 2)]
        return [(0, xl)]

    def tile_of(pieces, place, c):
        return tile_call(
            x_fwd, x_inv, pieces, parts_of(c), place, blocks, sorted_samples, offsets, counts, c, n, kl, xl
        )

    pieces, tiles, table = [], [], y_fwd
    for batch in batches:
        c = batch[0]
        moved = []
        for first, size in parts_of(c):
            half = list(forward_call(table, image, sensitivity, batch, first, size, n, kl))
            table, half[0] = lax.optimization_barrier((table, half[0]))
            moved += swap(half)
        pieces += [(moved, place) for place in range(len(batch))]
    table, samples = lax.optimization_barrier((table, samples))
    sorted_samples = sort_call(samples)
    for c in range(coils):
        arrived, place = pieces[c]
        if c:
            arrived = list(arrived)
            arrived[0], tiles[-1][0] = lax.optimization_barrier((arrived[0], tiles[-1][0]))
        tiles.append(list(tile_of(arrived, place, c)))
    early = max(coils - 3, 0)
    backs = list(tiles)
    for c in range(early):
        backs[c] = swap(tiles[c])
    results = finish_call(
        y_inv, backs, coils - early, sensitivity, image, auxiliary, scaled_dual, shares, n, kl
    )
    return tuple(store_call(*results))


def solution(mesh):
    return jax.shard_map(
        body,
        mesh=mesh,
        in_specs=(
            P(None, "slab", None, None),
            P("coil", None, "slab", None, None),
            P("slab", None, None, None),
            P("slab", None, None, "coil", None, None),
            P("slab", None),
            P("slab"),
            P(None, "slab", "coil", None),
            P(None, "slab", "coil", None),
        ),
        out_specs=(
            P(None, "slab", "coil", None),
            P(None, "slab", "coil", None),
            P(None, "slab", "coil", None),
        ),
        check_vma=False,
    )
```

```python
import functools
import math

import jax
import jax.numpy as jnp
import numpy as np
from jax import lax
from jax.experimental import pallas as pl
from jax.experimental.pallas import tpu as pltpu
from jax.sharding import PartitionSpec as P

step_size = 0.5
penalty = 1.0
threshold = 0.3
VMEM_LIMIT = 67000000
SPLIT = 4
F32 = jnp.float32
BF16 = jnp.bfloat16


def complex_table(length, inverse):
    index = np.arange(length, dtype=np.int64)
    angle = (index[:, None] * index[None, :] % length).astype(np.float64) * (2.0 * math.pi / length)
    factor = 1.0 / math.sqrt(length)
    re = np.cos(angle) * factor
    im = -np.sin(angle) * factor
    if inverse:
        whole = np.block([[re, im], [-im, re]])
    else:
        whole = np.block([[re, -im], [im, re]])
    return jnp.asarray(whole.astype(np.float32)).astype(BF16)


HBM = pl.BlockSpec(memory_space=pltpu.HBM)


def params(limit=VMEM_LIMIT, **extra):
    return pltpu.CompilerParams(vmem_limit_bytes=limit, **extra)


def ahead(me, off, n):
    return (me + off) % n


def behind(me, off, n):
    return (me + n - off) % n


def turns(n):
    return [*range(2, n, 2), *range(3, n, 2), 1]


def once(shape):
    return pl.BlockSpec(shape, lambda *i: (0,) * len(shape), pipeline_mode=pl.Buffered(1))


def cost(flops, nbytes):
    return pl.CostEstimate(flops=int(flops), bytes_accessed=int(nbytes), transcendentals=0)


def pitch(rows):
    tiles = -(-rows // 8)
    return 8 * (tiles + 1 - tiles % 2)


def gather_rows(ref, row, parts_n):
    pieces = []
    for p in range(2):
        for s in range(parts_n):
            pieces.append(ref[s, p, row])
    return jnp.concatenate(pieces, axis=0)


def forward_kernel(n, kl, xp, offs, table, image, sens, *refs):
    outs, flat = refs[: len(offs)], refs[len(offs)]
    rows, length = image.shape[1], image.shape[2]
    me = lax.axis_index("slab")
    coil, step = pl.program_id(0), pl.program_id(1)
    lines = 2 * length
    if len(offs) < n:
        whole, table = table, refs[len(offs) + 1]
        lines = table.shape[0]

        @pl.when((coil == 0) & (step == 0))
        def gather():
            for p in range(2):
                for i, off in enumerate(offs):
                    source = pl.ds(pl.multiple_of(p * length + ahead(me, off, n) * kl, kl), kl)
                    table[(p * len(offs) + i) * kl : (p * len(offs) + i + 1) * kl, :] = whole[source, :]

    def pair(i, carry):
        columns = []
        for h in range(2):
            x = 2 * i + h
            sr = sens[0, 0, x].astype(F32)
            si = sens[0, 1, x].astype(F32)
            ir = image[0, x]
            ii = image[1, x]
            columns.append(
                jnp.concatenate(
                    [(sr * ir - si * ii).astype(BF16), (sr * ii + si * ir).astype(BF16)], axis=0
                )
            )
        both = jnp.concatenate(columns, axis=1)
        half = jnp.dot(table[...], both, preferred_element_type=F32)
        depth = half.shape[1] // 2
        for h in range(2):
            where = pl.ds(step * rows + 2 * i + h, lines, stride=pitch(xp))
            flat[where, :] = half[:, h * depth : (h + 1) * depth]
        return carry

    lax.fori_loop(0, rows // 2, pair, 0, unroll=2)

    @pl.when(step == pl.num_programs(1) - 1)
    def last():
        for i, off in enumerate(offs):
            d = ahead(me, off, n) if len(offs) == n else i
            for p in range(2):

                def settle(k, carry):
                    base = pl.multiple_of(((p * len(offs) + d) * kl + 2 * k) * pitch(xp), 8)
                    for h in range(2):
                        outs[i][coil, p, 2 * k + h] = flat[pl.ds(base + h * pitch(xp), xp), :].astype(BF16)
                    return carry

                lax.fori_loop(0, kl // 2, settle, 0, unroll=4)


def forward_call(table, image, sensitivity, batch, first, xp, offs, n, kl):
    _, _, _, length, depth = sensitivity.shape
    rows = 8 if xp % 8 == 0 else xp
    steps, skip = xp // rows, first // rows
    shape = (len(batch), 2, kl, xp, depth)
    return pl.pallas_call(
        functools.partial(forward_kernel, n, kl, xp, offs),
        grid=(len(batch), steps),
        in_specs=[
            once(table.shape),
            pl.BlockSpec((2, rows, length, depth), lambda c, i: (0, skip + i, 0, 0)),
            pl.BlockSpec((1, 2, rows, length, depth), lambda c, i: (batch[0] + c, 0, skip + i, 0, 0)),
        ],
        out_specs=[once(shape)] * len(offs),
        out_shape=[jax.ShapeDtypeStruct(shape, BF16)] * len(offs),
        scratch_shapes=[pltpu.VMEM(((2 * len(offs) * kl + 1) * pitch(xp), depth), F32)]
        + ([pltpu.VMEM((2 * len(offs) * kl, table.shape[1]), BF16)] if len(offs) < n else []),
        compiler_params=params(),
        cost_estimate=cost(8 * len(batch) * length * length * xp * depth, 12 * len(batch) * xp * length * depth),
        name="forward",
    )(table, image, sensitivity)


def sort_kernel(samples, out, flat):
    parts = out.shape[0]
    psize = out.shape[2]
    depth = samples.shape[2]
    for g in range(samples.shape[0]):
        flat[...] = samples[g].astype(F32)
        for c in range(parts):
            for p in range(2):
                rows = flat[pl.ds(2 * c + p, psize, stride=2 * parts), :]
                out[c, g, :, p * depth : (p + 1) * depth] = rows.astype(BF16)


def sort_call(samples):
    _, slots, psize, coils, parts, depth = samples.shape
    group = 4 if slots % 4 == 0 else 1
    lines = psize * coils * parts
    return pl.pallas_call(
        sort_kernel,
        grid=(slots // group,),
        in_specs=[pl.BlockSpec((group, lines, depth), lambda i: (i, 0, 0))],
        out_specs=pl.BlockSpec((coils, group, psize, parts * depth), lambda i: (0, i, 0, 0)),
        out_shape=jax.ShapeDtypeStruct((coils, slots, psize, parts * depth), BF16),
        scratch_shapes=[pltpu.VMEM((lines, depth), F32)],
        compiler_params=params(),
        cost_estimate=cost(samples.size, 4 * samples.size),
        name="sort",
    )(samples.reshape(slots, lines, depth))


def tile_kernel(n, kl, xl, win, parts, coil, place, offsets, counts, fwd, inv, blocks, sorted_samples, *refs):
    count = n * len(parts)
    pieces, outs, refs = refs[:count], refs[count : count + n], refs[count + n :]
    total, kspace, weights, piece, samples, leaving, sem, piece_sem, *wide = refs
    me = lax.axis_index("slab")
    copies = []
    for off in range(n):
        for h, (start, size) in enumerate(parts):
            target = piece.at[behind(me, off, n), :, :, pl.ds(start, size)]
            copies.append(pltpu.make_async_copy(pieces[h * n + off].at[place], target, piece_sem.at[h * n + off]))
    for copy in copies:
        copy.start()
    for copy in copies:
        copy.wait()
    fetches = [
        pltpu.make_async_copy(blocks.at[0], weights, sem.at[0]),
        pltpu.make_async_copy(sorted_samples.at[coil], samples, sem.at[1]),
    ]
    for fetch in fetches:
        fetch.start()
    length = n * xl
    depth = piece.shape[-1]
    if wide:
        source = wide[0]
        for p in range(2):
            for s in range(n):
                source[s, p] = piece[s, p].astype(F32)
    else:
        source = piece

    def to_kspace(i, carry):
        columns = []
        for h in range(2):
            columns.append(gather_rows(source, 2 * i + h, n).astype(BF16))
        spec = jnp.dot(fwd[...], jnp.concatenate(columns, axis=1), preferred_element_type=F32)
        for h in range(2):
            for p in range(2):
                total[p, pl.ds(2 * i + h, length, stride=pitch(kl)), :] = spec[
                    p * length : (p + 1) * length, h * depth : (h + 1) * depth
                ]
        return carry

    lax.fori_loop(0, kl // 2, to_kspace, 0, unroll=2)

    def settle(i, carry):
        rows = pl.ds(pl.multiple_of(i * pitch(kl), 8), kl)
        target = pl.ds(pl.multiple_of(i * kl, kl), kl)
        for p in range(2):
            kspace[target, p * depth : (p + 1) * depth] = total[p, rows, :].astype(kspace.dtype)
            total[p, rows, :] = jnp.zeros((kl, depth), F32)
        return carry

    lax.fori_loop(0, length, settle, 0, unroll=8)
    for fetch in fetches:
        fetch.wait()
    cells = win * kl
    chunk = min(cells, 512)

    def misfit_of(slot):
        start = pl.multiple_of(offsets[0, slot] * kl, kl)
        window = kspace[pl.ds(start, cells), :].astype(BF16)
        predicted = jnp.dot(weights[slot], window, preferred_element_type=F32)
        return (predicted - samples[slot].astype(F32)).astype(BF16)

    def group(slot, misfit):
        following = misfit_of(jnp.minimum(slot + 1, weights.shape[0] - 1))
        first = offsets[0, slot]
        for c in range(0, cells, chunk):
            update = lax.dot_general(
                weights[slot, :, c : c + chunk],
                misfit,
                (((0,), (0,)), ((), ())),
                preferred_element_type=F32,
            )
            for k in range(chunk // kl):
                rows = pl.ds(pl.multiple_of((first + c // kl + k) * pitch(kl), 8), kl)
                for p in range(2):
                    total[p, rows, :] += update[k * kl : (k + 1) * kl, p * depth : (p + 1) * depth]
        return following

    lax.fori_loop(0, counts[0], group, misfit_of(0))

    def to_rows(i, carry):
        columns = []
        for h in range(2):
            columns.append(
                jnp.concatenate(
                    [total[p, pl.ds(2 * i + h, length, stride=pitch(kl)), :].astype(BF16) for p in range(2)], axis=0
                )
            )
        back = jnp.dot(inv[...], jnp.concatenate(columns, axis=1), preferred_element_type=F32)
        for h in range(2):
            for p in range(2):
                total[p, pl.ds(2 * i + h, length, stride=pitch(kl)), :] = back[
                    p * length : (p + 1) * length, h * depth : (h + 1) * depth
                ]
        return carry

    lax.fori_loop(0, kl // 2, to_rows, 0, unroll=2)
    for off in range(n):
        d = ahead(me, off, n)
        for p in range(2):

            def leave(k, carry):
                base = pl.multiple_of((d * xl + 2 * k) * pitch(kl), 8)
                rows = [total[p, pl.ds(base + h * pitch(kl), kl), :] for h in range(2)]
                target = pl.ds(pl.multiple_of(2 * k * kl, 2 * kl), 2 * kl)
                leaving[off, p, target, :] = jnp.concatenate(rows, axis=0).astype(BF16)
                return carry

            lax.fori_loop(0, xl // 2, leave, 0, unroll=4)
        pltpu.make_async_copy(leaving.at[off], outs[off], piece_sem.at[off]).start()
    for off in range(n):
        pltpu.make_async_copy(leaving.at[off], outs[off], piece_sem.at[off]).wait()


def tile_call(fwd, inv, pieces, parts, place, blocks, samples, offsets, counts, coil, n, kl, xl):
    depth = pieces[0].shape[-1]
    _, slots, psize, cells = blocks.shape
    length = n * xl
    narrow = kl % 16 == 0 and xl % 16 == 0
    scratch = [
        pltpu.VMEM((2, (length + 1) * pitch(kl), depth), F32),
        pltpu.VMEM((length * kl, 2 * depth), BF16 if narrow else F32),
        pltpu.VMEM(blocks.shape[1:], BF16),
        pltpu.VMEM((n, 2, kl, xl, depth), BF16),
        pltpu.VMEM((slots, psize, 2 * depth), BF16),
        pltpu.VMEM((n, 2, xl * kl, depth), BF16),
        pltpu.SemaphoreType.DMA((2,)),
        pltpu.SemaphoreType.DMA((len(pieces),)),
    ]
    if not narrow:
        scratch.append(pltpu.VMEM((n, 2, kl, xl, depth), F32))
    smem = pl.BlockSpec(memory_space=pltpu.SMEM)
    return pl.pallas_call(
        functools.partial(tile_kernel, n, kl, xl, cells // kl, parts, coil, place),
        grid=(1,),
        in_specs=[smem, smem, once(fwd.shape), once(inv.shape), HBM, HBM] + [HBM] * len(pieces),
        out_specs=[HBM] * n,
        out_shape=[jax.ShapeDtypeStruct((2, xl * kl, depth), BF16)] * n,
        scratch_shapes=scratch,
        compiler_params=params(),
        cost_estimate=cost(
            16 * length * length * kl * depth + 8 * slots * psize * cells * depth,
            8 * length * kl * depth + 2 * blocks.size,
        ),
        name="tile",
    )(offsets, counts, fwd, inv, blocks, samples, *pieces)


def haar_rows(first, second):
    even = lax.broadcasted_iota(jnp.int32, first.shape, 0) % 2 == 0
    rows = first.shape[0]

    def along(v):
        after = pltpu.roll(v, rows - 1, 0)
        ahead = pltpu.roll(v, 1, 0)
        return jnp.where(even, v + after, ahead - v) * 0.5

    return along(first + second), along(first - second)


def update_pair(m, image, gradient, auxiliary, dual, image_out, aux_out, dual_out):
    coeffs = []
    for p in range(2):
        target = haar_rows(auxiliary[p, m] - dual[p, m], auxiliary[p, m + 1] - dual[p, m + 1])
        following = []
        for h in range(2):
            current = image[p, m + h]
            value = current - step_size * (gradient[p, m + h] + penalty * (current - target[h]))
            following.append(value)
        for h in range(2):
            image_out[p, m + h] = following[h]
        spread = haar_rows(*following)
        coeffs.append([spread[h] + dual[p, m + h] for h in range(2)])
    for h in range(2):
        re, im = coeffs[0][h], coeffs[1][h]
        magnitude = jnp.sqrt(re * re + im * im)
        factor = jnp.maximum(1.0 - threshold / jnp.maximum(magnitude, threshold), 0.0)
        for p, value in enumerate((re, im)):
            kept = value * factor
            aux_out[p, m + h] = kept
            dual_out[p, m + h] = value - kept


def store_kernel(*refs):
    count = len(refs) // 2
    rows = refs[0].shape[1] // SPLIT
    copies = [
        pltpu.make_async_copy(
            refs[k].at[p, pl.ds(q * rows, rows)], refs[count + k].at[p, pl.ds(q * rows, rows)], refs[-1].at[k, p, q]
        )
        for k in range(count)
        for p in range(2)
        for q in range(SPLIT)
    ]
    for copy in copies:
        copy.start()
    for copy in copies:
        copy.wait()


def store_call(*values):
    return pl.pallas_call(
        store_kernel,
        in_specs=[pl.BlockSpec(memory_space=pltpu.VMEM)] * len(values),
        out_specs=[HBM] * len(values),
        out_shape=[jax.ShapeDtypeStruct(value.shape, value.dtype) for value in values],
        scratch_shapes=[pltpu.SemaphoreType.DMA((len(values), 2, SPLIT))],
        compiler_params=params(2**24),
        name="store",
    )(*values)


def finish_kernel(n, shares, kl, xl, chunks, sent, table_ref, sens, image, auxiliary, dual, *refs):
    coils = sens.shape[0]
    backs, refs = [refs[k * n : (k + 1) * n] for k in range(coils)], refs[coils * n :]
    image_out, aux_out, dual_out, table, held, landing, sens_v, grad, got, recv, send, local, grad_recv, grad_send, *wide = refs
    ready = coils - sent
    length = n * kl
    depth = landing.shape[-1]
    share = length // shares
    rows = xl // chunks
    band = rows * kl
    group = min(rows, 2)
    me = lax.axis_index("slab")
    mine = lax.axis_index("coil")

    barrier = pltpu.get_barrier_semaphore()

    def greet(off, carry):
        pl.semaphore_signal(
            barrier, inc=1, device_id={"slab": lax.rem(me + off, n)}, device_id_type=pl.DeviceIdType.MESH
        )
        return carry

    lax.fori_loop(1, n, greet, 0)
    for off in range(1, shares):
        pl.semaphore_signal(
            barrier, inc=1, device_id={"coil": lax.rem(mine + off, shares)}, device_id_type=pl.DeviceIdType.MESH
        )
    pl.semaphore_wait(barrier, n - 1 + shares - 1)

    def send_band(j, carry):
        where = pl.ds(pl.multiple_of(j * band, band), band)
        for k in range(ready, coils):
            for off in turns(n):
                pltpu.make_async_remote_copy(
                    src_ref=backs[k][off].at[:, where, :],
                    dst_ref=landing.at[k, me, :, where, :],
                    send_sem=send,
                    recv_sem=recv.at[j],
                    device_id={"slab": ahead(me, off, n)},
                    device_id_type=pl.DeviceIdType.MESH,
                ).start()
        return carry

    lax.fori_loop(0, chunks, send_band, 0)
    columns = pl.ds(pl.multiple_of(mine * share, share), share)
    copies = [pltpu.make_async_copy(table_ref, table, local.at[coils * n + coils])]
    for k, source in enumerate((image.at[:, :, columns], auxiliary, dual)):
        copies.append(pltpu.make_async_copy(source, held.at[k], local.at[coils * n + coils + 1 + k]))
    for k in range(coils):
        for off in range(n if k < ready else 1):
            origin = landing.at[k, behind(me, off, n)]
            copies.append(pltpu.make_async_copy(backs[k][off], origin, local.at[k * n + off]))
        copies.append(pltpu.make_async_copy(sens.at[k], sens_v.at[k], local.at[coils * n + k]))
    for copy in copies:
        copy.start()
    for copy in copies:
        copy.wait()

    def add_band(j):
        arrived = got.at[0 : shares - 1, :, pl.ds(j * rows, rows)]
        pltpu.make_async_copy(arrived, arrived, grad_recv.at[j]).wait()
        for i in range(rows):
            x = j * rows + i
            for p in range(2):
                value = grad[mine, p, x].astype(F32)
                for off in range(1, shares):
                    value += got[lax.rem(mine + off, shares), p, x].astype(F32)
                image_out[p, x] = value

    def settle(m):
        for k in range(2 // rows):
            add_band(2 // rows * m + k)
        update_pair(2 * m, held.at[0], image_out, held.at[1], held.at[2], image_out, aux_out, dual_out)

    def do_band(j, carry):
        where = pl.ds(pl.multiple_of(j * band, band), band)
        arrived = landing.at[ready:coils, 0 : n - 1, :, where, :]
        pltpu.make_async_copy(arrived, arrived, recv.at[j]).wait()
        if wide:
            for k in range(coils):
                for s in range(n):
                    for p in range(2):
                        wide[0][k, s, p] = landing[k, s, p, where, :].astype(F32)

        def columns_of(k, i):
            pieces = []
            for p in range(2):
                for s in range(n):
                    if wide:
                        pieces.append(wide[0][k, s, p, pl.ds(pl.multiple_of(i * kl, kl), kl), :])
                    else:
                        row = pl.multiple_of((j * rows + i) * kl, kl)
                        pieces.append(landing[k, s, p, pl.ds(row, kl), :])
            return jnp.concatenate(pieces, axis=0).astype(BF16)

        def pair(i, carry):
            total = [[None, None]] * group
            for k in range(coils):
                both = jnp.concatenate([columns_of(k, group * i + h) for h in range(group)], axis=1)
                adj = jnp.dot(table[...], both, preferred_element_type=F32)
                adj = adj.astype(BF16).astype(F32)
                for h in range(group):
                    x = j * rows + group * i + h
                    ar = adj[:length, h * depth : (h + 1) * depth]
                    ai = adj[length:, h * depth : (h + 1) * depth]
                    sr = sens_v[k, 0, x].astype(F32)
                    si = sens_v[k, 1, x].astype(F32)
                    re = sr * ar + si * ai
                    im = sr * ai - si * ar
                    total[h] = [re, im] if k == 0 else [total[h][0] + re, total[h][1] + im]
            for h in range(group):
                x = j * rows + group * i + h
                for p in range(2):
                    for q in range(shares):
                        grad[q, p, x] = total[h][p][q * share : (q + 1) * share].astype(BF16)
            return carry

        lax.fori_loop(0, rows // group, pair, 0)
        lines = pl.ds(j * rows, rows)
        for off in range(1, shares):
            target = lax.rem(mine + off, shares)
            pltpu.make_async_remote_copy(
                src_ref=grad.at[target, :, lines],
                dst_ref=got.at[mine, :, lines],
                send_sem=grad_send,
                recv_sem=grad_recv.at[j],
                device_id={"coil": target},
                device_id_type=pl.DeviceIdType.MESH,
            ).start()

        @pl.when((j % 2 == 1) & (j >= 3))
        def settled():
            settle((j - 3) // 2)

        return carry

    lax.fori_loop(0, chunks, do_band, 0)
    settle(chunks // 2 - 1)
    gone = landing.at[ready:coils, 0 : n - 1]
    pltpu.make_async_copy(gone, gone, send).wait()
    gone = got.at[0 : shares - 1]
    pltpu.make_async_copy(gone, gone, grad_send).wait()


def finish_call(table, backs, sent, sensitivity, image, auxiliary, dual, shares, n, kl):
    coils, _, xl, length, depth = sensitivity.shape
    chunks = xl
    rows = xl // chunks
    share = length // shares
    vmem = pl.BlockSpec(memory_space=pltpu.VMEM)
    scratch = [
        pltpu.VMEM(table.shape, BF16),
        pltpu.VMEM((3, 2, xl, share, depth), F32),
        pltpu.VMEM((coils, n, 2, xl * kl, depth), BF16),
        pltpu.VMEM(sensitivity.shape, BF16),
        pltpu.VMEM((shares, 2, xl, share, depth), BF16),
        pltpu.VMEM((shares, 2, xl, share, depth), BF16),
        pltpu.SemaphoreType.DMA((chunks,)),
        pltpu.SemaphoreType.DMA,
        pltpu.SemaphoreType.DMA((coils * n + coils + 4,)),
        pltpu.SemaphoreType.DMA((chunks,)),
        pltpu.SemaphoreType.DMA,
    ]
    if kl % 16:
        scratch.append(pltpu.VMEM((coils, n, 2, rows * kl, depth), F32))
    limit = VMEM_LIMIT - 26 * xl * share * depth
    return pl.pallas_call(
        functools.partial(finish_kernel, n, shares, kl, xl, chunks, sent),
        in_specs=[HBM] * (5 + coils * n),
        out_specs=[vmem] * 3,
        out_shape=[pltpu.VMEM((2, xl, share, depth), F32)] * 3,
        scratch_shapes=scratch,
        compiler_params=params(limit, collective_id=0, has_side_effects=True),
        name="finish",
    )(table, sensitivity, image, auxiliary, dual, *[piece for back in backs for piece in back])


def body(image, sensitivity, blocks, samples, offsets, counts, auxiliary, scaled_dual):
    coils, _, xl, length_y, _ = sensitivity.shape
    n = lax.axis_size("slab")
    shares = lax.axis_size("coil")
    kl = length_y // n
    y_fwd = complex_table(length_y, False)
    y_inv = complex_table(length_y, True)
    x_fwd = complex_table(n * xl, False)
    x_inv = complex_table(n * xl, True)

    def swap(parts, offs):
        moved = list(parts)
        for turn, off in enumerate(offs):
            if off:
                moved[turn] = lax.ppermute(parts[turn], "slab", [(i, ahead(i, off, n)) for i in range(n)])
        return moved

    batches = [[c] for c in range(coils)]

    def parts_of(c):
        if c == 0 and xl % 32 == 0:
            return [(0, xl // 2), (xl // 2, xl // 2)]
        return [(0, xl)]

    def tile_of(pieces, place, c):
        return tile_call(
            x_fwd, x_inv, pieces, parts_of(c), place, blocks, sorted_samples, offsets, counts, c, n, kl, xl
        )

    pieces, tiles, table = [], [], y_fwd
    for batch in batches:
        c = batch[0]
        everyone = [*turns(n), 0]
        moved = []
        jobs = [(first, size, everyone) for first, size in parts_of(c)]
        if len(jobs) > 1 and n >= 4 and kl % 16 == 0:
            first, size, _ = jobs[0]
            jobs[:1] = [(first, size, everyone[: n // 2]), (first, size, everyone[n // 2 :])]
        for first, size, offs in jobs:
            half = list(forward_call(table, image, sensitivity, batch, first, size, offs, n, kl))
            table, half[-1] = lax.optimization_barrier((table, half[-1]))
            moved += swap(half, offs)
        ordered = []
        for h in range(len(parts_of(c))):
            ordered += [moved[h * n + everyone.index(off)] for off in range(n)]
        moved = ordered
        pieces += [(moved, place) for place in range(len(batch))]
    table, samples = lax.optimization_barrier((table, samples))
    sorted_samples = sort_call(samples)
    for c in range(coils):
        arrived, place = pieces[c]
        if c:
            arrived = list(arrived)
            arrived[0], tiles[-1][0] = lax.optimization_barrier((arrived[0], tiles[-1][0]))
        tiles.append(list(tile_of(arrived, place, c)))
    early = max(coils - 3, 0)
    backs = list(tiles)
    for c in range(early):
        backs[c] = swap(tiles[c], range(n))
    results = finish_call(
        y_inv, backs, coils - early, sensitivity, image, auxiliary, scaled_dual, shares, n, kl
    )
    return tuple(store_call(*results))


def solution(mesh):
    return jax.shard_map(
        body,
        mesh=mesh,
        in_specs=(
            P(None, "slab", None, None),
            P("coil", None, "slab", None, None),
            P("slab", None, None, None),
            P("slab", None, None, "coil", None, None),
            P("slab", None),
            P("slab"),
            P(None, "slab", "coil", None),
            P(None, "slab", "coil", None),
        ),
        out_specs=(
            P(None, "slab", "coil", None),
            P(None, "slab", "coil", None),
            P(None, "slab", "coil", None),
        ),
        check_vma=False,
    )
```

```python
import functools
import math

import jax
import jax.numpy as jnp
import numpy as np
from jax import lax
from jax.experimental import pallas as pl
from jax.experimental.pallas import tpu as pltpu
from jax.sharding import PartitionSpec as P

step_size = 0.5
penalty = 1.0
threshold = 0.3
VMEM_LIMIT = 67000000
SPLIT = 4
F32 = jnp.float32
BF16 = jnp.bfloat16


def complex_table(length, inverse):
    index = np.arange(length, dtype=np.int64)
    angle = (index[:, None] * index[None, :] % length).astype(np.float64) * (2.0 * math.pi / length)
    factor = 1.0 / math.sqrt(length)
    re = np.cos(angle) * factor
    im = -np.sin(angle) * factor
    if inverse:
        whole = np.block([[re, im], [-im, re]])
    else:
        whole = np.block([[re, -im], [im, re]])
    return jnp.asarray(whole.astype(np.float32)).astype(BF16)


HBM = pl.BlockSpec(memory_space=pltpu.HBM)


def params(limit=VMEM_LIMIT, **extra):
    return pltpu.CompilerParams(vmem_limit_bytes=limit, **extra)


def ahead(me, off, n):
    return (me + off) % n


def behind(me, off, n):
    return (me + n - off) % n


def turns(n):
    return [*range(2, n, 2), *range(3, n, 2), 1]


def once(shape):
    return pl.BlockSpec(shape, lambda *i: (0,) * len(shape), pipeline_mode=pl.Buffered(1))


def cost(flops, nbytes):
    return pl.CostEstimate(flops=int(flops), bytes_accessed=int(nbytes), transcendentals=0)


def pitch(rows):
    tiles = -(-rows // 8)
    return 8 * (tiles + 1 - tiles % 2)


def gather_rows(ref, row, parts_n):
    pieces = []
    for p in range(2):
        for s in range(parts_n):
            pieces.append(ref[s, p, row])
    return jnp.concatenate(pieces, axis=0)


def forward_kernel(n, kl, xp, offs, table, image, sens, *refs):
    outs, flat = refs[: len(offs)], refs[len(offs)]
    rows, length = image.shape[1], image.shape[2]
    me = lax.axis_index("slab")
    coil, step = pl.program_id(0), pl.program_id(1)
    lines = 2 * length
    if len(offs) < n:
        whole, table = table, refs[len(offs) + 1]
        lines = table.shape[0]

        @pl.when((coil == 0) & (step == 0))
        def gather():
            for p in range(2):
                for i, off in enumerate(offs):
                    source = pl.ds(pl.multiple_of(p * length + ahead(me, off, n) * kl, kl), kl)
                    table[(p * len(offs) + i) * kl : (p * len(offs) + i + 1) * kl, :] = whole[source, :]

    def pair(i, carry):
        columns = []
        for h in range(2):
            x = 2 * i + h
            sr = sens[0, 0, x].astype(F32)
            si = sens[0, 1, x].astype(F32)
            ir = image[0, x]
            ii = image[1, x]
            columns.append(
                jnp.concatenate(
                    [(sr * ir - si * ii).astype(BF16), (sr * ii + si * ir).astype(BF16)], axis=0
                )
            )
        both = jnp.concatenate(columns, axis=1)
        half = jnp.dot(table[...], both, preferred_element_type=F32)
        depth = half.shape[1] // 2
        for h in range(2):
            where = pl.ds(step * rows + 2 * i + h, lines, stride=pitch(xp))
            flat[where, :] = half[:, h * depth : (h + 1) * depth]
        return carry

    lax.fori_loop(0, rows // 2, pair, 0, unroll=2)

    @pl.when(step == pl.num_programs(1) - 1)
    def last():
        for i, off in enumerate(offs):
            d = ahead(me, off, n) if len(offs) == n else i
            for p in range(2):

                def settle(k, carry):
                    base = pl.multiple_of(((p * len(offs) + d) * kl + 2 * k) * pitch(xp), 8)
                    for h in range(2):
                        outs[i][coil, p, 2 * k + h] = flat[pl.ds(base + h * pitch(xp), xp), :].astype(BF16)
                    return carry

                lax.fori_loop(0, kl // 2, settle, 0, unroll=4)


def forward_call(table, image, sensitivity, batch, first, xp, offs, n, kl):
    _, _, _, length, depth = sensitivity.shape
    rows = 8 if xp % 8 == 0 else xp
    steps, skip = xp // rows, first // rows
    shape = (len(batch), 2, kl, xp, depth)
    return pl.pallas_call(
        functools.partial(forward_kernel, n, kl, xp, offs),
        grid=(len(batch), steps),
        in_specs=[
            once(table.shape),
            pl.BlockSpec((2, rows, length, depth), lambda c, i: (0, skip + i, 0, 0)),
            pl.BlockSpec((1, 2, rows, length, depth), lambda c, i: (batch[0] + c, 0, skip + i, 0, 0)),
        ],
        out_specs=[once(shape)] * len(offs),
        out_shape=[jax.ShapeDtypeStruct(shape, BF16)] * len(offs),
        scratch_shapes=[pltpu.VMEM(((2 * len(offs) * kl + 1) * pitch(xp), depth), F32)]
        + ([pltpu.VMEM((2 * len(offs) * kl, table.shape[1]), BF16)] if len(offs) < n else []),
        compiler_params=params(),
        cost_estimate=cost(8 * len(batch) * length * length * xp * depth, 12 * len(batch) * xp * length * depth),
        name="forward",
    )(table, image, sensitivity)


def sort_kernel(samples, out, flat):
    parts = out.shape[0]
    psize = out.shape[2]
    depth = samples.shape[2]
    for g in range(samples.shape[0]):
        flat[...] = samples[g].astype(F32)
        for c in range(parts):
            for p in range(2):
                rows = flat[pl.ds(2 * c + p, psize, stride=2 * parts), :]
                out[c, g, :, p * depth : (p + 1) * depth] = rows.astype(BF16)


def sort_call(samples):
    _, slots, psize, coils, parts, depth = samples.shape
    group = 4 if slots % 4 == 0 else 1
    lines = psize * coils * parts
    return pl.pallas_call(
        sort_kernel,
        grid=(slots // group,),
        in_specs=[pl.BlockSpec((group, lines, depth), lambda i: (i, 0, 0))],
        out_specs=pl.BlockSpec((coils, group, psize, parts * depth), lambda i: (0, i, 0, 0)),
        out_shape=jax.ShapeDtypeStruct((coils, slots, psize, parts * depth), BF16),
        scratch_shapes=[pltpu.VMEM((lines, depth), F32)],
        compiler_params=params(),
        cost_estimate=cost(samples.size, 4 * samples.size),
        name="sort",
    )(samples.reshape(slots, lines, depth))


def tile_kernel(n, kl, xl, win, parts, coil, place, offsets, counts, fwd, inv, blocks, sorted_samples, *refs):
    count = n * len(parts)
    pieces, outs, refs = refs[:count], refs[count : count + n], refs[count + n :]
    total, kspace, weights, piece, samples, leaving, sem, piece_sem, *wide = refs
    me = lax.axis_index("slab")
    copies = []
    for off in range(n):
        for h, (start, size) in enumerate(parts):
            target = piece.at[behind(me, off, n), :, :, pl.ds(start, size)]
            copies.append(pltpu.make_async_copy(pieces[h * n + off].at[place], target, piece_sem.at[h * n + off]))
    for copy in copies:
        copy.start()
    for copy in copies:
        copy.wait()
    fetches = [
        pltpu.make_async_copy(blocks.at[0], weights, sem.at[0]),
        pltpu.make_async_copy(sorted_samples.at[coil], samples, sem.at[1]),
    ]
    for fetch in fetches:
        fetch.start()
    length = n * xl
    depth = piece.shape[-1]
    if wide:
        source = wide[0]
        for p in range(2):
            for s in range(n):
                source[s, p] = piece[s, p].astype(F32)
    else:
        source = piece

    def to_kspace(i, carry):
        columns = []
        for h in range(2):
            columns.append(gather_rows(source, 2 * i + h, n).astype(BF16))
        spec = jnp.dot(fwd[...], jnp.concatenate(columns, axis=1), preferred_element_type=F32)
        for h in range(2):
            for p in range(2):
                total[p, pl.ds(2 * i + h, length, stride=pitch(kl)), :] = spec[
                    p * length : (p + 1) * length, h * depth : (h + 1) * depth
                ]
        return carry

    lax.fori_loop(0, kl // 2, to_kspace, 0, unroll=2)

    def settle(i, carry):
        rows = pl.ds(pl.multiple_of(i * pitch(kl), 8), kl)
        target = pl.ds(pl.multiple_of(i * kl, kl), kl)
        for p in range(2):
            kspace[target, p * depth : (p + 1) * depth] = total[p, rows, :].astype(kspace.dtype)
            total[p, rows, :] = jnp.zeros((kl, depth), F32)
        return carry

    lax.fori_loop(0, length, settle, 0, unroll=8)
    for fetch in fetches:
        fetch.wait()
    cells = win * kl
    chunk = min(cells, 512)

    def misfit_of(slot):
        start = pl.multiple_of(offsets[0, slot] * kl, kl)
        window = kspace[pl.ds(start, cells), :].astype(BF16)
        predicted = jnp.dot(weights[slot], window, preferred_element_type=F32)
        return (predicted - samples[slot].astype(F32)).astype(BF16)

    def group(slot, misfit):
        following = misfit_of(jnp.minimum(slot + 1, weights.shape[0] - 1))
        first = offsets[0, slot]
        for c in range(0, cells, chunk):
            update = lax.dot_general(
                weights[slot, :, c : c + chunk],
                misfit,
                (((0,), (0,)), ((), ())),
                preferred_element_type=F32,
            )
            for k in range(chunk // kl):
                rows = pl.ds(pl.multiple_of((first + c // kl + k) * pitch(kl), 8), kl)
                for p in range(2):
                    total[p, rows, :] += update[k * kl : (k + 1) * kl, p * depth : (p + 1) * depth]
        return following

    lax.fori_loop(0, counts[0], group, misfit_of(0))

    def to_rows(i, carry):
        columns = []
        for h in range(2):
            columns.append(
                jnp.concatenate(
                    [total[p, pl.ds(2 * i + h, length, stride=pitch(kl)), :].astype(BF16) for p in range(2)], axis=0
                )
            )
        back = jnp.dot(inv[...], jnp.concatenate(columns, axis=1), preferred_element_type=F32)
        for h in range(2):
            for p in range(2):
                total[p, pl.ds(2 * i + h, length, stride=pitch(kl)), :] = back[
                    p * length : (p + 1) * length, h * depth : (h + 1) * depth
                ]
        return carry

    lax.fori_loop(0, kl // 2, to_rows, 0, unroll=2)
    for off in range(n):
        d = ahead(me, off, n)
        for p in range(2):

            def leave(k, carry):
                base = pl.multiple_of((d * xl + 2 * k) * pitch(kl), 8)
                rows = [total[p, pl.ds(base + h * pitch(kl), kl), :] for h in range(2)]
                target = pl.ds(pl.multiple_of(2 * k * kl, 2 * kl), 2 * kl)
                leaving[off, p, target, :] = jnp.concatenate(rows, axis=0).astype(BF16)
                return carry

            lax.fori_loop(0, xl // 2, leave, 0, unroll=4)
        pltpu.make_async_copy(leaving.at[off], outs[off], piece_sem.at[off]).start()
    for off in range(n):
        pltpu.make_async_copy(leaving.at[off], outs[off], piece_sem.at[off]).wait()


def tile_call(fwd, inv, pieces, parts, place, blocks, samples, offsets, counts, coil, n, kl, xl):
    depth = pieces[0].shape[-1]
    _, slots, psize, cells = blocks.shape
    length = n * xl
    narrow = kl % 16 == 0 and xl % 16 == 0
    scratch = [
        pltpu.VMEM((2, (length + 1) * pitch(kl), depth), F32),
        pltpu.VMEM((length * kl, 2 * depth), BF16 if narrow else F32),
        pltpu.VMEM(blocks.shape[1:], BF16),
        pltpu.VMEM((n, 2, kl, xl, depth), BF16),
        pltpu.VMEM((slots, psize, 2 * depth), BF16),
        pltpu.VMEM((n, 2, xl * kl, depth), BF16),
        pltpu.SemaphoreType.DMA((2,)),
        pltpu.SemaphoreType.DMA((len(pieces),)),
    ]
    if not narrow:
        scratch.append(pltpu.VMEM((n, 2, kl, xl, depth), F32))
    smem = pl.BlockSpec(memory_space=pltpu.SMEM)
    return pl.pallas_call(
        functools.partial(tile_kernel, n, kl, xl, cells // kl, parts, coil, place),
        grid=(1,),
        in_specs=[smem, smem, once(fwd.shape), once(inv.shape), HBM, HBM] + [HBM] * len(pieces),
        out_specs=[HBM] * n,
        out_shape=[jax.ShapeDtypeStruct((2, xl * kl, depth), BF16)] * n,
        scratch_shapes=scratch,
        compiler_params=params(),
        cost_estimate=cost(
            16 * length * length * kl * depth + 8 * slots * psize * cells * depth,
            8 * length * kl * depth + 2 * blocks.size,
        ),
        name="tile",
    )(offsets, counts, fwd, inv, blocks, samples, *pieces)


def haar_rows(first, second):
    even = lax.broadcasted_iota(jnp.int32, first.shape, 0) % 2 == 0
    rows = first.shape[0]

    def along(v):
        after = pltpu.roll(v, rows - 1, 0)
        ahead = pltpu.roll(v, 1, 0)
        return jnp.where(even, v + after, ahead - v) * 0.5

    return along(first + second), along(first - second)


def update_pair(m, image, gradient, auxiliary, dual, image_out, aux_out, dual_out):
    coeffs = []
    for p in range(2):
        target = haar_rows(auxiliary[p, m] - dual[p, m], auxiliary[p, m + 1] - dual[p, m + 1])
        following = []
        for h in range(2):
            current = image[p, m + h]
            value = current - step_size * (gradient[p, m + h] + penalty * (current - target[h]))
            following.append(value)
        for h in range(2):
            image_out[p, m + h] = following[h]
        spread = haar_rows(*following)
        coeffs.append([spread[h] + dual[p, m + h] for h in range(2)])
    for h in range(2):
        re, im = coeffs[0][h], coeffs[1][h]
        magnitude = jnp.sqrt(re * re + im * im)
        factor = jnp.maximum(1.0 - threshold / jnp.maximum(magnitude, threshold), 0.0)
        for p, value in enumerate((re, im)):
            kept = value * factor
            aux_out[p, m + h] = kept
            dual_out[p, m + h] = value - kept


def store_kernel(*refs):
    count = len(refs) // 2
    rows = refs[0].shape[1] // SPLIT
    copies = [
        pltpu.make_async_copy(
            refs[k].at[p, pl.ds(q * rows, rows)], refs[count + k].at[p, pl.ds(q * rows, rows)], refs[-1].at[k, p, q]
        )
        for k in range(count)
        for p in range(2)
        for q in range(SPLIT)
    ]
    for copy in copies:
        copy.start()
    for copy in copies:
        copy.wait()


def store_call(*values):
    return pl.pallas_call(
        store_kernel,
        in_specs=[pl.BlockSpec(memory_space=pltpu.VMEM)] * len(values),
        out_specs=[HBM] * len(values),
        out_shape=[jax.ShapeDtypeStruct(value.shape, value.dtype) for value in values],
        scratch_shapes=[pltpu.SemaphoreType.DMA((len(values), 2, SPLIT))],
        compiler_params=params(2**24),
        name="store",
    )(*values)


def finish_kernel(n, shares, kl, xl, sent, table_ref, sens, image, auxiliary, dual, *refs):
    coils = sens.shape[0]
    backs, refs = [refs[k * n : (k + 1) * n] for k in range(coils)], refs[coils * n :]
    image_out, aux_out, dual_out, table, held, landing, sens_v, grad, got, recv, send, local, grad_recv, grad_send, *wide = refs
    ready = coils - sent
    length = n * kl
    share = length // shares
    band = kl
    me = lax.axis_index("slab")
    mine = lax.axis_index("coil")

    barrier = pltpu.get_barrier_semaphore()

    def greet(off, carry):
        pl.semaphore_signal(
            barrier, inc=1, device_id={"slab": lax.rem(me + off, n)}, device_id_type=pl.DeviceIdType.MESH
        )
        return carry

    lax.fori_loop(1, n, greet, 0)
    for off in range(1, shares):
        pl.semaphore_signal(
            barrier, inc=1, device_id={"coil": lax.rem(mine + off, shares)}, device_id_type=pl.DeviceIdType.MESH
        )
    pl.semaphore_wait(barrier, n - 1 + shares - 1)

    def send_band(j, carry):
        where = pl.ds(pl.multiple_of(j * band, band), band)
        for k in range(ready, coils):
            for off in turns(n):
                pltpu.make_async_remote_copy(
                    src_ref=backs[k][off].at[:, where, :],
                    dst_ref=landing.at[k, me, :, where, :],
                    send_sem=send,
                    recv_sem=recv.at[j, k - ready],
                    device_id={"slab": ahead(me, off, n)},
                    device_id_type=pl.DeviceIdType.MESH,
                ).start()
        return carry

    lax.fori_loop(0, xl, send_band, 0)
    columns = pl.ds(pl.multiple_of(mine * share, share), share)
    copies = [pltpu.make_async_copy(table_ref, table, local.at[coils * n + coils])]
    for k, source in enumerate((image.at[:, :, columns], auxiliary, dual)):
        copies.append(pltpu.make_async_copy(source, held.at[k], local.at[coils * n + coils + 1 + k]))
    for k in range(coils):
        for off in range(n if k < ready else 1):
            origin = landing.at[k, behind(me, off, n)]
            copies.append(pltpu.make_async_copy(backs[k][off], origin, local.at[k * n + off]))
        copies.append(pltpu.make_async_copy(sens.at[k], sens_v.at[k], local.at[coils * n + k]))
    for copy in copies:
        copy.start()
    for copy in copies:
        copy.wait()

    def add_band(x):
        arrived = got.at[0 : shares - 1, :, x]
        pltpu.make_async_copy(arrived, arrived, grad_recv.at[x]).wait()
        for p in range(2):
            value = grad[mine, p, x].astype(F32)
            for off in range(1, shares):
                value += got[lax.rem(mine + off, shares), p, x].astype(F32)
            image_out[p, x] = value

    def settle(m):
        for h in range(2):
            add_band(2 * m + h)
        update_pair(2 * m, held.at[0], image_out, held.at[1], held.at[2], image_out, aux_out, dual_out)

    def farthest(turn):
        upper = mine // max(shares // 2, 1)
        down = shares - 2 - turn + (2 * shares - 2 - turn - mine) // shares
        up = turn + 1 - (shares + mine - turn - 1) // shares
        return down * (1 - upper) + up * upper

    def do_band(j, carry):
        where = pl.ds(pl.multiple_of(j * band, band), band)
        re = im = None
        for k in range(coils):
            if k >= ready:
                arrived = landing.at[k, 0 : n - 1, :, where, :]
                pltpu.make_async_copy(arrived, arrived, recv.at[j, k - ready]).wait()
            pieces = [landing[k, s, p, where, :] for p in range(2) for s in range(n)]
            if wide:
                for i, piece in enumerate(pieces):
                    wide[0][i * kl : (i + 1) * kl, :] = piece.astype(F32)
                both = wide[0][...].astype(BF16)
            else:
                both = jnp.concatenate(pieces, axis=0)
            adj = jnp.dot(table[...], both, preferred_element_type=F32)
            adj = adj.astype(BF16).astype(F32)
            ar, ai = adj[:length], adj[length:]
            sr = sens_v[k, 0, j].astype(F32)
            si = sens_v[k, 1, j].astype(F32)
            re = sr * ar + si * ai if k == 0 else re + (sr * ar + si * ai)
            im = sr * ai - si * ar if k == 0 else im + (sr * ai - si * ar)
        for p, value in enumerate((re, im)):
            for q in range(shares):
                grad[q, p, j] = value[q * share : (q + 1) * share].astype(BF16)
        for turn in range(shares - 1):
            target = farthest(turn)
            pltpu.make_async_remote_copy(
                src_ref=grad.at[target, :, j],
                dst_ref=got.at[mine, :, j],
                send_sem=grad_send,
                recv_sem=grad_recv.at[j],
                device_id={"coil": target},
                device_id_type=pl.DeviceIdType.MESH,
            ).start()

        @pl.when((j % 2 == 1) & (j >= 3))
        def settled():
            settle((j - 3) // 2)

        return carry

    lax.fori_loop(0, xl, do_band, 0)
    settle(xl // 2 - 1)
    gone = landing.at[ready:coils, 0 : n - 1]
    pltpu.make_async_copy(gone, gone, send).wait()
    gone = got.at[0 : shares - 1]
    pltpu.make_async_copy(gone, gone, grad_send).wait()


def finish_call(table, backs, sent, sensitivity, image, auxiliary, dual, shares, n, kl):
    coils, _, xl, length, depth = sensitivity.shape
    share = length // shares
    vmem = pl.BlockSpec(memory_space=pltpu.VMEM)
    scratch = [
        pltpu.VMEM(table.shape, BF16),
        pltpu.VMEM((3, 2, xl, share, depth), F32),
        pltpu.VMEM((coils, n, 2, xl * kl, depth), BF16),
        pltpu.VMEM(sensitivity.shape, BF16),
        pltpu.VMEM((shares, 2, xl, share, depth), BF16),
        pltpu.VMEM((shares, 2, xl, share, depth), BF16),
        pltpu.SemaphoreType.DMA((xl, sent)),
        pltpu.SemaphoreType.DMA,
        pltpu.SemaphoreType.DMA((coils * n + coils + 4,)),
        pltpu.SemaphoreType.DMA((xl,)),
        pltpu.SemaphoreType.DMA,
    ]
    if kl % 16:
        scratch.append(pltpu.VMEM((2 * length, depth), F32))
    limit = VMEM_LIMIT - 26 * xl * share * depth
    return pl.pallas_call(
        functools.partial(finish_kernel, n, shares, kl, xl, sent),
        in_specs=[HBM] * (5 + coils * n),
        out_specs=[vmem] * 3,
        out_shape=[pltpu.VMEM((2, xl, share, depth), F32)] * 3,
        scratch_shapes=scratch,
        compiler_params=params(limit, collective_id=0, has_side_effects=True),
        name="finish",
    )(table, sensitivity, image, auxiliary, dual, *[piece for back in backs for piece in back])


def body(image, sensitivity, blocks, samples, offsets, counts, auxiliary, scaled_dual):
    coils, _, xl, length_y, _ = sensitivity.shape
    n = lax.axis_size("slab")
    shares = lax.axis_size("coil")
    kl = length_y // n
    y_fwd = complex_table(length_y, False)
    y_inv = complex_table(length_y, True)
    x_fwd = complex_table(n * xl, False)
    x_inv = complex_table(n * xl, True)

    def swap(parts, offs):
        moved = list(parts)
        for turn, off in enumerate(offs):
            if off:
                moved[turn] = lax.ppermute(parts[turn], "slab", [(i, ahead(i, off, n)) for i in range(n)])
        return moved

    batches = [[c] for c in range(coils)]

    def parts_of(c):
        if c == 0 and xl % 32 == 0:
            return [(0, xl // 2), (xl // 2, xl // 2)]
        return [(0, xl)]

    def tile_of(pieces, place, c):
        return tile_call(
            x_fwd, x_inv, pieces, parts_of(c), place, blocks, sorted_samples, offsets, counts, c, n, kl, xl
        )

    pieces, tiles, table = [], [], y_fwd
    for batch in batches:
        c = batch[0]
        everyone = [*turns(n), 0]
        moved = []
        jobs = [(first, size, everyone) for first, size in parts_of(c)]
        if len(jobs) > 1 and n >= 4 and kl % 16 == 0:
            first, size, _ = jobs[0]
            jobs[:1] = [(first, size, everyone[: n // 2]), (first, size, everyone[n // 2 :])]
        for first, size, offs in jobs:
            half = list(forward_call(table, image, sensitivity, batch, first, size, offs, n, kl))
            table, half[-1] = lax.optimization_barrier((table, half[-1]))
            moved += swap(half, offs)
        ordered = []
        for h in range(len(parts_of(c))):
            ordered += [moved[h * n + everyone.index(off)] for off in range(n)]
        moved = ordered
        pieces += [(moved, place) for place in range(len(batch))]
    table, samples = lax.optimization_barrier((table, samples))
    sorted_samples = sort_call(samples)
    for c in range(coils):
        arrived, place = pieces[c]
        if c:
            arrived = list(arrived)
            arrived[0], tiles[-1][0] = lax.optimization_barrier((arrived[0], tiles[-1][0]))
        tiles.append(list(tile_of(arrived, place, c)))
    early = max(coils - 3, 0)
    backs = list(tiles)
    for c in range(early):
        backs[c] = swap(tiles[c], range(n))
    results = finish_call(
        y_inv, backs, coils - early, sensitivity, image, auxiliary, scaled_dual, shares, n, kl
    )
    return tuple(store_call(*results))


def solution(mesh):
    return jax.shard_map(
        body,
        mesh=mesh,
        in_specs=(
            P(None, "slab", None, None),
            P("coil", None, "slab", None, None),
            P("slab", None, None, None),
            P("slab", None, None, "coil", None, None),
            P("slab", None),
            P("slab"),
            P(None, "slab", "coil", None),
            P(None, "slab", "coil", None),
        ),
        out_specs=(
            P(None, "slab", "coil", None),
            P(None, "slab", "coil", None),
            P(None, "slab", "coil", None),
        ),
        check_vma=False,
    )
```

```python
import functools
import math

import jax
import jax.numpy as jnp
import numpy as np
from jax import lax
from jax.experimental import pallas as pl
from jax.experimental.pallas import tpu as pltpu
from jax.sharding import PartitionSpec as P

step_size = 0.5
penalty = 1.0
threshold = 0.3
VMEM_LIMIT = 67000000
SPLIT = 1
F32 = jnp.float32
BF16 = jnp.bfloat16


def complex_table(length, inverse):
    index = np.arange(length, dtype=np.int64)
    angle = (index[:, None] * index[None, :] % length).astype(np.float64) * (2.0 * math.pi / length)
    factor = 1.0 / math.sqrt(length)
    re = np.cos(angle) * factor
    im = -np.sin(angle) * factor
    if inverse:
        whole = np.block([[re, im], [-im, re]])
    else:
        whole = np.block([[re, -im], [im, re]])
    return jnp.asarray(whole.astype(np.float32)).astype(BF16)


HBM = pl.BlockSpec(memory_space=pltpu.HBM)


def params(limit=VMEM_LIMIT, **extra):
    return pltpu.CompilerParams(vmem_limit_bytes=limit, **extra)


def ahead(me, off, n):
    return (me + off) % n


def behind(me, off, n):
    return (me + n - off) % n


def turns(n):
    return [*range(2, n, 2), *range(3, n, 2), 1]


def once(shape):
    return pl.BlockSpec(shape, lambda *i: (0,) * len(shape), pipeline_mode=pl.Buffered(1))


def cost(flops, nbytes):
    return pl.CostEstimate(flops=int(flops), bytes_accessed=int(nbytes), transcendentals=0)


def pitch(rows):
    tiles = -(-rows // 8)
    return 8 * (tiles + 1 - tiles % 2)


def gather_rows(ref, row, parts_n):
    pieces = []
    for p in range(2):
        for s in range(parts_n):
            pieces.append(ref[s, p, row])
    return jnp.concatenate(pieces, axis=0)


def forward_kernel(n, kl, xp, offs, table, image, sens, *refs):
    outs, flat = refs[: len(offs)], refs[len(offs)]
    rows, length = image.shape[1], image.shape[2]
    me = lax.axis_index("slab")
    coil, step = pl.program_id(0), pl.program_id(1)
    lines = 2 * length
    if len(offs) < n:
        whole, table = table, refs[len(offs) + 1]
        lines = table.shape[0]

        @pl.when((coil == 0) & (step == 0))
        def gather():
            for p in range(2):
                for i, off in enumerate(offs):
                    source = pl.ds(pl.multiple_of(p * length + ahead(me, off, n) * kl, kl), kl)
                    table[(p * len(offs) + i) * kl : (p * len(offs) + i + 1) * kl, :] = whole[source, :]

    def pair(i, carry):
        columns = []
        for h in range(2):
            x = 2 * i + h
            sr = sens[0, 0, x].astype(F32)
            si = sens[0, 1, x].astype(F32)
            ir = image[0, x]
            ii = image[1, x]
            columns.append(
                jnp.concatenate(
                    [(sr * ir - si * ii).astype(BF16), (sr * ii + si * ir).astype(BF16)], axis=0
                )
            )
        both = jnp.concatenate(columns, axis=1)
        half = jnp.dot(table[...], both, preferred_element_type=F32)
        depth = half.shape[1] // 2
        for h in range(2):
            where = pl.ds(step * rows + 2 * i + h, lines, stride=pitch(xp))
            flat[where, :] = half[:, h * depth : (h + 1) * depth]
        return carry

    lax.fori_loop(0, rows // 2, pair, 0, unroll=4)

    @pl.when(step == pl.num_programs(1) - 1)
    def last():
        for i, off in enumerate(offs):
            d = ahead(me, off, n) if len(offs) == n else i
            for p in range(2):

                def settle(k, carry):
                    base = pl.multiple_of(((p * len(offs) + d) * kl + 2 * k) * pitch(xp), 8)
                    for h in range(2):
                        outs[i][coil, p, 2 * k + h] = flat[pl.ds(base + h * pitch(xp), xp), :].astype(BF16)
                    return carry

                lax.fori_loop(0, kl // 2, settle, 0, unroll=4)


def forward_call(table, image, sensitivity, batch, first, xp, offs, n, kl):
    _, _, _, length, depth = sensitivity.shape
    rows = 8 if xp % 8 == 0 else xp
    steps, skip = xp // rows, first // rows
    shape = (len(batch), 2, kl, xp, depth)
    return pl.pallas_call(
        functools.partial(forward_kernel, n, kl, xp, offs),
        grid=(len(batch), steps),
        in_specs=[
            once(table.shape),
            pl.BlockSpec((2, rows, length, depth), lambda c, i: (0, skip + i, 0, 0)),
            pl.BlockSpec((1, 2, rows, length, depth), lambda c, i: (batch[0] + c, 0, skip + i, 0, 0)),
        ],
        out_specs=[once(shape)] * len(offs),
        out_shape=[jax.ShapeDtypeStruct(shape, BF16)] * len(offs),
        scratch_shapes=[pltpu.VMEM(((2 * len(offs) * kl + 1) * pitch(xp), depth), F32)]
        + ([pltpu.VMEM((2 * len(offs) * kl, table.shape[1]), BF16)] if len(offs) < n else []),
        compiler_params=params(),
        cost_estimate=cost(8 * len(batch) * length * length * xp * depth, 12 * len(batch) * xp * length * depth),
        name="forward",
    )(table, image, sensitivity)


def sort_kernel(samples, out, flat):
    parts = out.shape[0]
    psize = out.shape[2]
    depth = samples.shape[2]
    for g in range(samples.shape[0]):
        flat[0 : samples.shape[1], :] = samples[g].astype(F32)
        for c in range(parts):
            for p in range(2):
                rows = flat[pl.ds(2 * c + p, psize, stride=2 * parts), :]
                out[c, g, :, p * depth : (p + 1) * depth] = rows.astype(BF16)


def sort_call(samples):
    _, slots, psize, coils, parts, depth = samples.shape
    group = 4 if slots % 4 == 0 else 1
    lines = psize * coils * parts
    return pl.pallas_call(
        sort_kernel,
        grid=(slots // group,),
        in_specs=[pl.BlockSpec((group, lines, depth), lambda i: (i, 0, 0))],
        out_specs=pl.BlockSpec((coils, group, psize, parts * depth), lambda i: (0, i, 0, 0)),
        out_shape=jax.ShapeDtypeStruct((coils, slots, psize, parts * depth), BF16),
        scratch_shapes=[pltpu.VMEM((lines + 2 * coils * parts, depth), F32)],
        compiler_params=params(),
        cost_estimate=cost(samples.size, 4 * samples.size),
        name="sort",
    )(samples.reshape(slots, lines, depth))


def tile_kernel(n, kl, xl, win, parts, coil, place, offsets, counts, fwd, inv, blocks, sorted_samples, *refs):
    count = n * len(parts)
    pieces, outs, refs = refs[:count], refs[count : count + n], refs[count + n :]
    total, kspace, weights, piece, samples, leaving, sem, piece_sem, *wide = refs
    me = lax.axis_index("slab")
    copies = []
    for off in range(n):
        for h, (start, size) in enumerate(parts):
            target = piece.at[behind(me, off, n), :, :, pl.ds(start, size)]
            copies.append(pltpu.make_async_copy(pieces[h * n + off].at[place], target, piece_sem.at[h * n + off]))
    for copy in copies:
        copy.start()
    for copy in copies:
        copy.wait()
    fetches = [
        pltpu.make_async_copy(blocks.at[0], weights, sem.at[0]),
        pltpu.make_async_copy(sorted_samples.at[coil], samples, sem.at[1]),
    ]
    for fetch in fetches:
        fetch.start()
    length = n * xl
    depth = piece.shape[-1]
    if wide:
        source = wide[0]
        for p in range(2):
            for s in range(n):
                source[s, p] = piece[s, p].astype(F32)
    else:
        source = piece

    def to_kspace(i, carry):
        columns = []
        for h in range(2):
            columns.append(gather_rows(source, 2 * i + h, n).astype(BF16))
        spec = jnp.dot(fwd[...], jnp.concatenate(columns, axis=1), preferred_element_type=F32)
        for h in range(2):
            for p in range(2):
                total[p, pl.ds(2 * i + h, length, stride=pitch(kl)), :] = spec[
                    p * length : (p + 1) * length, h * depth : (h + 1) * depth
                ]
        return carry

    lax.fori_loop(0, kl // 2, to_kspace, 0, unroll=2)

    def settle(i, carry):
        rows = pl.ds(pl.multiple_of(i * pitch(kl), 8), kl)
        target = pl.ds(pl.multiple_of(i * kl, kl), kl)
        for p in range(2):
            kspace[target, p * depth : (p + 1) * depth] = total[p, rows, :].astype(kspace.dtype)
            total[p, rows, :] = jnp.zeros((kl, depth), F32)
        return carry

    lax.fori_loop(0, length, settle, 0, unroll=8)
    for fetch in fetches:
        fetch.wait()
    cells = win * kl
    chunk = min(cells, 512)

    def misfit_of(slot):
        start = pl.multiple_of(offsets[0, slot] * kl, kl)
        window = kspace[pl.ds(start, cells), :].astype(BF16)
        predicted = jnp.dot(weights[slot], window, preferred_element_type=F32)
        return (predicted - samples[slot].astype(F32)).astype(BF16)

    def group(slot, misfit):
        following = misfit_of(jnp.minimum(slot + 1, weights.shape[0] - 1))
        first = offsets[0, slot]
        for c in range(0, cells, chunk):
            update = lax.dot_general(
                weights[slot, :, c : c + chunk],
                misfit,
                (((0,), (0,)), ((), ())),
                preferred_element_type=F32,
            )
            for k in range(chunk // kl):
                rows = pl.ds(pl.multiple_of((first + c // kl + k) * pitch(kl), 8), kl)
                for p in range(2):
                    total[p, rows, :] += update[k * kl : (k + 1) * kl, p * depth : (p + 1) * depth]
        return following

    lax.fori_loop(0, counts[0], group, misfit_of(0))

    def to_rows(i, carry):
        columns = []
        for h in range(2):
            columns.append(
                jnp.concatenate(
                    [total[p, pl.ds(2 * i + h, length, stride=pitch(kl)), :].astype(BF16) for p in range(2)], axis=0
                )
            )
        back = jnp.dot(inv[...], jnp.concatenate(columns, axis=1), preferred_element_type=F32)
        for h in range(2):
            for p in range(2):
                total[p, pl.ds(2 * i + h, length, stride=pitch(kl)), :] = back[
                    p * length : (p + 1) * length, h * depth : (h + 1) * depth
                ]
        return carry

    lax.fori_loop(0, kl // 2, to_rows, 0, unroll=2)
    for off in range(n):
        d = ahead(me, off, n)
        for p in range(2):

            def leave(k, carry):
                base = pl.multiple_of((d * xl + 2 * k) * pitch(kl), 8)
                rows = [total[p, pl.ds(base + h * pitch(kl), kl), :] for h in range(2)]
                target = pl.ds(pl.multiple_of(2 * k * kl, 2 * kl), 2 * kl)
                leaving[off, p, target, :] = jnp.concatenate(rows, axis=0).astype(BF16)
                return carry

            lax.fori_loop(0, xl // 2, leave, 0, unroll=4)
        pltpu.make_async_copy(leaving.at[off], outs[off], piece_sem.at[off]).start()
    for off in range(n):
        pltpu.make_async_copy(leaving.at[off], outs[off], piece_sem.at[off]).wait()


def tile_call(fwd, inv, pieces, parts, place, blocks, samples, offsets, counts, coil, n, kl, xl):
    depth = pieces[0].shape[-1]
    _, slots, psize, cells = blocks.shape
    length = n * xl
    narrow = kl % 16 == 0 and xl % 16 == 0
    scratch = [
        pltpu.VMEM((2, (length + 1) * pitch(kl), depth), F32),
        pltpu.VMEM((length * kl, 2 * depth), BF16 if narrow else F32),
        pltpu.VMEM(blocks.shape[1:], BF16),
        pltpu.VMEM((n, 2, kl, xl, depth), BF16),
        pltpu.VMEM((slots, psize, 2 * depth), BF16),
        pltpu.VMEM((n, 2, xl * kl, depth), BF16),
        pltpu.SemaphoreType.DMA((2,)),
        pltpu.SemaphoreType.DMA((len(pieces),)),
    ]
    if not narrow:
        scratch.append(pltpu.VMEM((n, 2, kl, xl, depth), F32))
    smem = pl.BlockSpec(memory_space=pltpu.SMEM)
    return pl.pallas_call(
        functools.partial(tile_kernel, n, kl, xl, cells // kl, parts, coil, place),
        grid=(1,),
        in_specs=[smem, smem, once(fwd.shape), once(inv.shape), HBM, HBM] + [HBM] * len(pieces),
        out_specs=[HBM] * n,
        out_shape=[jax.ShapeDtypeStruct((2, xl * kl, depth), BF16)] * n,
        scratch_shapes=scratch,
        compiler_params=params(),
        cost_estimate=cost(
            16 * length * length * kl * depth + 8 * slots * psize * cells * depth,
            8 * length * kl * depth + 2 * blocks.size,
        ),
        name="tile",
    )(offsets, counts, fwd, inv, blocks, samples, *pieces)


def haar_rows(first, second):
    even = lax.broadcasted_iota(jnp.int32, first.shape, 0) % 2 == 0
    rows = first.shape[0]

    def along(v):
        after = pltpu.roll(v, rows - 1, 0)
        ahead = pltpu.roll(v, 1, 0)
        return jnp.where(even, v + after, ahead - v) * 0.5

    return along(first + second), along(first - second)


def update_pair(m, image, gradient, auxiliary, dual, image_out, aux_out, dual_out):
    coeffs = []
    for p in range(2):
        target = haar_rows(auxiliary[p, m] - dual[p, m], auxiliary[p, m + 1] - dual[p, m + 1])
        following = []
        for h in range(2):
            current = image[p, m + h]
            value = current - step_size * (gradient[p, m + h] + penalty * (current - target[h]))
            following.append(value)
        for h in range(2):
            image_out[p, m + h] = following[h]
        spread = haar_rows(*following)
        coeffs.append([spread[h] + dual[p, m + h] for h in range(2)])
    for h in range(2):
        re, im = coeffs[0][h], coeffs[1][h]
        magnitude = jnp.sqrt(re * re + im * im)
        factor = jnp.maximum(1.0 - threshold / jnp.maximum(magnitude, threshold), 0.0)
        for p, value in enumerate((re, im)):
            kept = value * factor
            aux_out[p, m + h] = kept
            dual_out[p, m + h] = value - kept


def store_kernel(*refs):
    count = len(refs) // 2
    rows = refs[0].shape[1] // SPLIT
    copies = [
        pltpu.make_async_copy(
            refs[k].at[p, pl.ds(q * rows, rows)], refs[count + k].at[p, pl.ds(q * rows, rows)], refs[-1].at[k, p, q]
        )
        for k in range(count)
        for p in range(2)
        for q in range(SPLIT)
    ]
    for copy in copies:
        copy.start()
    for copy in copies:
        copy.wait()


def store_call(*values):
    return pl.pallas_call(
        store_kernel,
        in_specs=[pl.BlockSpec(memory_space=pltpu.VMEM)] * len(values),
        out_specs=[HBM] * len(values),
        out_shape=[jax.ShapeDtypeStruct(value.shape, value.dtype) for value in values],
        scratch_shapes=[pltpu.SemaphoreType.DMA((len(values), 2, SPLIT))],
        compiler_params=params(2**24),
        name="store",
    )(*values)


def finish_kernel(n, shares, kl, xl, chunks, sent, table_ref, sens, image, auxiliary, dual, *refs):
    coils = sens.shape[0]
    backs, refs = [refs[k * n : (k + 1) * n] for k in range(coils)], refs[coils * n :]
    image_out, aux_out, dual_out, table, held, landing, sens_v, grad, got, recv, send, local, grad_recv, grad_send, *wide = refs
    ready = coils - sent
    length = n * kl
    depth = landing.shape[-1]
    share = length // shares
    rows = xl // chunks
    band = rows * kl
    group = min(rows, 2)
    me = lax.axis_index("slab")
    mine = lax.axis_index("coil")

    barrier = pltpu.get_barrier_semaphore()

    def greet(off, carry):
        pl.semaphore_signal(
            barrier, inc=1, device_id={"slab": lax.rem(me + off, n)}, device_id_type=pl.DeviceIdType.MESH
        )
        return carry

    lax.fori_loop(1, n, greet, 0)
    for off in range(1, shares):
        pl.semaphore_signal(
            barrier, inc=1, device_id={"coil": lax.rem(mine + off, shares)}, device_id_type=pl.DeviceIdType.MESH
        )
    pl.semaphore_wait(barrier, n - 1 + shares - 1)

    def send_band(j, carry):
        where = pl.ds(pl.multiple_of(j * band, band), band)
        for k in range(ready, coils):
            for off in turns(n):
                pltpu.make_async_remote_copy(
                    src_ref=backs[k][off].at[:, where, :],
                    dst_ref=landing.at[k, me, :, where, :],
                    send_sem=send,
                    recv_sem=recv.at[j],
                    device_id={"slab": ahead(me, off, n)},
                    device_id_type=pl.DeviceIdType.MESH,
                ).start()
        return carry

    lax.fori_loop(0, chunks, send_band, 0)
    columns = pl.ds(pl.multiple_of(mine * share, share), share)
    copies = [pltpu.make_async_copy(table_ref, table, local.at[coils * n + coils])]
    for k, source in enumerate((image.at[:, :, columns], auxiliary, dual)):
        copies.append(pltpu.make_async_copy(source, held.at[k], local.at[coils * n + coils + 1 + k]))
    for k in range(coils):
        for off in range(n if k < ready else 1):
            origin = landing.at[k, behind(me, off, n)]
            copies.append(pltpu.make_async_copy(backs[k][off], origin, local.at[k * n + off]))
        copies.append(pltpu.make_async_copy(sens.at[k], sens_v.at[k], local.at[coils * n + k]))
    for copy in copies:
        copy.start()
    for copy in copies:
        copy.wait()

    def add_band(j):
        arrived = got.at[0 : shares - 1, :, pl.ds(j * rows, rows)]
        pltpu.make_async_copy(arrived, arrived, grad_recv.at[j]).wait()
        for i in range(rows):
            x = j * rows + i
            for p in range(2):
                value = grad[mine, p, x].astype(F32)
                for off in range(1, shares):
                    value += got[lax.rem(mine + off, shares), p, x].astype(F32)
                image_out[p, x] = value

    def settle(m):
        for k in range(2 // rows):
            add_band(2 // rows * m + k)
        update_pair(2 * m, held.at[0], image_out, held.at[1], held.at[2], image_out, aux_out, dual_out)

    def do_band(j, carry):
        where = pl.ds(pl.multiple_of(j * band, band), band)
        arrived = landing.at[ready:coils, 0 : n - 1, :, where, :]
        pltpu.make_async_copy(arrived, arrived, recv.at[j]).wait()
        if wide:
            for k in range(coils):
                for s in range(n):
                    for p in range(2):
                        wide[0][k, s, p] = landing[k, s, p, where, :].astype(F32)

        def columns_of(k, i):
            pieces = []
            for p in range(2):
                for s in range(n):
                    if wide:
                        pieces.append(wide[0][k, s, p, pl.ds(pl.multiple_of(i * kl, kl), kl), :])
                    else:
                        row = pl.multiple_of((j * rows + i) * kl, kl)
                        pieces.append(landing[k, s, p, pl.ds(row, kl), :])
            return jnp.concatenate(pieces, axis=0).astype(BF16)

        def pair(i, carry):
            total = [[None, None]] * group
            for k in range(coils):
                both = jnp.concatenate([columns_of(k, group * i + h) for h in range(group)], axis=1)
                adj = jnp.dot(table[...], both, preferred_element_type=F32)
                adj = adj.astype(BF16).astype(F32)
                for h in range(group):
                    x = j * rows + group * i + h
                    ar = adj[:length, h * depth : (h + 1) * depth]
                    ai = adj[length:, h * depth : (h + 1) * depth]
                    sr = sens_v[k, 0, x].astype(F32)
                    si = sens_v[k, 1, x].astype(F32)
                    re = sr * ar + si * ai
                    im = sr * ai - si * ar
                    total[h] = [re, im] if k == 0 else [total[h][0] + re, total[h][1] + im]
            for h in range(group):
                x = j * rows + group * i + h
                for p in range(2):
                    for q in range(shares):
                        grad[q, p, x] = total[h][p][q * share : (q + 1) * share].astype(BF16)
            return carry

        lax.fori_loop(0, rows // group, pair, 0)
        lines = pl.ds(j * rows, rows)
        for off in range(1, shares):
            target = lax.rem(mine + off, shares)
            pltpu.make_async_remote_copy(
                src_ref=grad.at[target, :, lines],
                dst_ref=got.at[mine, :, lines],
                send_sem=grad_send,
                recv_sem=grad_recv.at[j],
                device_id={"coil": target},
                device_id_type=pl.DeviceIdType.MESH,
            ).start()

        @pl.when((j % 2 == 1) & (j >= 3))
        def settled():
            settle((j - 3) // 2)

        return carry

    lax.fori_loop(0, chunks, do_band, 0)
    settle(chunks // 2 - 1)
    gone = landing.at[ready:coils, 0 : n - 1]
    pltpu.make_async_copy(gone, gone, send).wait()
    gone = got.at[0 : shares - 1]
    pltpu.make_async_copy(gone, gone, grad_send).wait()


def finish_call(table, backs, sent, sensitivity, image, auxiliary, dual, shares, n, kl):
    coils, _, xl, length, depth = sensitivity.shape
    chunks = xl
    rows = xl // chunks
    share = length // shares
    vmem = pl.BlockSpec(memory_space=pltpu.VMEM)
    scratch = [
        pltpu.VMEM(table.shape, BF16),
        pltpu.VMEM((3, 2, xl, share, depth), F32),
        pltpu.VMEM((coils, n, 2, xl * kl, depth), BF16),
        pltpu.VMEM(sensitivity.shape, BF16),
        pltpu.VMEM((shares, 2, xl, share, depth), BF16),
        pltpu.VMEM((shares, 2, xl, share, depth), BF16),
        pltpu.SemaphoreType.DMA((chunks,)),
        pltpu.SemaphoreType.DMA,
        pltpu.SemaphoreType.DMA((coils * n + coils + 4,)),
        pltpu.SemaphoreType.DMA((chunks,)),
        pltpu.SemaphoreType.DMA,
    ]
    if kl % 16:
        scratch.append(pltpu.VMEM((coils, n, 2, rows * kl, depth), F32))
    limit = VMEM_LIMIT - 26 * xl * share * depth
    return pl.pallas_call(
        functools.partial(finish_kernel, n, shares, kl, xl, chunks, sent),
        in_specs=[HBM] * (5 + coils * n),
        out_specs=[vmem] * 3,
        out_shape=[pltpu.VMEM((2, xl, share, depth), F32)] * 3,
        scratch_shapes=scratch,
        compiler_params=params(limit, collective_id=0, has_side_effects=True),
        name="finish",
    )(table, sensitivity, image, auxiliary, dual, *[piece for back in backs for piece in back])


def body(image, sensitivity, blocks, samples, offsets, counts, auxiliary, scaled_dual):
    coils, _, xl, length_y, _ = sensitivity.shape
    n = lax.axis_size("slab")
    shares = lax.axis_size("coil")
    kl = length_y // n
    y_fwd = complex_table(length_y, False)
    y_inv = complex_table(length_y, True)
    x_fwd = complex_table(n * xl, False)
    x_inv = complex_table(n * xl, True)

    def swap(parts, offs):
        moved = list(parts)
        for turn, off in enumerate(offs):
            if off:
                moved[turn] = lax.ppermute(parts[turn], "slab", [(i, ahead(i, off, n)) for i in range(n)])
        return moved

    batches = [[c] for c in range(coils)]

    def parts_of(c):
        if c == 0 and xl % 32 == 0:
            return [(0, xl // 2), (xl // 2, xl // 2)]
        return [(0, xl)]

    def tile_of(pieces, place, c):
        return tile_call(
            x_fwd, x_inv, pieces, parts_of(c), place, blocks, sorted_samples, offsets, counts, c, n, kl, xl
        )

    pieces, tiles, table = [], [], y_fwd
    for batch in batches:
        c = batch[0]
        everyone = [*turns(n), 0]
        moved = []
        jobs = [(first, size, everyone) for first, size in parts_of(c)]
        if len(jobs) > 1 and n >= 4 and kl % 16 == 0:
            first, size, _ = jobs[0]
            jobs[:1] = [(first, size, everyone[: n // 2]), (first, size, everyone[n // 2 :])]
        for first, size, offs in jobs:
            half = list(forward_call(table, image, sensitivity, batch, first, size, offs, n, kl))
            table, half[-1] = lax.optimization_barrier((table, half[-1]))
            moved += swap(half, offs)
        ordered = []
        for h in range(len(parts_of(c))):
            ordered += [moved[h * n + everyone.index(off)] for off in range(n)]
        moved = ordered
        pieces += [(moved, place) for place in range(len(batch))]
    table, samples = lax.optimization_barrier((table, samples))
    sorted_samples = sort_call(samples)
    for c in range(coils):
        arrived, place = pieces[c]
        if c:
            arrived = list(arrived)
            arrived[0], tiles[-1][0] = lax.optimization_barrier((arrived[0], tiles[-1][0]))
        tiles.append(list(tile_of(arrived, place, c)))
    early = max(coils - 3, 0)
    backs = list(tiles)
    for c in range(early):
        backs[c] = swap(tiles[c], range(n))
    results = finish_call(
        y_inv, backs, coils - early, sensitivity, image, auxiliary, scaled_dual, shares, n, kl
    )
    return tuple(store_call(*results))


def solution(mesh):
    return jax.shard_map(
        body,
        mesh=mesh,
        in_specs=(
            P(None, "slab", None, None),
            P("coil", None, "slab", None, None),
            P("slab", None, None, None),
            P("slab", None, None, "coil", None, None),
            P("slab", None),
            P("slab"),
            P(None, "slab", "coil", None),
            P(None, "slab", "coil", None),
        ),
        out_specs=(
            P(None, "slab", "coil", None),
            P(None, "slab", "coil", None),
            P(None, "slab", "coil", None),
        ),
        check_vma=False,
    )
```
